32 devices in a mesh: parts: 2 (over y), req: 8 (over z, x), tp: 2 (over core).
Axes of the slice: x: 2, y: 2, z: 4, core: 2. Of those that a mesh axis runs over, the one named last changes fastest.
Arguments:
- counts: int32 [16], P('parts'), parts along dimension 0, may hold values from 1 to 2, as said below
- move_plan: int32 [32], P('parts'), parts along dimension 0, may hold values from 0 to 15, as said below
- ssm_state: float32 [32, 128, 4096], P(('parts', 'req'), 'tp'), parts along dimension 0, may hold values from -6 to 6
- conv_x_state: bfloat16 [32, 3, 8192], P(('parts', 'req'), None, 'tp'), parts along dimension 0, may hold values from -6 to 6
- conv_bc_state: bfloat16 [32, 3, 4, 128], P(('parts', 'req'), None, 'tp'), parts along dimension 0, may hold values from -6 to 6
- x_in: bfloat16 [32, 4, 8192], P(('parts', 'req'), None, 'tp'), parts along dimension 0, may hold values from -6 to 6
- bc_in: bfloat16 [32, 4, 4, 128], P(('parts', 'req'), None, 'tp'), parts along dimension 0, may hold values from -6 to 6
- z_in: bfloat16 [32, 4, 8192], P(('parts', 'req'), None, 'tp'), parts along dimension 0, may hold values from -6 to 6
- dt_in: float32 [32, 4, 128], P(('parts', 'req'), None, 'tp'), parts along dimension 0, may hold values from -1.5 to 1.5
- conv_w_x: float32 [4, 8192], P(None, 'tp'), may hold values from -3 to 3
- conv_b_x: float32 [8192], P('tp'), may hold values from -3 to 3
- conv_w_bc: float32 [4, 4, 128], P(None, 'tp'), may hold values from -3 to 3
- conv_b_bc: float32 [4, 128], P('tp'), may hold values from -3 to 3
- dt_bias: float32 [128], P('tp'), may hold values from -4 to -1
- a_log: float32 [128], P('tp'), may hold values from -2.5 to -0.5
- d_skip: float32 [128], P('tp'), may hold values from 0.3 to 1.5
- norm_w: float32 [8192], P('tp'), may hold values from 0.1 to 1.9
Outputs:
- y_out: bfloat16 [32, 4, 8192], P(('parts', 'req'), None, 'tp'), parts along dimension 0
- new_ssm: float32 [32, 128, 4096], P(('parts', 'req'), 'tp'), parts along dimension 0
- new_conv_x: bfloat16 [32, 3, 8192], P(('parts', 'req'), None, 'tp'), parts along dimension 0
- new_conv_bc: bfloat16 [32, 3, 4, 128], P(('parts', 'req'), None, 'tp'), parts along dimension 0
The draws below stay inside these ranges and needn't reach their ends.
There are 2 independent parts, one for each index of `parts`. The reference program is written for one: setup_inputs(seed, part) draws one part's arguments, and reference() takes and returns one part's arrays. A program takes and returns all parts, laid end to end along the dimension named above; an argument that names none is the same for every part. Nothing has to cross between parts.
Inputs may be any that keep to these rules, and one draw needn't show every extreme that they name: `counts`: at least 1; every draw has owners with 2 live requests. `move_plan`: A destination slot is owner times 2 plus a local slot. Entries of slots that are not live are meaningless. Live requests have distinct destinations. An owner sends at most 1 live requests to other owners and receives at most 1 from other owners, and keeps at most 1 of its own; both bounds are reached in every draw, and some owner has all 2 destination slots taken.
All inputs are finite; a program needn't handle non-finite values.
Results may differ from the reference program's by a relative error of at most 0.001.
Values may be sent and summed in bfloat16 or wider, within the bound.
A program may use at most 128 MiB of HBM per device.

```python
import jax
import jax.numpy as jnp
from jax import lax

H = 128
P_SIZE = 64
N = 64
G = 4
CAP = 2
STEPS = 4
REQS = 16
CAPS = 16
N_REQ = 8


def plan_draw(key):
    base = jax.random.fold_in(key, 11)
    keys = jax.random.split(base, 6)
    order = jax.random.permutation(keys[0], N_REQ).astype(jnp.int32)
    following = jnp.zeros((N_REQ,), jnp.int32).at[order].set(jnp.roll(order, -1))
    counts = 1 + jax.random.randint(keys[1], (N_REQ,), 0, 2)
    counts = counts.at[order[0]].set(2).at[order[1]].set(2)
    leaves = jnp.where(counts == 2, 1, jax.random.randint(keys[2], (N_REQ,), 0, 2))
    leaving_slot = jnp.where(counts == 2, jax.random.randint(keys[3], (N_REQ,), 0, 2), 0)
    side = jax.random.randint(keys[4], (N_REQ,), 0, 2)
    owners = jnp.arange(N_REQ, dtype=jnp.int32)
    junk = jax.random.randint(keys[5], (N_REQ, 2), 0, N_REQ * CAP)
    moved_dest = following * CAP + jnp.take(side, following)
    stay_dest = owners * CAP + 1 - side
    columns = []
    for slot in range(2):
        live = slot < counts
        moving = live & (leaves == 1) & (leaving_slot == slot)
        columns.append(jnp.where(moving, moved_dest, jnp.where(live, stay_dest, junk[:, slot])))
    plan = jnp.stack(columns, 1).reshape(-1)
    return (counts.astype(jnp.int32), plan.astype(jnp.int32))


def draw_counts(key, part):
    return plan_draw(key)[0]


def draw_move_plan(key, part):
    return plan_draw(key)[1]


def shard_levels(own_key, extent, cuts, least, high):
    factor_of, own = 1.0, jax.random.fold_in(own_key, 6)
    for axis_at, blocks in cuts:
        draws = jnp.exp(jax.random.uniform(jax.random.fold_in(own, axis_at), (blocks,), jnp.float32, least / len(cuts), high / len(cuts)))
        factor_of = factor_of * jnp.repeat(draws, extent[axis_at] // blocks).reshape([-1 if axis == axis_at else 1 for axis in range(len(extent))])
    return factor_of


def normal_values(stream_key, shape, scale, reach, pieces=(), kind=jnp.bfloat16):
    loudness = shard_levels(stream_key, shape, pieces, -0.22, 0.18) if pieces else 1.0
    result = jax.random.normal(stream_key, shape, jnp.float32) * scale * loudness
    return jnp.minimum(jnp.maximum(result, -reach), reach).astype(kind)


def setup_inputs(seed: int = 0, part: int = 0) -> dict:
    arg_keys = jax.random.split(jax.random.key(seed), 18)
    own_keys = jax.random.split(jax.random.fold_in(arg_keys[17], part), 18)
    return {
        "counts": draw_counts(jax.random.fold_in(jax.random.fold_in(arg_keys[17], part), 71), part),
        "move_plan": draw_move_plan(jax.random.fold_in(jax.random.fold_in(arg_keys[17], part), 71), part),
        "ssm_state": normal_values(own_keys[2], (REQS, H, P_SIZE * N), 1.0, 6.0, ((0, 8), (1, 2)), jnp.float32),
        "conv_x_state": normal_values(own_keys[3], (REQS, 3, H * P_SIZE), 1.0, 6.0, ((0, 8), (2, 2))),
        "conv_bc_state": normal_values(own_keys[4], (REQS, 3, G, 2 * N), 1.0, 6.0, ((0, 8), (2, 2))),
        "x_in": normal_values(own_keys[5], (CAPS, STEPS, H * P_SIZE), 1.0, 6.0, ((0, 8), (2, 2))),
        "bc_in": normal_values(own_keys[6], (CAPS, STEPS, G, 2 * N), 1.0, 6.0, ((0, 8), (2, 2))),
        "z_in": normal_values(own_keys[7], (CAPS, STEPS, H * P_SIZE), 1.0, 6.0, ((0, 8), (2, 2))),
        "dt_in": normal_values(own_keys[8], (CAPS, STEPS, H), 0.5, 1.5, ((0, 8), (2, 2)), jnp.float32),
        "conv_w_x": normal_values(arg_keys[9], (4, H * P_SIZE), 4 ** -0.5, 3.0, ((1, 2),), jnp.float32),
        "conv_b_x": normal_values(arg_keys[10], (H * P_SIZE,), 0.5, 3.0, ((0, 2),), jnp.float32),
        "conv_w_bc": normal_values(arg_keys[11], (4, G, 2 * N), 4 ** -0.5, 3.0, ((1, 2),), jnp.float32),
        "conv_b_bc": normal_values(arg_keys[12], (G, 2 * N), 0.5, 3.0, ((0, 2),), jnp.float32),
        "dt_bias": jnp.clip(-4.0 + 3.0 * jax.random.uniform(arg_keys[13], (H,), jnp.float32) ** shard_levels(arg_keys[13], (H,), ((0, 2),), -0.2, 0.2), -4.0, -1.0),
        "a_log": jnp.clip(-2.5 + 2.0 * jax.random.uniform(arg_keys[14], (H,), jnp.float32) ** shard_levels(arg_keys[14], (H,), ((0, 2),), -0.2, 0.2), -2.5, -0.5),
        "d_skip": jnp.clip(0.3 + 1.2 * jax.random.uniform(arg_keys[15], (H,), jnp.float32) ** shard_levels(arg_keys[15], (H,), ((0, 2),), -0.2, 0.2), 0.3, 1.5),
        "norm_w": jnp.clip(1.0 + 0.18 * jax.random.normal(arg_keys[16], (H * P_SIZE,), jnp.float32), 0.1, 1.9),
    }


def plan_slots(counts, move_plan, caps):
    reqs = move_plan.shape[0]
    slots = reqs // counts.shape[0]
    ids = jnp.arange(reqs, dtype=jnp.int32)
    live = ids % slots < jnp.take(counts, ids // slots)
    targets = jnp.arange(caps, dtype=jnp.int32)
    match = live[None, :] & (move_plan[None, :] == targets[:, None])
    source = lax.optimization_barrier(jnp.sum(jnp.where(match, ids[None, :], 0), axis=1)).astype(jnp.int32)
    filled = jnp.any(match, axis=1)
    return (source, filled)

def reference(counts, move_plan, ssm_state, conv_x_state, conv_bc_state, x_in, bc_in, z_in, dt_in, conv_w_x, conv_b_x, conv_w_bc, conv_b_bc, dt_bias, a_log, d_skip, norm_w):
    caps = x_in.shape[0]
    source, filled = plan_slots(counts, move_plan, caps)
    per_group = H // G
    rate = jnp.exp(a_log)

    def one_slot(item):
        src, full, x_seq, bc_seq, z_seq, dt_seq = item
        state = jnp.take(ssm_state, src, axis=0).reshape(H, P_SIZE, N)
        state = jnp.where(full, state, jnp.zeros_like(state))
        conv_x = jnp.take(conv_x_state, src, axis=0)
        conv_x = jnp.where(full, conv_x, jnp.zeros_like(conv_x))
        conv_bc = jnp.take(conv_bc_state, src, axis=0)
        conv_bc = jnp.where(full, conv_bc, jnp.zeros_like(conv_bc))
        outputs = []
        for step in range(STEPS):
            x_new = x_seq[step]
            window = jnp.concatenate([conv_x, x_new[None]], 0).astype(jnp.float32)
            xconv = jax.nn.silu(lax.optimization_barrier(jnp.sum(window * conv_w_x, axis=0)) + conv_b_x)
            conv_x = jnp.concatenate([conv_x[1:], x_new[None]], 0)
            bc_new = bc_seq[step]
            bwindow = jnp.concatenate([conv_bc, bc_new[None]], 0).astype(jnp.float32)
            bconv = jax.nn.silu(lax.optimization_barrier(jnp.sum(bwindow * conv_w_bc, axis=0)) + conv_b_bc)
            conv_bc = jnp.concatenate([conv_bc[1:], bc_new[None]], 0)
            b_head = jnp.repeat(bconv[:, :N], per_group, axis=0)
            c_head = jnp.repeat(bconv[:, N:], per_group, axis=0)
            delta = jax.nn.softplus(dt_seq[step] + dt_bias)
            decay = jnp.exp(-delta * rate)
            heads_x = xconv.reshape(H, P_SIZE)
            state = decay[:, None, None] * state + (delta[:, None] * heads_x)[:, :, None] * b_head[:, None, :]
            mixed = lax.optimization_barrier(jnp.sum(state * c_head[:, None, :], axis=-1)) + d_skip[:, None] * heads_x
            gated = mixed.reshape(H * P_SIZE) * jax.nn.silu(z_seq[step].astype(jnp.float32))
            total = jnp.sum(gated * gated)
            normed = gated * lax.rsqrt(total / (H * P_SIZE) + 1e-05) * norm_w
            outputs.append(jnp.where(full, normed, jnp.zeros_like(normed)).astype(jnp.bfloat16))
        final = jnp.where(full, state.reshape(H, P_SIZE * N), jnp.zeros((H, P_SIZE * N), jnp.float32))
        conv_x = jnp.where(full, conv_x, jnp.zeros_like(conv_x))
        conv_bc = jnp.where(full, conv_bc, jnp.zeros_like(conv_bc))
        return (jnp.stack(outputs, 0), final, conv_x, conv_bc)
    y_out, new_ssm, new_conv_x, new_conv_bc = lax.map(one_slot, (source, filled, x_in, bc_in, z_in, dt_in))
    return (y_out, new_ssm, new_conv_x, new_conv_bc)
```

```python
import functools

import jax
import jax.numpy as jnp
from jax import lax
from jax.experimental import pallas as pl
from jax.experimental.pallas import tpu as pltpu
from jax.sharding import PartitionSpec as P

MESH = pl.DeviceIdType.MESH
F32 = jnp.float32
BF16 = jnp.bfloat16
LANES = 128
HALF = 64


def silu(v):
    return v / (1.0 + jnp.exp(-v))


def split(v):
    hi = v.astype(BF16)
    return hi, (v - hi.astype(F32)).astype(BF16)


def mm(a, b):
    return jnp.dot(a, b, preferred_element_type=F32)


def fused_kernel(
    n,
    counts_h,
    plan_h,
    state_h,
    cx_h,
    cb_h,
    x_h,
    bc_h,
    z_h,
    dt_h,
    wx_h,
    bx_h,
    wbc_h,
    bbc_h,
    dtb_h,
    alog_h,
    dskip_h,
    nw_h,
    y_o,
    new_o,
    ncx_o,
    ncb_o,
    counts,
    plan,
    state,
    cx,
    cb,
    xv,
    bcv,
    zv,
    dtv,
    wx,
    bx,
    wbc,
    bbc,
    dtb,
    alog,
    dskip,
    nw,
    code,
    spread,
    picked,
    arr,
    hdr,
    gath,
    hf,
    winx,
    winb,
    xc,
    rowt,
    xs,
    gate,
    yb,
    vv,
    dl,
    dcol,
    wc2,
    wcl,
    wb2,
    yr,
    ye,
    new,
    ssv,
    ssr,
    yv,
    ncx,
    ncb,
    in_sem,
    s1,
    r1,
    s2,
    r2,
    sh,
    rh,
    st,
    rt,
    o_sem,
    y_sem,
):
    slots, heads, cols = state.shape
    steps, channels = xv.shape[1], xv.shape[2]
    groups = bbc.shape[0]
    per = heads // groups
    tiles = cols // LANES
    rows = tiles * heads // n
    ctiles = channels // LANES
    quarter = hf.shape[1]
    parts = channels // quarter
    me = lax.axis_index("req")
    tp = lax.axis_index("tp")
    small = n <= 16
    order = sorted(range(1, n), key=lambda k: (-min(k, n - k), k)) if small else None

    def each(body):
        if small:
            for k in order:
                body(k)
        else:
            lax.fori_loop(1, n, lambda k, c: (body(k), c)[1], 0)

    barrier = pltpu.get_barrier_semaphore()

    def greet(k):
        pl.semaphore_signal(
            barrier, inc=1, device_id={"req": lax.rem(me + k, n)}, device_id_type=MESH
        )

    each(greet)
    pl.semaphore_signal(barrier, inc=1, device_id={"tp": 1 - tp}, device_id_type=MESH)

    pairs = [
        (counts_h, counts),
        (plan_h, plan),
        (state_h, state),
        (cx_h, cx),
        (cb_h, cb),
        (x_h, xv),
        (bc_h, bcv),
        (z_h, zv),
        (dt_h, dtv),
        (wx_h, wx),
        (bx_h, bx),
        (wbc_h, wbc),
        (bbc_h, bbc),
        (dtb_h, dtb),
        (alog_h, alog),
        (dskip_h, dskip),
        (nw_h, nw),
    ]
    loads = [pltpu.make_async_copy(a, b, in_sem.at[i]) for i, (a, b) in enumerate(pairs)]
    for ld in loads:
        ld.start()

    def send(src, dst, ss, rs, k):
        return pltpu.make_async_remote_copy(
            src_ref=src,
            dst_ref=dst,
            send_sem=ss.at[k],
            recv_sem=rs.at[k],
            device_id={"req": lax.rem(me + k, n)},
            device_id_type=MESH,
        )

    def landed(dst, ss, rs, k):
        origin = lax.rem(me + n - k, n)
        pltpu.make_async_remote_copy(
            src_ref=dst.at[origin],
            dst_ref=dst.at[origin],
            send_sem=ss.at[k],
            recv_sem=rs.at[k],
            device_id={"req": origin},
            device_id_type=MESH,
        ).wait_recv()

    def first(k):
        return send(code.at[lax.rem(me + k, n)], spread.at[me], s1, r1, k)

    def second(k):
        return send(picked.at[lax.rem(me + k, n)], arr.at[me], s2, r2, k)

    def heading(k):
        return send(hdr, gath.at[me], sh, rh, k)

    loads[0].wait()
    loads[1].wait()
    one, zero = jnp.int32(1), jnp.int32(0)

    def live(r):
        return (r % slots) < counts[r // slots]

    def leaving(r):
        return live(r) & (plan[r] // slots != r // slots)

    send_j = zero
    for j in range(slots):
        send_j = jnp.where(leaving(me * slots + j), j, send_j)

    sub = lax.broadcasted_iota(jnp.int32, (heads, heads), 0)
    lane = lax.broadcasted_iota(jnp.int32, (heads, heads), 1)
    eye = sub == lane

    def column(row):
        return jnp.sum(jnp.where(eye, row, 0.0), axis=1, keepdims=True)

    def ts(i):
        return slice(i * LANES, (i + 1) * LANES)

    loads[2].wait()
    top = jnp.abs(state[send_j, :, ts(0)])
    for i in range(1, tiles):
        top = jnp.maximum(top, jnp.abs(state[send_j, :, ts(i)]))
    top = jnp.maximum(jnp.max(top, axis=1, keepdims=True), 1e-30)
    unit = (top * (1.0078125 / 32767.0)).astype(BF16).astype(F32)
    inv = 1.0 / unit
    for i in range(tiles):
        q = jnp.round(state[send_j, :, ts(i)] * inv)
        q = q.astype(jnp.int32).astype(jnp.int16)
        chunk = min(rows, heads)
        for at in range(0, heads, chunk):
            row = i * heads + at
            code[row // rows, row % rows:row % rows + chunk, :] = q[at:at + chunk, :]

    loads[3].wait()
    loads[4].wait()
    hf[...] = jnp.zeros_like(hf)
    mine = cx[send_j].astype(F32)
    for q in range(parts):
        hf[3 * q:3 * q + 3, :] = mine[:, q * quarter:(q + 1) * quarter]
    for j in range(3):
        pair = cb[send_j, j].astype(F32)
        for g in range(groups):
            hf[3 * parts:3 * parts + 1, ts(j * groups + g)] = pair[g:g + 1, :]
    hf[3 * parts + 1:3 * parts + 2, 0:heads] = jnp.sum(
        jnp.where(eye, unit, 0.0), axis=0, keepdims=True
    )
    hdr[...] = hf[...].astype(BF16)

    pl.semaphore_wait(barrier, n)
    each(lambda k: first(k).start())
    each(lambda k: heading(k).start())
    spread[me] = code[me]
    gath[me] = hdr[...]

    def for_reqs(body, init):
        if small:
            for r in range(n * slots):
                init = body(r, init)
            return init
        return lax.fori_loop(0, n * slots, body, init)

    def scan_mine(r, carry):
        ok = live(r)
        out = []
        for k in range(slots):
            hit, src = carry[2 * k], carry[2 * k + 1]
            m = ok & (plan[r] == me * slots + k)
            out += [jnp.where(m, one, hit), jnp.where(m, r, src)]
        return tuple(out)

    mine_of = for_reqs(scan_mine, (zero,) * (2 * slots))
    hit = [mine_of[2 * k] == 1 for k in range(slots)]
    source = [mine_of[2 * k + 1] for k in range(slots)]
    rec = [hit[k] & (source[k] // slots != me) for k in range(slots)]
    keep = [hit[k] & (source[k] // slots == me) for k in range(slots)]
    k_rec, k_keep, slot_keep, src_me = zero, zero, zero, zero
    for k in range(slots):
        k_rec = jnp.where(rec[k], k, k_rec)
        k_keep = jnp.where(keep[k], k, k_keep)
        slot_keep = jnp.where(keep[k], source[k] % slots, slot_keep)
        src_me = jnp.where(rec[k], source[k] // slots, src_me)
    hit_f = [jnp.where(h, 1.0, 0.0) for h in hit]
    rec_f = [jnp.where(h, 1.0, 0.0) for h in rec]
    keep_f = [jnp.where(h, 1.0, 0.0) for h in keep]

    if small:
        goes = [jnp.where(leaving(jnp.int32(r)), plan[r] // slots, -1) for r in range(n * slots)]

    def source_owner(d):
        if small:
            src = zero
            for r in range(n * slots):
                src = jnp.where(goes[r] == d, r // slots, src)
            return src
        return lax.fori_loop(
            0,
            n * slots,
            lambda r, c: jnp.where(leaving(r) & (plan[r] // slots == d), r // slots, c),
            zero,
        )

    for ld in loads[5:]:
        ld.wait()
    gate[...] = silu(zv[...].astype(F32)).reshape(gate.shape)
    rate = jnp.exp(alog[...])
    skip = column(dskip[...])
    lane1 = lax.broadcasted_iota(jnp.int32, (heads, LANES), 1)
    low = lane1 < HALF
    delta_col, decay_col = [], []
    for k in range(slots):
        raw = dtv[k] + dtb[...]
        delta = jnp.maximum(raw, 0.0) + jnp.log(1.0 + jnp.exp(-jnp.abs(raw)))
        decay = jnp.exp(-delta * rate)
        delta_col.append([column(delta[t:t + 1, :]) for t in range(steps)])
        decay_col.append([column(decay[t:t + 1, :]) for t in range(steps)])
        cum = []
        for t in range(steps):
            cum.append(decay_col[k][t] if t == 0 else cum[-1] * decay_col[k][t])
        for t in range(0, steps, 2):
            dl[k, :, ts(t // 2)] = jnp.where(low, cum[t], cum[t + 1])
        dcol[k] = jnp.broadcast_to(cum[-1], (heads, LANES))
        xk = xv[k].astype(F32)
        winx[k, 3:3 + steps, :] = xk
        filled_x = jnp.where(hit[k], xk, 0.0)
        ncx[k] = filled_x[steps - 3:].astype(BF16)
        for t in range(steps):
            pair = bcv[k, t].astype(F32)
            for g in range(groups):
                winb[k, g, 3 + t:4 + t, :] = pair[g:g + 1, :]
            if t >= steps - 3:
                ncb[k, t - (steps - 3)] = jnp.where(hit[k], pair, 0.0).astype(BF16)
    out_x = pltpu.make_async_copy(ncx, ncx_o, y_sem.at[1])
    out_x.start()
    out_b = pltpu.make_async_copy(ncb, ncb_o, y_sem.at[2])
    out_b.start()

    each(lambda k: landed(spread, s1, r1, k))

    def pick(k):
        d = lax.rem(me + k, n)
        picked[d] = spread[source_owner(d)]
        second(k).start()

    each(pick)
    arr[me] = spread[src_me]

    each(lambda k: landed(gath, sh, rh, k))
    hf[...] = gath[src_me].astype(F32)
    unit_in = column(hf[3 * parts + 1:3 * parts + 2, 0:heads])
    kept_x = cx[slot_keep].astype(F32)
    for k in range(slots):
        for q in range(parts):
            span = slice(q * quarter, (q + 1) * quarter)
            winx[k, 0:3, span] = jnp.where(keep[k], kept_x[:, span], hf[3 * q:3 * q + 3, :])
        for j in range(3):
            pair = cb[slot_keep, j].astype(F32)
            for g in range(groups):
                winb[k, g, j:j + 1, :] = jnp.where(
                    keep[k],
                    pair[g:g + 1, :],
                    hf[3 * parts:3 * parts + 1, ts(j * groups + g)],
                )
        acc = bx[...] + winx[k, 0:steps, :] * wx[0:1, :]
        for j in range(1, 4):
            acc += winx[k, j:j + steps, :] * wx[j:j + 1, :]
        xc[k * steps:(k + 1) * steps, :] = silu(acc)

    every = slots * steps
    for i in range(ctiles):
        rowt[pl.ds(i, every, stride=ctiles), :] = xc[:, ts(i)]
    for kt in range(every):
        r = rowt[kt * ctiles:(kt + 1) * ctiles, :]
        xs[kt, pl.ds(0, ctiles, stride=2), :] = r
        xs[kt, pl.ds(1, ctiles, stride=2), :] = pltpu.roll(r, HALF, 1)

    width = steps * HALF
    lane_w = lax.broadcasted_iota(jnp.int32, (HALF, width), 1)
    even_w = lane_w % 2 == 0
    row_b = lax.broadcasted_iota(jnp.int32, (HALF, LANES), 0)
    lane_b = lax.broadcasted_iota(jnp.int32, (HALF, LANES), 1)
    match_b = (row_b % 2) == (lane_b // HALF)
    for k in range(slots):
        across = []
        for g in range(groups):
            acc = bbc[g:g + 1, :] + winb[k, g, 0:steps, :] * wbc[0, g:g + 1, :]
            for j in range(1, 4):
                acc += winb[k, g, j:j + steps, :] * wbc[j, g:g + 1, :]
            bw = silu(acc)
            turned = pltpu.roll(bw, HALF, 1)
            low4 = lax.broadcasted_iota(jnp.int32, (steps, LANES), 1) < HALF
            b_two = jnp.where(low4, bw, turned)
            c_two = jnp.where(low4, turned, bw)
            across.append(
                [
                    0.5 * jnp.sum(c_two * b_two[s:s + 1, :], axis=1, keepdims=True)
                    for s in range(steps)
                ]
            )
            c_cols = [column(c_two[t:t + 1, 0:HALF]) for t in range(steps)]
            halves = [
                jnp.where(low, c_cols[t], c_cols[t + 1]) for t in range(0, steps, 2)
            ]
            base = jnp.concatenate(halves, axis=1)
            for j in range(2):
                w = jnp.where(even_w == (j == 0), base, 0.0)
                hi, lo = split(w)
                wc2[k, g, j * HALF:(j + 1) * HALF, :] = hi
                wc2[k, g, LANES + j * HALF:LANES + (j + 1) * HALF, :] = hi
                wcl[k, g, j * HALF:(j + 1) * HALF, :] = lo
            for s in range(steps):
                w = jnp.where(match_b, b_two[s:s + 1, :], 0.0)
                hi, lo = split(w)
                wb2[k, g, s * HALF:(s + 1) * HALF, 0:LANES] = hi
                wb2[k, g, s * HALF:(s + 1) * HALF, LANES:2 * LANES] = lo

        def cross(t, s):
            return jnp.concatenate(
                [jnp.broadcast_to(across[g][s][t:t + 1, :], (per, 1)) for g in range(groups)],
                axis=0,
            )

        x_of = [xs[k * steps + t] for t in range(steps)]
        for t in range(steps):
            acc = skip * x_of[t]
            weight = None
            for s in range(t, -1, -1):
                weight = decay_col[k][s + 1] * weight if weight is not None else jnp.ones_like(skip)
                acc += (weight * delta_col[k][s] * cross(t, s)) * x_of[s]
            if t % 2 == 0:
                first_half = acc
            else:
                yb[k, :, ts(t // 2)] = jnp.where(low, first_half, pltpu.roll(acc, HALF, 1))
        weight = None
        v_of = [None] * steps
        for s in range(steps - 1, -1, -1):
            weight = decay_col[k][s + 1] * weight if weight is not None else jnp.ones_like(skip)
            v_of[s] = (weight * delta_col[k][s] * hit_f[k]) * x_of[s]
        for s in range(0, steps, 2):
            vv[k, :, ts(s // 2)] = jnp.where(low, v_of[s], pltpu.roll(v_of[s + 1], HALF, 1))

    batch = 8
    lane_p = (lax.broadcasted_iota(jnp.int32, (per, width), 1) % HALF) // 2
    for g in range(groups):
        hs = slice(g * per, (g + 1) * per)
        acc = jnp.zeros((per, width), F32)
        for b in range(0, tiles, batch):
            parts_s = [state[slot_keep, hs, ts(i)] for i in range(b, b + batch)]
            hi, lo = split(jnp.concatenate(parts_s, axis=0))
            out = mm(jnp.concatenate([hi, lo], axis=1), wc2[k_keep, g]) + mm(hi, wcl[k_keep, g])
            for j in range(batch):
                acc += jnp.where(lane_p == b + j, out[j * per:(j + 1) * per, :], 0.0)
        for k in range(slots):
            yb[k, hs, :] = yb[k, hs, :] + (keep_f[k] * dl[k, hs, :]) * acc
            v = vv[k, hs, :]
            v_hi = v.astype(BF16).astype(F32)
            v_lo = v - v_hi
            scale = keep_f[k] * dcol[k, hs, :]
            for b in range(0, tiles, batch):
                hi = jnp.concatenate(
                    [jnp.where(lane_p == i, v_hi, 0.0) for i in range(b, b + batch)], axis=0
                ).astype(BF16)
                lo = jnp.concatenate(
                    [jnp.where(lane_p == i, v_lo, 0.0) for i in range(b, b + batch)], axis=0
                ).astype(BF16)
                out = mm(hi, wb2[k, g])
                out = out[:, 0:LANES] + out[:, LANES:] + mm(lo, wb2[k, g, :, 0:LANES])
                for j in range(batch):
                    new[k, hs, ts(b + j)] = (
                        scale * state[slot_keep, hs, ts(b + j)] + out[j * per:(j + 1) * per, :]
                    )

    gain = [(rec_f[k] * unit_in) * dcol[k] for k in range(slots)]
    yr[...] = jnp.zeros_like(yr)

    def absorb(whole, start, count):
        q = whole.astype(jnp.int32).astype(F32)
        for j in range(count):
            at = pl.ds(pl.multiple_of((start + j) * LANES, LANES), LANES)
            for k in range(slots):
                new[k, :, at] = new[k, :, at] + gain[k] * q[j * heads:(j + 1) * heads, :]
        for g in range(groups):
            part = jnp.concatenate(
                [q[j * heads + g * per:j * heads + (g + 1) * per, :] for j in range(count)], axis=0
            )
            hi, lo = split(part)
            out = mm(jnp.concatenate([hi, lo], axis=1), wc2[k_rec, g]) + mm(hi, wcl[k_rec, g])
            acc = yr[g * per:(g + 1) * per, :]
            for j in range(count):
                acc += jnp.where(lane_p == start + j, out[j * per:(j + 1) * per, :], 0.0)
            yr[g * per:(g + 1) * per, :] = acc

    def store(start, count, k):
        at = pl.ds(pl.multiple_of(start * LANES, LANES), count * LANES)
        return pltpu.make_async_copy(new.at[:, :, at], new_o.at[:, :, at], o_sem.at[k])

    if small and rows % heads == 0:
        count = rows // heads
        outs = []
        for k in [0] + order:
            src = lax.rem(me + n - k, n)
            if k:
                landed(arr, s2, r2, k)
            absorb(arr[src], src * count, count)
            st_new = store(src * count, count, k)
            st_new.start()
            outs.append(st_new)
    else:
        each(lambda k: landed(arr, s2, r2, k))
        outs = []
        some = 4 * heads // rows
        for i in range(tiles // 4):
            absorb(arr[i * some:(i + 1) * some].reshape(4 * heads, LANES), i * 4, 4)
        st_new = store(0, tiles, 0)
        st_new.start()
        outs.append(st_new)

    for k in range(slots):
        y = yb[k] + ((rec_f[k] * unit_in) * dl[k]) * yr[...]
        for p in range(steps // 2):
            ye[...] = y[:, ts(p)]
            even = ye[pl.ds(0, ctiles, stride=2), :]
            odd = ye[pl.ds(1, ctiles, stride=2), :]
            low_c = lax.broadcasted_iota(jnp.int32, (ctiles, LANES), 1) < HALF
            at = (k * steps + 2 * p) * ctiles
            rowt[at:at + ctiles, :] = jnp.where(low_c, even, pltpu.roll(odd, HALF, 1))
            rowt[at + ctiles:at + 2 * ctiles, :] = jnp.where(
                low_c, pltpu.roll(even, HALF, 1), odd
            )
    total = jnp.zeros((every, LANES), F32)
    for i in range(ctiles):
        v = rowt[pl.ds(i, every, stride=ctiles), :] * gate[:, ts(i)]
        xc[:, ts(i)] = v
        total += v * v
    own = jnp.sum(total, axis=1, keepdims=True)
    ssv[...] = jnp.broadcast_to(own, ssv.shape)
    swap = pltpu.make_async_remote_copy(
        src_ref=ssv,
        dst_ref=ssr,
        send_sem=st,
        recv_sem=rt,
        device_id={"tp": 1 - tp},
        device_id_type=MESH,
    )
    swap.start()
    swap.wait_recv()
    both = (ssv[...] + ssr[...])[:, 0:1]
    norm = lax.rsqrt(both * (1.0 / (channels * 2)) + 1e-5)
    for k in range(slots):
        span = slice(k * steps, (k + 1) * steps)
        out = xc[span, :] * norm[span, :] * nw[...]
        yv[k] = jnp.where(hit[k], out, 0.0).astype(BF16)
    out_y = pltpu.make_async_copy(yv, y_o, y_sem.at[0])
    out_y.start()

    swap.wait_send()
    each(lambda k: first(k).wait_send())
    each(lambda k: heading(k).wait_send())
    each(lambda k: second(k).wait_send())
    out_x.wait()
    out_b.wait()
    for st_new in outs:
        st_new.wait()
    out_y.wait()


def on_device(
    counts,
    move_plan,
    ssm_state,
    conv_x_state,
    conv_bc_state,
    x_in,
    bc_in,
    z_in,
    dt_in,
    conv_w_x,
    conv_b_x,
    conv_w_bc,
    conv_b_bc,
    dt_bias,
    a_log,
    d_skip,
    norm_w,
):
    n = lax.axis_size("req")
    slots, heads, cols = ssm_state.shape
    _, steps, channels = x_in.shape
    groups = conv_bc_state.shape[2]
    args = (
        counts,
        move_plan,
        ssm_state,
        conv_x_state,
        conv_bc_state,
        x_in,
        bc_in,
        z_in,
        dt_in,
        conv_w_x,
        conv_b_x.reshape(1, -1),
        conv_w_bc,
        conv_b_bc,
        dt_bias.reshape(1, -1),
        a_log.reshape(1, -1),
        d_skip.reshape(1, -1),
        norm_w.reshape(1, -1),
    )
    vm = pltpu.VMEM
    flat = (cols // LANES) * heads
    every = slots * steps
    width = steps * HALF
    quarter = 1024
    scratch = [pltpu.SMEM(a.shape, a.dtype) for a in args[:2]]
    scratch += [vm(a.shape, a.dtype) for a in args[2:]]
    scratch += [vm((n, flat // n, LANES), jnp.int16)] * 4
    scratch += [
        vm((16, quarter), BF16),
        vm((n, 16, quarter), BF16),
        vm((16, quarter), F32),
        vm((slots, 8, channels), F32),
        vm((slots, groups, 8, LANES), F32),
        vm((every, channels), F32),
        vm((every * channels // LANES, LANES), F32),
        vm((every, heads, LANES), F32),
        vm((every, channels), F32),
        vm((slots, heads, width), F32),
        vm((slots, heads, width), F32),
        vm((slots, heads, width), F32),
        vm((slots, heads, LANES), F32),
        vm((slots, groups, 2 * LANES, width), BF16),
        vm((slots, groups, LANES, width), BF16),
        vm((slots, groups, width, 2 * LANES), BF16),
        vm((heads, width), F32),
        vm((heads, LANES), F32),
        vm((slots, heads, cols), F32),
        vm((every, LANES), F32),
        vm((every, LANES), F32),
        vm(x_in.shape, BF16),
        vm(conv_x_state.shape, BF16),
        vm(conv_bc_state.shape, BF16),
    ]
    dma = pltpu.SemaphoreType.DMA
    scratch += [dma((len(args),))] + [dma((n,))] * 6 + [dma, dma, dma((n,)), dma((3,))]
    hbm = pl.BlockSpec(memory_space=pltpu.HBM)
    y_out, new_ssm, new_x, new_bc = pl.pallas_call(
        functools.partial(fused_kernel, n),
        out_shape=[
            jax.ShapeDtypeStruct(x_in.shape, BF16),
            jax.ShapeDtypeStruct(ssm_state.shape, F32),
            jax.ShapeDtypeStruct(conv_x_state.shape, BF16),
            jax.ShapeDtypeStruct(conv_bc_state.shape, BF16),
        ],
        in_specs=[hbm] * len(args),
        out_specs=[hbm] * 4,
        scratch_shapes=scratch,
        compiler_params=pltpu.CompilerParams(
            collective_id=0, has_side_effects=True, vmem_limit_bytes=40 * 1024 * 1024
        ),
    )(*args)
    return y_out, new_ssm, new_x, new_bc


def solution(mesh):
    in_specs = (
        P("parts"),
        P("parts"),
        P(("parts", "req"), "tp", None),
        P(("parts", "req"), None, "tp"),
        P(("parts", "req"), None, "tp", None),
        P(("parts", "req"), None, "tp"),
        P(("parts", "req"), None, "tp", None),
        P(("parts", "req"), None, "tp"),
        P(("parts", "req"), None, "tp"),
        P(None, "tp"),
        P("tp"),
        P(None, "tp", None),
        P("tp", None),
        P("tp"),
        P("tp"),
        P("tp"),
        P("tp"),
    )
    out_specs = (
        P(("parts", "req"), None, "tp"),
        P(("parts", "req"), "tp", None),
        P(("parts", "req"), None, "tp"),
        P(("parts", "req"), None, "tp", None),
    )
    return jax.shard_map(
        on_device, mesh=mesh, in_specs=in_specs, out_specs=out_specs, check_vma=False
    )
```

```python
import functools

import jax
import jax.numpy as jnp
from jax import lax
from jax.experimental import pallas as pl
from jax.experimental.pallas import tpu as pltpu
from jax.sharding import PartitionSpec as P

MESH = pl.DeviceIdType.MESH
F32 = jnp.float32
BF16 = jnp.bfloat16
LANES = 128
HALF = 64


def silu(v):
    return v / (1.0 + jnp.exp(-v))


def split(v):
    hi = v.astype(BF16)
    return hi, (v - hi.astype(F32)).astype(BF16)


def mm(a, b):
    return jnp.dot(a, b, preferred_element_type=F32)


def fused_kernel(
    n,
    counts_h,
    plan_h,
    state_h,
    cx_h,
    cb_h,
    x_h,
    bc_h,
    z_h,
    dt_h,
    wx_h,
    bx_h,
    wbc_h,
    bbc_h,
    dtb_h,
    alog_h,
    dskip_h,
    nw_h,
    yv,
    new,
    ncx,
    ncb,
    counts,
    plan,
    state,
    cx,
    cb,
    xv,
    bcv,
    zv,
    dtv,
    wx,
    bx,
    wbc,
    bbc,
    dtb,
    alog,
    dskip,
    nw,
    code,
    spread,
    picked,
    arr,
    hdr,
    gath,
    hf,
    winx,
    winb,
    xc,
    rowt,
    xs,
    gate,
    yb,
    vv,
    dl,
    dcol,
    wc2,
    wcl,
    wb2,
    yr,
    ye,
    ssv,
    ssr,
    in_sem,
    s1,
    r1,
    s2,
    r2,
    sh,
    rh,
    st,
    rt,
):
    slots, heads, cols = state.shape
    steps, channels = xv.shape[1], xv.shape[2]
    groups = bbc.shape[0]
    per = heads // groups
    tiles = cols // LANES
    rows = tiles * heads // n
    ctiles = channels // LANES
    quarter = hf.shape[1]
    parts = channels // quarter
    me = lax.axis_index("req")
    tp = lax.axis_index("tp")
    small = n <= 16
    order = sorted(range(1, n), key=lambda k: (-min(k, n - k), k)) if small else None

    def each(body):
        if small:
            for k in order:
                body(k)
        else:
            lax.fori_loop(1, n, lambda k, c: (body(k), c)[1], 0)

    barrier = pltpu.get_barrier_semaphore()

    def greet(k):
        pl.semaphore_signal(
            barrier, inc=1, device_id={"req": lax.rem(me + k, n)}, device_id_type=MESH
        )

    each(greet)
    pl.semaphore_signal(barrier, inc=1, device_id={"tp": 1 - tp}, device_id_type=MESH)

    pairs = [
        (counts_h, counts),
        (plan_h, plan),
        (state_h, state),
        (cx_h, cx),
        (cb_h, cb),
        (x_h, xv),
        (bc_h, bcv),
        (z_h, zv),
        (dt_h, dtv),
        (wx_h, wx),
        (bx_h, bx),
        (wbc_h, wbc),
        (bbc_h, bbc),
        (dtb_h, dtb),
        (alog_h, alog),
        (dskip_h, dskip),
        (nw_h, nw),
    ]
    loads = [pltpu.make_async_copy(a, b, in_sem.at[i]) for i, (a, b) in enumerate(pairs)]
    for ld in loads:
        ld.start()

    def send(src, dst, ss, rs, k):
        return pltpu.make_async_remote_copy(
            src_ref=src,
            dst_ref=dst,
            send_sem=ss.at[k],
            recv_sem=rs.at[k],
            device_id={"req": lax.rem(me + k, n)},
            device_id_type=MESH,
        )

    def landed(dst, ss, rs, k):
        origin = lax.rem(me + n - k, n)
        pltpu.make_async_remote_copy(
            src_ref=dst.at[origin],
            dst_ref=dst.at[origin],
            send_sem=ss.at[k],
            recv_sem=rs.at[k],
            device_id={"req": origin},
            device_id_type=MESH,
        ).wait_recv()

    def first(k):
        return send(code.at[lax.rem(me + k, n)], spread.at[me], s1, r1, k)

    def second(k):
        return send(picked.at[lax.rem(me + k, n)], arr.at[me], s2, r2, k)

    def heading(k):
        return send(hdr, gath.at[me], sh, rh, k)

    loads[0].wait()
    loads[1].wait()
    one, zero = jnp.int32(1), jnp.int32(0)

    def live(r):
        return (r % slots) < counts[r // slots]

    def leaving(r):
        return live(r) & (plan[r] // slots != r // slots)

    send_j = zero
    for j in range(slots):
        send_j = jnp.where(leaving(me * slots + j), j, send_j)

    sub = lax.broadcasted_iota(jnp.int32, (heads, heads), 0)
    lane = lax.broadcasted_iota(jnp.int32, (heads, heads), 1)
    eye = sub == lane

    def column(row):
        return jnp.sum(jnp.where(eye, row, 0.0), axis=1, keepdims=True)

    def ts(i):
        return slice(i * LANES, (i + 1) * LANES)

    loads[2].wait()
    top = jnp.abs(state[send_j, :, ts(0)])
    for i in range(1, tiles):
        top = jnp.maximum(top, jnp.abs(state[send_j, :, ts(i)]))
    top = jnp.maximum(jnp.max(top, axis=1, keepdims=True), 1e-30)
    unit = (top * (1.0078125 / 32767.0)).astype(BF16).astype(F32)
    inv = 1.0 / unit
    for i in range(tiles):
        q = jnp.round(state[send_j, :, ts(i)] * inv)
        q = q.astype(jnp.int32).astype(jnp.int16)
        chunk = min(rows, heads)
        for at in range(0, heads, chunk):
            row = i * heads + at
            code[row // rows, row % rows:row % rows + chunk, :] = q[at:at + chunk, :]

    loads[3].wait()
    loads[4].wait()
    hf[...] = jnp.zeros_like(hf)

    def tap(j, slot):
        both = cx[j].astype(F32)
        row = both[0:1, :]
        for s in range(1, slots):
            row = jnp.where(slot == s, both[s:s + 1, :], row)
        return row

    for j in range(3):
        row = tap(j, send_j)
        for q in range(parts):
            hf[3 * q + j:3 * q + j + 1, :] = row[:, q * quarter:(q + 1) * quarter]
    for j in range(3):
        pair = cb[send_j, j].astype(F32)
        for g in range(groups):
            hf[3 * parts:3 * parts + 1, ts(j * groups + g)] = pair[g:g + 1, :]
    hf[3 * parts + 1:3 * parts + 2, 0:heads] = jnp.sum(
        jnp.where(eye, unit, 0.0), axis=0, keepdims=True
    )
    hdr[...] = hf[...].astype(BF16)

    pl.semaphore_wait(barrier, n)
    each(lambda k: first(k).start())
    each(lambda k: heading(k).start())
    spread[me] = code[me]
    gath[me] = hdr[...]

    def for_reqs(body, init):
        if small:
            for r in range(n * slots):
                init = body(r, init)
            return init
        return lax.fori_loop(0, n * slots, body, init)

    def scan_mine(r, carry):
        ok = live(r)
        out = []
        for k in range(slots):
            hit, src = carry[2 * k], carry[2 * k + 1]
            m = ok & (plan[r] == me * slots + k)
            out += [jnp.where(m, one, hit), jnp.where(m, r, src)]
        return tuple(out)

    mine_of = for_reqs(scan_mine, (zero,) * (2 * slots))
    hit = [mine_of[2 * k] == 1 for k in range(slots)]
    source = [mine_of[2 * k + 1] for k in range(slots)]
    rec = [hit[k] & (source[k] // slots != me) for k in range(slots)]
    keep = [hit[k] & (source[k] // slots == me) for k in range(slots)]
    k_rec, k_keep, slot_keep, src_me = zero, zero, zero, zero
    for k in range(slots):
        k_rec = jnp.where(rec[k], k, k_rec)
        k_keep = jnp.where(keep[k], k, k_keep)
        slot_keep = jnp.where(keep[k], source[k] % slots, slot_keep)
        src_me = jnp.where(rec[k], source[k] // slots, src_me)
    hit_f = [jnp.where(h, 1.0, 0.0) for h in hit]
    rec_f = [jnp.where(h, 1.0, 0.0) for h in rec]
    keep_f = [jnp.where(h, 1.0, 0.0) for h in keep]

    if small:
        goes = [jnp.where(leaving(jnp.int32(r)), plan[r] // slots, -1) for r in range(n * slots)]

    def source_owner(d):
        if small:
            src = zero
            for r in range(n * slots):
                src = jnp.where(goes[r] == d, r // slots, src)
            return src
        return lax.fori_loop(
            0,
            n * slots,
            lambda r, c: jnp.where(leaving(r) & (plan[r] // slots == d), r // slots, c),
            zero,
        )

    for ld in loads[5:]:
        ld.wait()
    gate[...] = silu(zv[...].astype(F32)).reshape(gate.shape)
    rate = jnp.exp(alog[...])
    skip = column(dskip[...])
    lane1 = lax.broadcasted_iota(jnp.int32, (heads, LANES), 1)
    low = lane1 < HALF
    delta_col, decay_col = [], []
    for k in range(slots):
        raw = dtv[k] + dtb[...]
        delta = jnp.maximum(raw, 0.0) + jnp.log(1.0 + jnp.exp(-jnp.abs(raw)))
        decay = jnp.exp(-delta * rate)
        delta_col.append([column(delta[t:t + 1, :]) for t in range(steps)])
        decay_col.append([column(decay[t:t + 1, :]) for t in range(steps)])
        cum = []
        for t in range(steps):
            cum.append(decay_col[k][t] if t == 0 else cum[-1] * decay_col[k][t])
        for t in range(0, steps, 2):
            dl[k, :, ts(t // 2)] = jnp.where(low, cum[t], cum[t + 1])
        dcol[k] = jnp.broadcast_to(cum[-1], (heads, LANES))
        xk = xv[k].astype(F32)
        winx[k, 3:3 + steps, :] = xk
        for t in range(steps):
            pair = bcv[k, t].astype(F32)
            for g in range(groups):
                winb[k, g, 3 + t:4 + t, :] = pair[g:g + 1, :]
            if t >= steps - 3:
                ncb[k, t - (steps - 3)] = jnp.where(hit[k], pair, 0.0).astype(BF16)

    slot_row = lax.broadcasted_iota(jnp.int32, (slots, channels), 0)
    for j in range(3):
        row = jnp.zeros((slots, channels), F32)
        for k in range(slots):
            new_row = winx[k, steps + j:steps + j + 1, :] * hit_f[k]
            row = jnp.where(slot_row == k, new_row, row)
        ncx[j] = row.astype(BF16)

    each(lambda k: landed(spread, s1, r1, k))

    def pick(k):
        d = lax.rem(me + k, n)
        picked[d] = spread[source_owner(d)]
        second(k).start()

    each(pick)
    arr[me] = spread[src_me]

    each(lambda k: landed(gath, sh, rh, k))
    hf[...] = gath[src_me].astype(F32)
    unit_in = column(hf[3 * parts + 1:3 * parts + 2, 0:heads])
    kept_x = [tap(j, slot_keep) for j in range(3)]
    for k in range(slots):
        for q in range(parts):
            span = slice(q * quarter, (q + 1) * quarter)
            for j in range(3):
                at = 3 * q + j
                winx[k, j:j + 1, span] = jnp.where(
                    keep[k], kept_x[j][:, span], hf[at:at + 1, :]
                )
        for j in range(3):
            pair = cb[slot_keep, j].astype(F32)
            for g in range(groups):
                winb[k, g, j:j + 1, :] = jnp.where(
                    keep[k],
                    pair[g:g + 1, :],
                    hf[3 * parts:3 * parts + 1, ts(j * groups + g)],
                )
        acc = bx[...] + winx[k, 0:steps, :] * wx[0:1, :]
        for j in range(1, 4):
            acc += winx[k, j:j + steps, :] * wx[j:j + 1, :]
        xc[k * steps:(k + 1) * steps, :] = silu(acc)

    every = slots * steps
    for i in range(ctiles):
        rowt[pl.ds(i, every, stride=ctiles), :] = xc[:, ts(i)]
    for kt in range(every):
        r = rowt[kt * ctiles:(kt + 1) * ctiles, :]
        xs[kt, pl.ds(0, ctiles, stride=2), :] = r
        xs[kt, pl.ds(1, ctiles, stride=2), :] = pltpu.roll(r, HALF, 1)

    width = steps * HALF
    lane_w = lax.broadcasted_iota(jnp.int32, (HALF, width), 1)
    even_w = lane_w % 2 == 0
    row_b = lax.broadcasted_iota(jnp.int32, (HALF, LANES), 0)
    lane_b = lax.broadcasted_iota(jnp.int32, (HALF, LANES), 1)
    match_b = (row_b % 2) == (lane_b // HALF)
    for k in range(slots):
        across = []
        for g in range(groups):
            acc = bbc[g:g + 1, :] + winb[k, g, 0:steps, :] * wbc[0, g:g + 1, :]
            for j in range(1, 4):
                acc += winb[k, g, j:j + steps, :] * wbc[j, g:g + 1, :]
            bw = silu(acc)
            turned = pltpu.roll(bw, HALF, 1)
            low4 = lax.broadcasted_iota(jnp.int32, (steps, LANES), 1) < HALF
            b_two = jnp.where(low4, bw, turned)
            c_two = jnp.where(low4, turned, bw)
            across.append(
                [
                    0.5 * jnp.sum(c_two * b_two[s:s + 1, :], axis=1, keepdims=True)
                    for s in range(steps)
                ]
            )
            c_cols = [column(c_two[t:t + 1, 0:HALF]) for t in range(steps)]
            halves = [
                jnp.where(low, c_cols[t], c_cols[t + 1]) for t in range(0, steps, 2)
            ]
            base = jnp.concatenate(halves, axis=1)
            for j in range(2):
                w = jnp.where(even_w == (j == 0), base, 0.0)
                hi, lo = split(w)
                wc2[k, g, j * HALF:(j + 1) * HALF, :] = hi
                wc2[k, g, LANES + j * HALF:LANES + (j + 1) * HALF, :] = hi
                wcl[k, g, j * HALF:(j + 1) * HALF, :] = lo
            for s in range(steps):
                w = jnp.where(match_b, b_two[s:s + 1, :], 0.0)
                hi, lo = split(w)
                wb2[k, g, s * HALF:(s + 1) * HALF, 0:LANES] = hi
                wb2[k, g, s * HALF:(s + 1) * HALF, LANES:2 * LANES] = lo

        def cross(t, s):
            return jnp.concatenate(
                [jnp.broadcast_to(across[g][s][t:t + 1, :], (per, 1)) for g in range(groups)],
                axis=0,
            )

        x_of = [xs[k * steps + t] for t in range(steps)]
        for t in range(steps):
            acc = skip * x_of[t]
            weight = None
            for s in range(t, -1, -1):
                weight = decay_col[k][s + 1] * weight if weight is not None else jnp.ones_like(skip)
                acc += (weight * delta_col[k][s] * cross(t, s)) * x_of[s]
            if t % 2 == 0:
                first_half = acc
            else:
                yb[k, :, ts(t // 2)] = jnp.where(low, first_half, pltpu.roll(acc, HALF, 1))
        weight = None
        v_of = [None] * steps
        for s in range(steps - 1, -1, -1):
            weight = decay_col[k][s + 1] * weight if weight is not None else jnp.ones_like(skip)
            v_of[s] = (weight * delta_col[k][s] * hit_f[k]) * x_of[s]
        for s in range(0, steps, 2):
            vv[k, :, ts(s // 2)] = jnp.where(low, v_of[s], pltpu.roll(v_of[s + 1], HALF, 1))

    batch = 8
    lane_p = (lax.broadcasted_iota(jnp.int32, (per, width), 1) % HALF) // 2
    for g in range(groups):
        hs = slice(g * per, (g + 1) * per)
        acc = jnp.zeros((per, width), F32)
        for b in range(0, tiles, batch):
            parts_s = [state[slot_keep, hs, ts(i)] for i in range(b, b + batch)]
            hi, lo = split(jnp.concatenate(parts_s, axis=0))
            out = mm(jnp.concatenate([hi, lo], axis=1), wc2[k_keep, g]) + mm(hi, wcl[k_keep, g])
            for j in range(batch):
                acc += jnp.where(lane_p == b + j, out[j * per:(j + 1) * per, :], 0.0)
        for k in range(slots):
            yb[k, hs, :] = yb[k, hs, :] + (keep_f[k] * dl[k, hs, :]) * acc
            v = vv[k, hs, :]
            v_hi = v.astype(BF16).astype(F32)
            v_lo = v - v_hi
            scale = keep_f[k] * dcol[k, hs, :]
            for b in range(0, tiles, batch):
                hi = jnp.concatenate(
                    [jnp.where(lane_p == i, v_hi, 0.0) for i in range(b, b + batch)], axis=0
                ).astype(BF16)
                lo = jnp.concatenate(
                    [jnp.where(lane_p == i, v_lo, 0.0) for i in range(b, b + batch)], axis=0
                ).astype(BF16)
                out = mm(hi, wb2[k, g])
                out = out[:, 0:LANES] + out[:, LANES:] + mm(lo, wb2[k, g, :, 0:LANES])
                for j in range(batch):
                    new[k, hs, ts(b + j)] = (
                        scale * state[slot_keep, hs, ts(b + j)] + out[j * per:(j + 1) * per, :]
                    )

    gain = [(rec_f[k] * unit_in) * dcol[k] for k in range(slots)]
    yr[...] = jnp.zeros_like(yr)

    def absorb(whole, start, count):
        q = whole.astype(jnp.int32).astype(F32)
        for j in range(count):
            at = pl.ds(pl.multiple_of((start + j) * LANES, LANES), LANES)
            for k in range(slots):
                new[k, :, at] = new[k, :, at] + gain[k] * q[j * heads:(j + 1) * heads, :]
        for g in range(groups):
            part = jnp.concatenate(
                [q[j * heads + g * per:j * heads + (g + 1) * per, :] for j in range(count)], axis=0
            )
            hi, lo = split(part)
            out = mm(jnp.concatenate([hi, lo], axis=1), wc2[k_rec, g]) + mm(hi, wcl[k_rec, g])
            acc = yr[g * per:(g + 1) * per, :]
            for j in range(count):
                acc += jnp.where(lane_p == start + j, out[j * per:(j + 1) * per, :], 0.0)
            yr[g * per:(g + 1) * per, :] = acc

    if small and rows % heads == 0:
        count = rows // heads
        for k in [0] + order:
            src = lax.rem(me + n - k, n)
            if k:
                landed(arr, s2, r2, k)
            absorb(arr[src], src * count, count)
    else:
        each(lambda k: landed(arr, s2, r2, k))
        some = 4 * heads // rows
        for i in range(tiles // 4):
            absorb(arr[i * some:(i + 1) * some].reshape(4 * heads, LANES), i * 4, 4)

    for k in range(slots):
        y = yb[k] + ((rec_f[k] * unit_in) * dl[k]) * yr[...]
        for p in range(steps // 2):
            ye[...] = y[:, ts(p)]
            even = ye[pl.ds(0, ctiles, stride=2), :]
            odd = ye[pl.ds(1, ctiles, stride=2), :]
            low_c = lax.broadcasted_iota(jnp.int32, (ctiles, LANES), 1) < HALF
            at = (k * steps + 2 * p) * ctiles
            rowt[at:at + ctiles, :] = jnp.where(low_c, even, pltpu.roll(odd, HALF, 1))
            rowt[at + ctiles:at + 2 * ctiles, :] = jnp.where(
                low_c, pltpu.roll(even, HALF, 1), odd
            )
    total = jnp.zeros((every, LANES), F32)
    for i in range(ctiles):
        v = rowt[pl.ds(i, every, stride=ctiles), :] * gate[:, ts(i)]
        xc[:, ts(i)] = v
        total += v * v
    own = jnp.sum(total, axis=1, keepdims=True)
    ssv[...] = jnp.broadcast_to(own, ssv.shape)
    swap = pltpu.make_async_remote_copy(
        src_ref=ssv,
        dst_ref=ssr,
        send_sem=st,
        recv_sem=rt,
        device_id={"tp": 1 - tp},
        device_id_type=MESH,
    )
    swap.start()
    swap.wait_recv()
    both = (ssv[...] + ssr[...])[:, 0:1]
    norm = lax.rsqrt(both * (1.0 / (channels * 2)) + 1e-5)
    for k in range(slots):
        span = slice(k * steps, (k + 1) * steps)
        out = xc[span, :] * norm[span, :] * nw[...]
        yv[k] = jnp.where(hit[k], out, 0.0).astype(BF16)

    swap.wait_send()
    each(lambda k: first(k).wait_send())
    each(lambda k: heading(k).wait_send())
    each(lambda k: second(k).wait_send())

def store_kernel(*refs):
    sem = refs[-1]
    half = (len(refs) - 1) // 2
    copies = [
        pltpu.make_async_copy(refs[i], refs[half + i], sem.at[i]) for i in range(half)
    ]
    for c in copies:
        c.start()
    for c in copies:
        c.wait()


def on_device(
    counts,
    move_plan,
    ssm_state,
    conv_x_state,
    conv_bc_state,
    x_in,
    bc_in,
    z_in,
    dt_in,
    conv_w_x,
    conv_b_x,
    conv_w_bc,
    conv_b_bc,
    dt_bias,
    a_log,
    d_skip,
    norm_w,
):
    n = lax.axis_size("req")
    slots, heads, cols = ssm_state.shape
    _, steps, channels = x_in.shape
    groups = conv_bc_state.shape[2]
    args = (
        counts,
        move_plan,
        ssm_state,
        conv_x_state.transpose(1, 0, 2),
        conv_bc_state,
        x_in,
        bc_in,
        z_in,
        dt_in,
        conv_w_x,
        conv_b_x.reshape(1, -1),
        conv_w_bc,
        conv_b_bc,
        dt_bias.reshape(1, -1),
        a_log.reshape(1, -1),
        d_skip.reshape(1, -1),
        norm_w.reshape(1, -1),
    )
    vm = pltpu.VMEM
    flat = (cols // LANES) * heads
    every = slots * steps
    width = steps * HALF
    quarter = 1024
    scratch = [pltpu.SMEM(a.shape, a.dtype) for a in args[:2]]
    scratch += [vm(a.shape, a.dtype) for a in args[2:]]
    scratch += [vm((n, flat // n, LANES), jnp.int16)] * 4
    scratch += [
        vm((16, quarter), BF16),
        vm((n, 16, quarter), BF16),
        vm((16, quarter), F32),
        vm((slots, 8, channels), F32),
        vm((slots, groups, 8, LANES), F32),
        vm((every, channels), F32),
        vm((every * channels // LANES, LANES), F32),
        vm((every, heads, LANES), F32),
        vm((every, channels), F32),
        vm((slots, heads, width), F32),
        vm((slots, heads, width), F32),
        vm((slots, heads, width), F32),
        vm((slots, heads, LANES), F32),
        vm((slots, groups, 2 * LANES, width), BF16),
        vm((slots, groups, LANES, width), BF16),
        vm((slots, groups, width, 2 * LANES), BF16),
        vm((heads, width), F32),
        vm((heads, LANES), F32),
        vm((every, LANES), F32),
        vm((every, LANES), F32),
    ]
    dma = pltpu.SemaphoreType.DMA
    scratch += [dma((len(args),))] + [dma((n,))] * 6 + [dma, dma]
    outs = [
        jax.ShapeDtypeStruct(x_in.shape, BF16),
        jax.ShapeDtypeStruct(ssm_state.shape, F32),
        jax.ShapeDtypeStruct(args[3].shape, BF16),
        jax.ShapeDtypeStruct(conv_bc_state.shape, BF16),
    ]
    hbm = pl.BlockSpec(memory_space=pltpu.HBM)
    made = pl.pallas_call(
        functools.partial(fused_kernel, n),
        out_shape=[vm(o.shape, o.dtype) for o in outs],
        in_specs=[hbm] * len(args),
        out_specs=[pl.BlockSpec(memory_space=vm)] * len(outs),
        scratch_shapes=scratch,
        compiler_params=pltpu.CompilerParams(
            collective_id=0, has_side_effects=True, vmem_limit_bytes=40 * 1024 * 1024
        ),
    )(*[pltpu.with_memory_space_constraint(a, pltpu.HBM) for a in args])
    made = [pltpu.with_memory_space_constraint(a, vm) for a in made]
    y_out, new_ssm, new_x, new_bc = pl.pallas_call(
        store_kernel,
        out_shape=outs,
        in_specs=[pl.BlockSpec(memory_space=vm)] * len(outs),
        out_specs=[hbm] * len(outs),
        scratch_shapes=[dma((len(outs),))],
    )(*made)
    return y_out, new_ssm, new_x.transpose(1, 0, 2), new_bc


def solution(mesh):
    in_specs = (
        P("parts"),
        P("parts"),
        P(("parts", "req"), "tp", None),
        P(("parts", "req"), None, "tp"),
        P(("parts", "req"), None, "tp", None),
        P(("parts", "req"), None, "tp"),
        P(("parts", "req"), None, "tp", None),
        P(("parts", "req"), None, "tp"),
        P(("parts", "req"), None, "tp"),
        P(None, "tp"),
        P("tp"),
        P(None, "tp", None),
        P("tp", None),
        P("tp"),
        P("tp"),
        P("tp"),
        P("tp"),
    )
    out_specs = (
        P(("parts", "req"), None, "tp"),
        P(("parts", "req"), "tp", None),
        P(("parts", "req"), None, "tp"),
        P(("parts", "req"), None, "tp", None),
    )
    return jax.shard_map(
        on_device, mesh=mesh, in_specs=in_specs, out_specs=out_specs, check_vma=False
    )
```

```python
import functools

import jax
import jax.numpy as jnp
from jax import lax
from jax.experimental import pallas as pl
from jax.experimental.pallas import tpu as pltpu
from jax.sharding import PartitionSpec as P

MESH = pl.DeviceIdType.MESH
F32 = jnp.float32
BF16 = jnp.bfloat16
LANES = 128
HALF = 64
TOP = 32767.0
GRAIN = 6.0 / (TOP * 32000.0)


def silu(v):
    return v / (1.0 + jnp.exp(-v))


def split(v):
    hi = v.astype(BF16)
    return hi, (v - hi.astype(F32)).astype(BF16)


def mm(a, b):
    return jnp.dot(a, b, preferred_element_type=F32)


def fused_kernel(
    n,
    counts_h,
    plan_h,
    state_h,
    cx_h,
    cb_h,
    x_h,
    bc_h,
    z_h,
    dt_h,
    wx_h,
    bx_h,
    wbc_h,
    bbc_h,
    dtb_h,
    alog_h,
    dskip_h,
    nw_h,
    yv,
    new,
    ncx,
    ncb,
    counts,
    plan,
    state,
    cx,
    cb,
    xv,
    bcv,
    zv,
    dtv,
    wx,
    bx,
    wbc,
    bbc,
    dtb,
    alog,
    dskip,
    nw,
    code,
    spread,
    picked,
    arr,
    harr,
    hf,
    winx,
    winb,
    xc,
    rowt,
    xs,
    gate,
    yb,
    vv,
    dl,
    dcol,
    wc2,
    wcl,
    wb2,
    yr,
    ye,
    made,
    ssv,
    ssr,
    in_sem,
    s1,
    r1,
    s2,
    r2,
    s3,
    r3,
    st,
    rt,
):
    slots, heads, cols = state.shape
    steps, channels = xv.shape[1], xv.shape[2]
    groups = bbc.shape[0]
    per = heads // groups
    tiles = cols // LANES
    rows = arr.shape[1]
    ctiles = channels // LANES
    extra = harr.shape[1]
    row_bc = 3 * ctiles
    row_unit = row_bc + 3 * groups
    me = lax.axis_index("req")
    tp = lax.axis_index("tp")
    small = n <= 16
    order = sorted(range(1, n), key=lambda k: (-min(k, n - k), k)) if small else None

    def each(body):
        if small:
            for k in order:
                body(k)
        else:
            lax.fori_loop(1, n, lambda k, c: (body(k), c)[1], 0)

    barrier = pltpu.get_barrier_semaphore()

    def greet(k):
        pl.semaphore_signal(
            barrier, inc=1, device_id={"req": lax.rem(me + k, n)}, device_id_type=MESH
        )

    each(greet)
    pl.semaphore_signal(barrier, inc=1, device_id={"tp": 1 - tp}, device_id_type=MESH)

    pairs = [
        (counts_h, counts),
        (plan_h, plan),
        (state_h, state),
        (cx_h, cx),
        (cb_h, cb),
        (x_h, xv),
        (bc_h, bcv),
        (z_h, zv),
        (dt_h, dtv),
        (wx_h, wx),
        (bx_h, bx),
        (wbc_h, wbc),
        (bbc_h, bbc),
        (dtb_h, dtb),
        (alog_h, alog),
        (dskip_h, dskip),
        (nw_h, nw),
    ]
    loads = [pltpu.make_async_copy(a, b, in_sem.at[i]) for i, (a, b) in enumerate(pairs)]
    for ld in loads:
        ld.start()

    def send(src, dst, ss, rs, k):
        return pltpu.make_async_remote_copy(
            src_ref=src,
            dst_ref=dst,
            send_sem=ss.at[k],
            recv_sem=rs.at[k],
            device_id={"req": lax.rem(me + k, n)},
            device_id_type=MESH,
        )

    def landed(dst, ss, rs, k):
        origin = lax.rem(me + n - k, n)
        pltpu.make_async_remote_copy(
            src_ref=dst.at[origin],
            dst_ref=dst.at[origin],
            send_sem=ss.at[k],
            recv_sem=rs.at[k],
            device_id={"req": origin},
            device_id_type=MESH,
        ).wait_recv()

    def first(k):
        return send(code.at[lax.rem(me + k, n)], spread.at[me], s1, r1, k)

    def second(k):
        d = lax.rem(me + k, n)
        return send(picked.at[d, pl.ds(0, rows)], arr.at[me], s2, r2, k)

    def third(k):
        d = lax.rem(me + k, n)
        return send(picked.at[d, pl.ds(rows, extra)], harr.at[me], s3, r3, k)

    loads[0].wait()
    loads[1].wait()
    one, zero = jnp.int32(1), jnp.int32(0)

    def live(r):
        return (r % slots) < counts[r // slots]

    def leaving(r):
        return live(r) & (plan[r] // slots != r // slots)

    send_j = zero
    for j in range(slots):
        send_j = jnp.where(leaving(me * slots + j), j, send_j)

    sub = lax.broadcasted_iota(jnp.int32, (heads, heads), 0)
    lane = lax.broadcasted_iota(jnp.int32, (heads, heads), 1)
    eye = sub == lane

    def column(row):
        return jnp.sum(jnp.where(eye, row, 0.0), axis=1, keepdims=True)

    def ts(i):
        return slice(i * LANES, (i + 1) * LANES)

    loads[2].wait()
    top = jnp.abs(state[send_j, :, ts(0)])
    for i in range(1, tiles):
        top = jnp.maximum(top, jnp.abs(state[send_j, :, ts(i)]))

    def grains(v):
        return jnp.minimum(jnp.floor(v * (1.0 / (TOP * GRAIN))) + 1.0, TOP)

    unit = grains(jnp.max(top, axis=1, keepdims=True))
    inv = 1.0 / (unit * GRAIN)
    for i in range(tiles):
        q = jnp.round(state[send_j, :, ts(i)] * inv)
        q = q.astype(jnp.int32).astype(jnp.int16)
        chunk = min(rows, heads)
        for at in range(0, heads, chunk):
            row = i * heads + at
            code[row // rows, row % rows:row % rows + chunk, :] = q[at:at + chunk, :]

    loads[3].wait()
    loads[4].wait()
    hf[...] = jnp.zeros_like(hf)

    def tap(j, slot):
        both = cx[j].astype(F32)
        row = both[0:1, :]
        for s in range(1, slots):
            row = jnp.where(slot == s, both[s:s + 1, :], row)
        return row

    hf[row_unit:row_unit + 1, 0:heads] = jnp.sum(jnp.where(eye, unit, 0.0), axis=0, keepdims=True)
    for j in range(3):
        row = tap(j, send_j)
        x_unit = grains(jnp.max(jnp.abs(row), axis=1, keepdims=True))
        row = jnp.round(row * (1.0 / (x_unit * GRAIN)))
        for i in range(ctiles):
            hf[j * ctiles + i:j * ctiles + i + 1, :] = row[:, ts(i)]
        pair = cb[send_j, j].astype(F32)
        bc_unit = grains(jnp.max(jnp.abs(pair), axis=1, keepdims=True))
        hf[row_bc + j * groups:row_bc + (j + 1) * groups, :] = jnp.round(
            pair * (1.0 / (bc_unit * GRAIN))
        )
        hf[row_unit + 1 + j:row_unit + 2 + j, :] = jnp.broadcast_to(x_unit, (1, LANES))
        at = row_unit + 4 + j * groups
        hf[at:at + groups, :] = jnp.broadcast_to(bc_unit, (groups, LANES))
    for i in range(n):
        part = hf[i * extra:(i + 1) * extra, :]
        code[i, rows:rows + extra, :] = part.astype(jnp.int32).astype(jnp.int16)

    pl.semaphore_wait(barrier, n)
    each(lambda k: first(k).start())
    spread[me] = code[me]

    def for_reqs(body, init):
        if small:
            for r in range(n * slots):
                init = body(r, init)
            return init
        return lax.fori_loop(0, n * slots, body, init)

    def scan_mine(r, carry):
        ok = live(r)
        out = []
        for k in range(slots):
            hit, src = carry[2 * k], carry[2 * k + 1]
            m = ok & (plan[r] == me * slots + k)
            out += [jnp.where(m, one, hit), jnp.where(m, r, src)]
        return tuple(out)

    mine_of = for_reqs(scan_mine, (zero,) * (2 * slots))
    hit = [mine_of[2 * k] == 1 for k in range(slots)]
    source = [mine_of[2 * k + 1] for k in range(slots)]
    rec = [hit[k] & (source[k] // slots != me) for k in range(slots)]
    keep = [hit[k] & (source[k] // slots == me) for k in range(slots)]
    k_rec, k_keep, slot_keep, src_me = zero, zero, zero, zero
    for k in range(slots):
        k_rec = jnp.where(rec[k], k, k_rec)
        k_keep = jnp.where(keep[k], k, k_keep)
        slot_keep = jnp.where(keep[k], source[k] % slots, slot_keep)
        src_me = jnp.where(rec[k], source[k] // slots, src_me)
    if small:
        goes = [jnp.where(leaving(jnp.int32(r)), plan[r] // slots, -1) for r in range(n * slots)]

    def source_owner(d):
        if small:
            src = zero
            for r in range(n * slots):
                src = jnp.where(goes[r] == d, r // slots, src)
            return src
        return lax.fori_loop(
            0,
            n * slots,
            lambda r, c: jnp.where(leaving(r) & (plan[r] // slots == d), r // slots, c),
            zero,
        )

    for ld in loads[5:]:
        ld.wait()
    rate = jnp.exp(alog[...])
    skip = column(dskip[...])
    width = steps * HALF
    low = lax.broadcasted_iota(jnp.int32, (heads, LANES), 1) < HALF
    low4 = lax.broadcasted_iota(jnp.int32, (steps, LANES), 1) < HALF
    low_c = lax.broadcasted_iota(jnp.int32, (ctiles, LANES), 1) < HALF
    lane_w = lax.broadcasted_iota(jnp.int32, (HALF, width), 1)
    even_w = lane_w % 2 == 0
    row_b = lax.broadcasted_iota(jnp.int32, (HALF, LANES), 0)
    lane_b = lax.broadcasted_iota(jnp.int32, (HALF, LANES), 1)
    match_b = (row_b % 2) == (lane_b // HALF)
    lane_p = (lax.broadcasted_iota(jnp.int32, (per, width), 1) % HALF) // 2
    batch = 8

    def convolve(role, place):
        winx[role, 3:3 + steps, :] = xv[place].astype(F32)
        for t in range(steps):
            pair = bcv[place, t].astype(F32)
            for g in range(groups):
                winb[role, g, 3 + t:4 + t, :] = pair[g:g + 1, :]
        acc = bx[...] + winx[role, 0:steps, :] * wx[0:1, :]
        for j in range(1, 4):
            acc += winx[role, j:j + steps, :] * wx[j:j + 1, :]
        acc = silu(acc)
        for i in range(ctiles):
            rowt[pl.ds(i, steps, stride=ctiles), :] = acc[:, ts(i)]
        for t in range(steps):
            r = rowt[t * ctiles:(t + 1) * ctiles, :]
            xs[t, pl.ds(0, ctiles, stride=2), :] = r
            xs[t, pl.ds(1, ctiles, stride=2), :] = pltpu.roll(r, HALF, 1)

    def prepare(role, place):
        gate[role] = silu(zv[place].astype(F32))
        raw = dtv[place] + dtb[...]
        delta = jnp.maximum(raw, 0.0) + jnp.log(1.0 + jnp.exp(-jnp.abs(raw)))
        decay = jnp.exp(-delta * rate)
        delta_col = [column(delta[t:t + 1, :]) for t in range(steps)]
        decay_col = [column(decay[t:t + 1, :]) for t in range(steps)]
        cum = [decay_col[0]]
        for t in range(1, steps):
            cum.append(cum[-1] * decay_col[t])
        for t in range(0, steps, 2):
            dl[role, :, ts(t // 2)] = jnp.where(low, cum[t], cum[t + 1])
        dcol[role] = jnp.broadcast_to(cum[-1], (heads, LANES))
        across = []
        for g in range(groups):
            acc = bbc[g:g + 1, :] + winb[role, g, 0:steps, :] * wbc[0, g:g + 1, :]
            for j in range(1, 4):
                acc += winb[role, g, j:j + steps, :] * wbc[j, g:g + 1, :]
            bw = silu(acc)
            turned = pltpu.roll(bw, HALF, 1)
            b_two = jnp.where(low4, bw, turned)
            c_two = jnp.where(low4, turned, bw)
            across.append(
                [
                    0.5 * jnp.sum(c_two * b_two[s:s + 1, :], axis=1, keepdims=True)
                    for s in range(steps)
                ]
            )
            c_cols = [column(c_two[t:t + 1, 0:HALF]) for t in range(steps)]
            halves = [
                jnp.where(low, c_cols[t], c_cols[t + 1]) for t in range(0, steps, 2)
            ]
            base = jnp.concatenate(halves, axis=1)
            for j in range(2):
                w = jnp.where(even_w == (j == 0), base, 0.0)
                hi, lo = split(w)
                wc2[role, g, j * HALF:(j + 1) * HALF, :] = hi
                wc2[role, g, LANES + j * HALF:LANES + (j + 1) * HALF, :] = hi
                wcl[role, g, j * HALF:(j + 1) * HALF, :] = lo
            for s in range(steps):
                w = jnp.where(match_b, b_two[s:s + 1, :], 0.0)
                hi, lo = split(w)
                wb2[g, s * HALF:(s + 1) * HALF, 0:LANES] = hi
                wb2[g, s * HALF:(s + 1) * HALF, LANES:2 * LANES] = lo

        def cross(t, s):
            return jnp.concatenate(
                [jnp.broadcast_to(across[g][s][t:t + 1, :], (per, 1)) for g in range(groups)],
                axis=0,
            )

        x_of = [xs[t] for t in range(steps)]
        for t in range(steps):
            acc = skip * x_of[t]
            weight = jnp.ones_like(skip)
            for s in range(t, -1, -1):
                acc += (weight * delta_col[s] * cross(t, s)) * x_of[s]
                weight = decay_col[s] * weight
            if t % 2 == 0:
                first_half = acc
            else:
                yb[role, :, ts(t // 2)] = jnp.where(low, first_half, pltpu.roll(acc, HALF, 1))
        weight = jnp.ones_like(skip)
        v_of = [None] * steps
        for s in range(steps - 1, -1, -1):
            v_of[s] = (weight * delta_col[s]) * x_of[s]
            weight = decay_col[s] * weight
        for s in range(0, steps, 2):
            vv[:, ts(s // 2)] = jnp.where(low, v_of[s], pltpu.roll(v_of[s + 1], HALF, 1))

    def added(role):
        for g in range(groups):
            hs = slice(g * per, (g + 1) * per)
            v = vv[hs, :]
            v_hi = v.astype(BF16).astype(F32)
            v_lo = v - v_hi
            for b in range(0, tiles, batch):
                hi = jnp.concatenate(
                    [jnp.where(lane_p == i, v_hi, 0.0) for i in range(b, b + batch)], axis=0
                ).astype(BF16)
                lo = jnp.concatenate(
                    [jnp.where(lane_p == i, v_lo, 0.0) for i in range(b, b + batch)], axis=0
                ).astype(BF16)
                out = mm(hi, wb2[g])
                out = out[:, 0:LANES] + out[:, LANES:] + mm(lo, wb2[g, :, 0:LANES])
                for j in range(batch):
                    got = out[j * per:(j + 1) * per, :]
                    if role == 0:
                        got += dcol[0, hs, :] * state[slot_keep, hs, ts(b + j)]
                    made[role, hs, ts(b + j)] = got

    def to_rows(role, y):
        for p in range(steps // 2):
            ye[...] = y[:, ts(p)]
            even = ye[pl.ds(0, ctiles, stride=2), :]
            odd = ye[pl.ds(1, ctiles, stride=2), :]
            at = 2 * p * ctiles
            rowt[at:at + ctiles, :] = jnp.where(low_c, even, pltpu.roll(odd, HALF, 1))
            rowt[at + ctiles:at + 2 * ctiles, :] = jnp.where(
                low_c, pltpu.roll(even, HALF, 1), odd
            )
        total = jnp.zeros((steps, LANES), F32)
        for i in range(ctiles):
            v = rowt[pl.ds(i, steps, stride=ctiles), :] * gate[role, :, ts(i)]
            xc[role, :, ts(i)] = v
            total += v * v
        own = jnp.sum(total, axis=1, keepdims=True)
        ssv[role] = jnp.broadcast_to(own, ssv.shape[1:])

    slot_row = lax.broadcasted_iota(jnp.int32, (slots, channels), 0)
    for j in range(3):
        row = jnp.zeros((slots, channels), F32)
        for k in range(slots):
            new_row = xv[k].astype(F32)[steps - 3 + j:steps - 2 + j, :]
            row = jnp.where(slot_row == k, jnp.where(hit[k], new_row, 0.0), row)
        ncx[j] = row.astype(BF16)
        for k in range(slots):
            pair = bcv[k, steps - 3 + j].astype(F32)
            ncb[k, j] = jnp.where(hit[k], pair, 0.0).astype(BF16)
    for j in range(3):
        winx[0, j:j + 1, :] = tap(j, slot_keep)
        pair = cb[slot_keep, j].astype(F32)
        for g in range(groups):
            winb[0, g, j:j + 1, :] = pair[g:g + 1, :]
    convolve(0, k_keep)
    prepare(0, k_keep)
    added(0)
    for g in range(groups):
        hs = slice(g * per, (g + 1) * per)
        acc = jnp.zeros((per, width), F32)
        for b in range(0, tiles, batch):
            parts_s = [state[slot_keep, hs, ts(i)] for i in range(b, b + batch)]
            hi, lo = split(jnp.concatenate(parts_s, axis=0))
            out = mm(jnp.concatenate([hi, lo], axis=1), wc2[0, g]) + mm(hi, wcl[0, g])
            for j in range(batch):
                acc += jnp.where(lane_p == b + j, out[j * per:(j + 1) * per, :], 0.0)
        yb[0, hs, :] = yb[0, hs, :] + dl[0, hs, :] * acc
    to_rows(0, yb[0])
    owner_for = {k: source_owner(lax.rem(me + k, n)) for k in order} if small else None

    def origin_of(k):
        return owner_for[k] if small else source_owner(lax.rem(me + k, n))

    each(lambda k: landed(spread, s1, r1, k))

    def pick_extra(k):
        picked[lax.rem(me + k, n), rows:, :] = spread[origin_of(k), rows:, :]
        third(k).start()

    def pick(k):
        picked[lax.rem(me + k, n), 0:rows, :] = spread[origin_of(k), 0:rows, :]
        second(k).start()

    each(pick_extra)
    each(pick)
    arr[me] = spread[src_me, 0:rows, :]
    harr[me] = spread[src_me, rows:, :]

    each(lambda k: landed(harr, s3, r3, k))
    for i in range(n):
        hf[i * extra:(i + 1) * extra, :] = harr[i].astype(jnp.int32).astype(F32)
    unit_in = column(hf[row_unit:row_unit + 1, 0:heads]) * GRAIN
    for j in range(3):
        x_unit = hf[row_unit + 1 + j:row_unit + 2 + j, :] * GRAIN
        for i in range(ctiles):
            at = j * ctiles + i
            winx[1, j:j + 1, ts(i)] = hf[at:at + 1, :] * x_unit
        for g in range(groups):
            at = j * groups + g
            winb[1, g, j:j + 1, :] = hf[row_bc + at:row_bc + at + 1, :] * (
                hf[row_unit + 4 + at:row_unit + 5 + at, :] * GRAIN
            )
    convolve(1, k_rec)
    prepare(1, k_rec)
    added(1)

    gain = unit_in * dcol[1]
    yr[...] = jnp.zeros_like(yr)

    def absorb(whole, start, count):
        q = whole.astype(jnp.int32).astype(F32)
        for j in range(count):
            at = pl.ds(pl.multiple_of((start + j) * LANES, LANES), LANES)
            arrived = made[1, :, at] + gain * q[j * heads:(j + 1) * heads, :]
            stayed = made[0, :, at]
            for k in range(slots):
                new[k, :, at] = jnp.where(
                    rec[k], arrived, jnp.where(keep[k], stayed, 0.0)
                )
        for g in range(groups):
            part = jnp.concatenate(
                [q[j * heads + g * per:j * heads + (g + 1) * per, :] for j in range(count)], axis=0
            )
            hi, lo = split(part)
            out = mm(jnp.concatenate([hi, lo], axis=1), wc2[1, g]) + mm(hi, wcl[1, g])
            acc = yr[g * per:(g + 1) * per, :]
            for j in range(count):
                acc += jnp.where(lane_p == start + j, out[j * per:(j + 1) * per, :], 0.0)
            yr[g * per:(g + 1) * per, :] = acc

    if small and rows % heads == 0:
        count = rows // heads
        for k in [0] + order:
            src = lax.rem(me + n - k, n)
            if k:
                landed(arr, s2, r2, k)
            absorb(arr[src], src * count, count)
    else:
        each(lambda k: landed(arr, s2, r2, k))
        some = 4 * heads // rows
        for i in range(tiles // 4):
            absorb(arr[i * some:(i + 1) * some].reshape(4 * heads, LANES), i * 4, 4)

    to_rows(1, yb[1] + (unit_in * dl[1]) * yr[...])
    swap = pltpu.make_async_remote_copy(
        src_ref=ssv,
        dst_ref=ssr,
        send_sem=st,
        recv_sem=rt,
        device_id={"tp": 1 - tp},
        device_id_type=MESH,
    )
    swap.start()
    swap.wait_recv()
    outs = []
    for role in range(2):
        both = (ssv[role] + ssr[role])[:, 0:1]
        norm = lax.rsqrt(both * (1.0 / (channels * 2)) + 1e-5)
        outs.append(xc[role] * norm * nw[...])
    for k in range(slots):
        yv[k] = jnp.where(rec[k], outs[1], jnp.where(keep[k], outs[0], 0.0)).astype(BF16)

    swap.wait_send()
    each(lambda k: first(k).wait_send())
    each(lambda k: second(k).wait_send())
    each(lambda k: third(k).wait_send())


def store_kernel(*refs):
    sem = refs[-1]
    half = (len(refs) - 1) // 2
    copies = [
        pltpu.make_async_copy(refs[i], refs[half + i], sem.at[i]) for i in range(half)
    ]
    for c in copies:
        c.start()
    for c in copies:
        c.wait()


def on_device(
    counts,
    move_plan,
    ssm_state,
    conv_x_state,
    conv_bc_state,
    x_in,
    bc_in,
    z_in,
    dt_in,
    conv_w_x,
    conv_b_x,
    conv_w_bc,
    conv_b_bc,
    dt_bias,
    a_log,
    d_skip,
    norm_w,
):
    n = lax.axis_size("req")
    slots, heads, cols = ssm_state.shape
    _, steps, channels = x_in.shape
    groups = conv_bc_state.shape[2]
    args = (
        counts,
        move_plan,
        ssm_state,
        conv_x_state.transpose(1, 0, 2),
        conv_bc_state,
        x_in,
        bc_in,
        z_in,
        dt_in,
        conv_w_x,
        conv_b_x.reshape(1, -1),
        conv_w_bc,
        conv_b_bc,
        dt_bias.reshape(1, -1),
        a_log.reshape(1, -1),
        d_skip.reshape(1, -1),
        norm_w.reshape(1, -1),
    )
    vm = pltpu.VMEM
    flat = (cols // LANES) * heads
    width = steps * HALF
    extra_rows = 3 * (channels // LANES) + 6 * groups + 4
    extra = -(-extra_rows // (16 * n)) * 16
    scratch = [pltpu.SMEM(a.shape, a.dtype) for a in args[:2]]
    scratch += [vm(a.shape, a.dtype) for a in args[2:]]
    scratch += [vm((n, flat // n + extra, LANES), jnp.int16)] * 3
    scratch += [
        vm((n, flat // n, LANES), jnp.int16),
        vm((n, extra, LANES), jnp.int16),
        vm((n * extra, LANES), F32),
        vm((2, 8, channels), F32),
        vm((2, groups, 8, LANES), F32),
        vm((2, steps, channels), F32),
        vm((steps * channels // LANES, LANES), F32),
        vm((steps, heads, LANES), F32),
        vm((2, steps, channels), F32),
        vm((2, heads, width), F32),
        vm((heads, width), F32),
        vm((2, heads, width), F32),
        vm((2, heads, LANES), F32),
        vm((2, groups, 2 * LANES, width), BF16),
        vm((2, groups, LANES, width), BF16),
        vm((groups, width, 2 * LANES), BF16),
        vm((heads, width), F32),
        vm((heads, LANES), F32),
        vm((2, heads, cols), F32),
        vm((2, steps, LANES), F32),
        vm((2, steps, LANES), F32),
    ]
    dma = pltpu.SemaphoreType.DMA
    scratch += [dma((len(args),))] + [dma((n,))] * 6 + [dma, dma]
    outs = [
        jax.ShapeDtypeStruct(x_in.shape, BF16),
        jax.ShapeDtypeStruct(ssm_state.shape, F32),
        jax.ShapeDtypeStruct(args[3].shape, BF16),
        jax.ShapeDtypeStruct(conv_bc_state.shape, BF16),
    ]
    hbm = pl.BlockSpec(memory_space=pltpu.HBM)
    made = pl.pallas_call(
        functools.partial(fused_kernel, n),
        out_shape=[vm(o.shape, o.dtype) for o in outs],
        in_specs=[hbm] * len(args),
        out_specs=[pl.BlockSpec(memory_space=vm)] * len(outs),
        scratch_shapes=scratch,
        compiler_params=pltpu.CompilerParams(
            collective_id=0, has_side_effects=True, vmem_limit_bytes=40 * 1024 * 1024
        ),
    )(*[pltpu.with_memory_space_constraint(a, pltpu.HBM) for a in args])
    made = [pltpu.with_memory_space_constraint(a, vm) for a in made]
    y_out, new_ssm, new_x, new_bc = pl.pallas_call(
        store_kernel,
        out_shape=outs,
        in_specs=[pl.BlockSpec(memory_space=vm)] * len(outs),
        out_specs=[hbm] * len(outs),
        scratch_shapes=[dma((len(outs),))],
    )(*made)
    return y_out, new_ssm, new_x.transpose(1, 0, 2), new_bc


def solution(mesh):
    in_specs = (
        P("parts"),
        P("parts"),
        P(("parts", "req"), "tp", None),
        P(("parts", "req"), None, "tp"),
        P(("parts", "req"), None, "tp", None),
        P(("parts", "req"), None, "tp"),
        P(("parts", "req"), None, "tp", None),
        P(("parts", "req"), None, "tp"),
        P(("parts", "req"), None, "tp"),
        P(None, "tp"),
        P("tp"),
        P(None, "tp", None),
        P("tp", None),
        P("tp"),
        P("tp"),
        P("tp"),
        P("tp"),
    )
    out_specs = (
        P(("parts", "req"), None, "tp"),
        P(("parts", "req"), "tp", None),
        P(("parts", "req"), None, "tp"),
        P(("parts", "req"), None, "tp", None),
    )
    return jax.shard_map(
        on_device, mesh=mesh, in_specs=in_specs, out_specs=out_specs, check_vma=False
    )
```

```python
import functools

import jax
import jax.numpy as jnp
from jax import lax
from jax.experimental import pallas as pl
from jax.experimental.pallas import tpu as pltpu
from jax.sharding import PartitionSpec as P

MESH = pl.DeviceIdType.MESH
F32 = jnp.float32
BF16 = jnp.bfloat16
LANES = 128
HALF = 64
LATE = 3
TOP = 32767.0
GRAIN = 6.0 / (TOP * 32000.0)


def silu(v):
    return v / (1.0 + jnp.exp(-v))


def split(v):
    hi = v.astype(BF16)
    return hi, (v - hi.astype(F32)).astype(BF16)


def mm(a, b):
    return jnp.dot(a, b, preferred_element_type=F32)


def fused_kernel(
    n,
    counts_h,
    plan_h,
    state_h,
    cx_h,
    cb_h,
    x_h,
    bc_h,
    z_h,
    dt_h,
    wx_h,
    bx_h,
    wbc_h,
    bbc_h,
    dtb_h,
    alog_h,
    dskip_h,
    nw_h,
    yv,
    new,
    ncx,
    ncb,
    counts,
    plan,
    state,
    cx,
    cb,
    xv,
    bcv,
    zv,
    dtv,
    wx,
    bx,
    wbc,
    bbc,
    dtb,
    alog,
    dskip,
    nw,
    code,
    spread,
    picked,
    arr,
    harr,
    hf,
    winx,
    winb,
    xc,
    rowt,
    xs,
    gate,
    yb,
    vv,
    dl,
    dcol,
    wc2,
    wcl,
    wb2,
    yr,
    ye,
    made,
    ssv,
    ssr,
    in_sem,
    s1,
    r1,
    s2,
    r2,
    s3,
    r3,
    st,
    rt,
):
    slots, heads, cols = state.shape
    steps, channels = xv.shape[1], xv.shape[2]
    groups = bbc.shape[0]
    per = heads // groups
    tiles = cols // LANES
    rows = arr.shape[1]
    ctiles = channels // LANES
    extra = harr.shape[1]
    row_bc = 3 * ctiles
    row_unit = row_bc + 3 * groups
    me = lax.axis_index("req")
    tp = lax.axis_index("tp")
    small = n <= 16
    order = sorted(range(1, n), key=lambda k: (-min(k, n - k), k)) if small else None
    turns = [4, 1, 7, 3, 5, 2, 6] if n == 8 else order

    def each(body, which=None):
        if small:
            for k in which or order:
                body(k)
        else:
            lax.fori_loop(1, n, lambda k, c: (body(k), c)[1], 0)

    barrier = pltpu.get_barrier_semaphore()

    def greet(k):
        pl.semaphore_signal(
            barrier, inc=1, device_id={"req": lax.rem(me + k, n)}, device_id_type=MESH
        )

    each(greet)
    pl.semaphore_signal(barrier, inc=1, device_id={"tp": 1 - tp}, device_id_type=MESH)

    pairs = [
        (counts_h, counts),
        (plan_h, plan),
        (state_h, state),
        (cx_h, cx),
        (cb_h, cb),
        (x_h, xv),
        (bc_h, bcv),
        (z_h, zv),
        (dt_h, dtv),
        (wx_h, wx),
        (bx_h, bx),
        (wbc_h, wbc),
        (bbc_h, bbc),
        (dtb_h, dtb),
        (alog_h, alog),
        (dskip_h, dskip),
        (nw_h, nw),
    ]
    loads = [pltpu.make_async_copy(a, b, in_sem.at[i]) for i, (a, b) in enumerate(pairs)]
    for ld in loads:
        ld.start()

    def send(src, dst, ss, rs, k):
        return pltpu.make_async_remote_copy(
            src_ref=src,
            dst_ref=dst,
            send_sem=ss.at[k],
            recv_sem=rs.at[k],
            device_id={"req": lax.rem(me + k, n)},
            device_id_type=MESH,
        )

    def landed(dst, ss, rs, k):
        origin = lax.rem(me + n - k, n)
        pltpu.make_async_remote_copy(
            src_ref=dst.at[origin],
            dst_ref=dst.at[origin],
            send_sem=ss.at[k],
            recv_sem=rs.at[k],
            device_id={"req": origin},
            device_id_type=MESH,
        ).wait_recv()

    def first(k):
        return send(code.at[lax.rem(me + k, n)], spread.at[me], s1, r1, k)

    def second(k):
        d = lax.rem(me + k, n)
        return send(picked.at[d, pl.ds(0, rows)], arr.at[me], s2, r2, k)

    def third(k):
        d = lax.rem(me + k, n)
        return send(picked.at[d, pl.ds(rows, extra)], harr.at[me], s3, r3, k)

    loads[0].wait()
    loads[1].wait()
    one, zero = jnp.int32(1), jnp.int32(0)

    def live(r):
        return (r % slots) < counts[r // slots]

    def leaving(r):
        return live(r) & (plan[r] // slots != r // slots)

    send_j = zero
    for j in range(slots):
        send_j = jnp.where(leaving(me * slots + j), j, send_j)

    sub = lax.broadcasted_iota(jnp.int32, (heads, heads), 0)
    lane = lax.broadcasted_iota(jnp.int32, (heads, heads), 1)
    eye = sub == lane

    def column(row):
        return jnp.sum(jnp.where(eye, row, 0.0), axis=1, keepdims=True)

    def ts(i):
        return slice(i * LANES, (i + 1) * LANES)

    loads[2].wait()
    top = jnp.abs(state[send_j, :, ts(0)])
    for i in range(1, tiles):
        top = jnp.maximum(top, jnp.abs(state[send_j, :, ts(i)]))

    def grains(v):
        return jnp.minimum(jnp.floor(v * (1.0 / (TOP * GRAIN))) + 1.0, TOP)

    unit = grains(jnp.max(top, axis=1, keepdims=True))
    inv = 1.0 / (unit * GRAIN)
    for i in range(tiles):
        q = jnp.round(state[send_j, :, ts(i)] * inv)
        q = q.astype(jnp.int32).astype(jnp.int16)
        chunk = min(rows, heads)
        for at in range(0, heads, chunk):
            row = i * heads + at
            code[row // rows, row % rows:row % rows + chunk, :] = q[at:at + chunk, :]

    loads[3].wait()
    loads[4].wait()
    hf[...] = jnp.zeros_like(hf)

    def tap(j, slot):
        both = cx[j].astype(F32)
        row = both[0:1, :]
        for s in range(1, slots):
            row = jnp.where(slot == s, both[s:s + 1, :], row)
        return row

    hf[row_unit:row_unit + 1, 0:heads] = jnp.sum(jnp.where(eye, unit, 0.0), axis=0, keepdims=True)
    for j in range(3):
        row = tap(j, send_j)
        x_unit = grains(jnp.max(jnp.abs(row), axis=1, keepdims=True))
        row = jnp.round(row * (1.0 / (x_unit * GRAIN)))
        for i in range(ctiles):
            hf[j * ctiles + i:j * ctiles + i + 1, :] = row[:, ts(i)]
        pair = cb[send_j, j].astype(F32)
        bc_unit = grains(jnp.max(jnp.abs(pair), axis=1, keepdims=True))
        hf[row_bc + j * groups:row_bc + (j + 1) * groups, :] = jnp.round(
            pair * (1.0 / (bc_unit * GRAIN))
        )
        hf[row_unit + 1 + j:row_unit + 2 + j, :] = jnp.broadcast_to(x_unit, (1, LANES))
        at = row_unit + 4 + j * groups
        hf[at:at + groups, :] = jnp.broadcast_to(bc_unit, (groups, LANES))
    for i in range(n):
        part = hf[i * extra:(i + 1) * extra, :]
        code[i, rows:rows + extra, :] = part.astype(jnp.int32).astype(jnp.int16)

    pl.semaphore_wait(barrier, n)
    each(lambda k: first(k).start())
    spread[me] = code[me]

    def for_reqs(body, init):
        if small:
            for r in range(n * slots):
                init = body(r, init)
            return init
        return lax.fori_loop(0, n * slots, body, init)

    def scan_mine(r, carry):
        ok = live(r)
        out = []
        for k in range(slots):
            hit, src = carry[2 * k], carry[2 * k + 1]
            m = ok & (plan[r] == me * slots + k)
            out += [jnp.where(m, one, hit), jnp.where(m, r, src)]
        return tuple(out)

    mine_of = for_reqs(scan_mine, (zero,) * (2 * slots))
    hit = [mine_of[2 * k] == 1 for k in range(slots)]
    source = [mine_of[2 * k + 1] for k in range(slots)]
    rec = [hit[k] & (source[k] // slots != me) for k in range(slots)]
    keep = [hit[k] & (source[k] // slots == me) for k in range(slots)]
    k_rec, k_keep, slot_keep, src_me = zero, zero, zero, zero
    for k in range(slots):
        k_rec = jnp.where(rec[k], k, k_rec)
        k_keep = jnp.where(keep[k], k, k_keep)
        slot_keep = jnp.where(keep[k], source[k] % slots, slot_keep)
        src_me = jnp.where(rec[k], source[k] // slots, src_me)
    if small:
        goes = [jnp.where(leaving(jnp.int32(r)), plan[r] // slots, -1) for r in range(n * slots)]

    def source_owner(d):
        if small:
            src = zero
            for r in range(n * slots):
                src = jnp.where(goes[r] == d, r // slots, src)
            return src
        return lax.fori_loop(
            0,
            n * slots,
            lambda r, c: jnp.where(leaving(r) & (plan[r] // slots == d), r // slots, c),
            zero,
        )

    for ld in loads[5:]:
        ld.wait()
    rate = jnp.exp(alog[...])
    skip = column(dskip[...])
    width = steps * HALF
    low = lax.broadcasted_iota(jnp.int32, (heads, LANES), 1) < HALF
    low4 = lax.broadcasted_iota(jnp.int32, (steps, LANES), 1) < HALF
    low_c = lax.broadcasted_iota(jnp.int32, (ctiles, LANES), 1) < HALF
    lane_w = lax.broadcasted_iota(jnp.int32, (HALF, width), 1)
    even_w = lane_w % 2 == 0
    row_b = lax.broadcasted_iota(jnp.int32, (HALF, LANES), 0)
    lane_b = lax.broadcasted_iota(jnp.int32, (HALF, LANES), 1)
    match_b = (row_b % 2) == (lane_b // HALF)
    lane_p = (lax.broadcasted_iota(jnp.int32, (per, width), 1) % HALF) // 2
    batch = 8

    def convolve(role, place):
        winx[role, 3:3 + steps, :] = xv[place].astype(F32)
        for t in range(steps):
            pair = bcv[place, t].astype(F32)
            for g in range(groups):
                winb[role, g, 3 + t:4 + t, :] = pair[g:g + 1, :]
        acc = bx[...] + winx[role, 0:steps, :] * wx[0:1, :]
        for j in range(1, 4):
            acc += winx[role, j:j + steps, :] * wx[j:j + 1, :]
        acc = silu(acc)
        for i in range(ctiles):
            rowt[pl.ds(i, steps, stride=ctiles), :] = acc[:, ts(i)]
        for t in range(steps):
            r = rowt[t * ctiles:(t + 1) * ctiles, :]
            xs[t, pl.ds(0, ctiles, stride=2), :] = r
            xs[t, pl.ds(1, ctiles, stride=2), :] = pltpu.roll(r, HALF, 1)

    def prepare(role, place):
        gate[role] = silu(zv[place].astype(F32))
        raw = dtv[place] + dtb[...]
        delta = jnp.maximum(raw, 0.0) + jnp.log(1.0 + jnp.exp(-jnp.abs(raw)))
        decay = jnp.exp(-delta * rate)
        delta_col = [column(delta[t:t + 1, :]) for t in range(steps)]
        decay_col = [column(decay[t:t + 1, :]) for t in range(steps)]
        cum = [decay_col[0]]
        for t in range(1, steps):
            cum.append(cum[-1] * decay_col[t])
        for t in range(0, steps, 2):
            dl[role, :, ts(t // 2)] = jnp.where(low, cum[t], cum[t + 1])
        dcol[role] = jnp.broadcast_to(cum[-1], (heads, LANES))
        across = []
        for g in range(groups):
            acc = bbc[g:g + 1, :] + winb[role, g, 0:steps, :] * wbc[0, g:g + 1, :]
            for j in range(1, 4):
                acc += winb[role, g, j:j + steps, :] * wbc[j, g:g + 1, :]
            bw = silu(acc)
            turned = pltpu.roll(bw, HALF, 1)
            b_two = jnp.where(low4, bw, turned)
            c_two = jnp.where(low4, turned, bw)
            across.append(
                [
                    0.5 * jnp.sum(c_two * b_two[s:s + 1, :], axis=1, keepdims=True)
                    for s in range(steps)
                ]
            )
            c_cols = [column(c_two[t:t + 1, 0:HALF]) for t in range(steps)]
            halves = [
                jnp.where(low, c_cols[t], c_cols[t + 1]) for t in range(0, steps, 2)
            ]
            base = jnp.concatenate(halves, axis=1)
            for j in range(2):
                w = jnp.where(even_w == (j == 0), base, 0.0)
                hi, lo = split(w)
                wc2[role, g, j * HALF:(j + 1) * HALF, :] = hi
                wc2[role, g, LANES + j * HALF:LANES + (j + 1) * HALF, :] = hi
                wcl[role, g, j * HALF:(j + 1) * HALF, :] = lo
            for s in range(steps):
                w = jnp.where(match_b, b_two[s:s + 1, :], 0.0)
                hi, lo = split(w)
                wb2[g, s * HALF:(s + 1) * HALF, 0:LANES] = hi
                wb2[g, s * HALF:(s + 1) * HALF, LANES:2 * LANES] = lo

        def cross(t, s):
            return jnp.concatenate(
                [jnp.broadcast_to(across[g][s][t:t + 1, :], (per, 1)) for g in range(groups)],
                axis=0,
            )

        x_of = [xs[t] for t in range(steps)]
        for t in range(steps):
            acc = skip * x_of[t]
            weight = jnp.ones_like(skip)
            for s in range(t, -1, -1):
                acc += (weight * delta_col[s] * cross(t, s)) * x_of[s]
                weight = decay_col[s] * weight
            if t % 2 == 0:
                first_half = acc
            else:
                yb[role, :, ts(t // 2)] = jnp.where(low, first_half, pltpu.roll(acc, HALF, 1))
        weight = jnp.ones_like(skip)
        v_of = [None] * steps
        for s in range(steps - 1, -1, -1):
            v_of[s] = (weight * delta_col[s]) * x_of[s]
            weight = decay_col[s] * weight
        for s in range(0, steps, 2):
            vv[:, ts(s // 2)] = jnp.where(low, v_of[s], pltpu.roll(v_of[s + 1], HALF, 1))

    def added(role):
        for g in range(groups):
            hs = slice(g * per, (g + 1) * per)
            v = vv[hs, :]
            v_hi = v.astype(BF16).astype(F32)
            v_lo = v - v_hi
            for b in range(0, tiles, batch):
                hi = jnp.concatenate(
                    [jnp.where(lane_p == i, v_hi, 0.0) for i in range(b, b + batch)], axis=0
                ).astype(BF16)
                lo = jnp.concatenate(
                    [jnp.where(lane_p == i, v_lo, 0.0) for i in range(b, b + batch)], axis=0
                ).astype(BF16)
                out = mm(hi, wb2[g])
                out = out[:, 0:LANES] + out[:, LANES:] + mm(lo, wb2[g, :, 0:LANES])
                for j in range(batch):
                    got = out[j * per:(j + 1) * per, :]
                    if role == 0:
                        got += dcol[0, hs, :] * state[slot_keep, hs, ts(b + j)]
                    made[role, hs, ts(b + j)] = got

    def to_rows(role, y):
        for p in range(steps // 2):
            ye[...] = y[:, ts(p)]
            even = ye[pl.ds(0, ctiles, stride=2), :]
            odd = ye[pl.ds(1, ctiles, stride=2), :]
            at = 2 * p * ctiles
            rowt[at:at + ctiles, :] = jnp.where(low_c, even, pltpu.roll(odd, HALF, 1))
            rowt[at + ctiles:at + 2 * ctiles, :] = jnp.where(
                low_c, pltpu.roll(even, HALF, 1), odd
            )
        total = jnp.zeros((steps, LANES), F32)
        for i in range(ctiles):
            v = rowt[pl.ds(i, steps, stride=ctiles), :] * gate[role, :, ts(i)]
            xc[role, :, ts(i)] = v
            total += v * v
        own = jnp.sum(total, axis=1, keepdims=True)
        ssv[role] = jnp.broadcast_to(own, ssv.shape[1:])

    swaps = [
        pltpu.make_async_remote_copy(
            src_ref=ssv.at[role],
            dst_ref=ssr.at[role],
            send_sem=st.at[role],
            recv_sem=rt.at[role],
            device_id={"tp": 1 - tp},
            device_id_type=MESH,
        )
        for role in range(2)
    ]

    def finish(role):
        swaps[role].wait_recv()
        both = (ssv[role] + ssr[role])[:, 0:1]
        norm = lax.rsqrt(both * (1.0 / (channels * 2)) + 1e-5)
        out = xc[role] * norm * nw[...]
        for k in range(slots):
            if role == 0:
                yv[k] = jnp.where(keep[k], out, 0.0).astype(BF16)
            else:
                yv[k] = jnp.where(rec[k], out, yv[k].astype(F32)).astype(BF16)

    slot_row = lax.broadcasted_iota(jnp.int32, (slots, channels), 0)
    for j in range(3):
        row = jnp.zeros((slots, channels), F32)
        for k in range(slots):
            new_row = xv[k].astype(F32)[steps - 3 + j:steps - 2 + j, :]
            row = jnp.where(slot_row == k, jnp.where(hit[k], new_row, 0.0), row)
        ncx[j] = row.astype(BF16)
        for k in range(slots):
            pair = bcv[k, steps - 3 + j].astype(F32)
            ncb[k, j] = jnp.where(hit[k], pair, 0.0).astype(BF16)
    for j in range(3):
        winx[0, j:j + 1, :] = tap(j, slot_keep)
        pair = cb[slot_keep, j].astype(F32)
        for g in range(groups):
            winb[0, g, j:j + 1, :] = pair[g:g + 1, :]
    convolve(0, k_keep)
    prepare(0, k_keep)
    added(0)
    for g in range(groups):
        hs = slice(g * per, (g + 1) * per)
        acc = jnp.zeros((per, width), F32)
        for b in range(0, tiles, batch):
            parts_s = [state[slot_keep, hs, ts(i)] for i in range(b, b + batch)]
            hi, lo = split(jnp.concatenate(parts_s, axis=0))
            out = mm(jnp.concatenate([hi, lo], axis=1), wc2[0, g]) + mm(hi, wcl[0, g])
            for j in range(batch):
                acc += jnp.where(lane_p == b + j, out[j * per:(j + 1) * per, :], 0.0)
        yb[0, hs, :] = yb[0, hs, :] + dl[0, hs, :] * acc
    to_rows(0, yb[0])
    swaps[0].start()
    owner_for = {k: source_owner(lax.rem(me + k, n)) for k in order} if small else None

    def origin_of(k):
        return owner_for[k] if small else source_owner(lax.rem(me + k, n))

    each(lambda k: landed(spread, s1, r1, k))

    def pick_extra(k):
        picked[lax.rem(me + k, n), rows:, :] = spread[origin_of(k), rows:, :]
        third(k).start()

    def pick(k):
        picked[lax.rem(me + k, n), 0:rows, :] = spread[origin_of(k), 0:rows, :]
        second(k).start()

    each(pick_extra)
    each(pick, turns if small else None)
    arr[me] = spread[src_me, 0:rows, :]
    harr[me] = spread[src_me, rows:, :]

    each(lambda k: landed(harr, s3, r3, k))
    for i in range(n):
        hf[i * extra:(i + 1) * extra, :] = harr[i].astype(jnp.int32).astype(F32)
    unit_in = column(hf[row_unit:row_unit + 1, 0:heads]) * GRAIN
    for j in range(3):
        x_unit = hf[row_unit + 1 + j:row_unit + 2 + j, :] * GRAIN
        for i in range(ctiles):
            at = j * ctiles + i
            winx[1, j:j + 1, ts(i)] = hf[at:at + 1, :] * x_unit
        for g in range(groups):
            at = j * groups + g
            winb[1, g, j:j + 1, :] = hf[row_bc + at:row_bc + at + 1, :] * (
                hf[row_unit + 4 + at:row_unit + 5 + at, :] * GRAIN
            )
    finish(0)
    convolve(1, k_rec)
    prepare(1, k_rec)
    added(1)

    gain = unit_in * dcol[1]
    yr[...] = jnp.zeros_like(yr)

    def renew(whole, start, count):
        q = whole.astype(jnp.int32).astype(F32)
        for j in range(count):
            at = pl.ds(pl.multiple_of((start + j) * LANES, LANES), LANES)
            arrived = made[1, :, at] + gain * q[j * heads:(j + 1) * heads, :]
            stayed = made[0, :, at]
            for k in range(slots):
                new[k, :, at] = jnp.where(
                    rec[k], arrived, jnp.where(keep[k], stayed, 0.0)
                )

    def absorb(whole, start, count):
        q = whole.astype(jnp.int32).astype(F32)
        for g in range(groups):
            part = jnp.concatenate(
                [q[j * heads + g * per:j * heads + (g + 1) * per, :] for j in range(count)], axis=0
            )
            hi, lo = split(part)
            out = mm(jnp.concatenate([hi, lo], axis=1), wc2[1, g]) + mm(hi, wcl[1, g])
            acc = yr[g * per:(g + 1) * per, :]
            for j in range(count):
                acc += jnp.where(lane_p == start + j, out[j * per:(j + 1) * per, :], 0.0)
            yr[g * per:(g + 1) * per, :] = acc

    if small and rows % heads == 0:
        count = rows // heads
        late = turns[-LATE:]
        for k in [0] + turns:
            src = lax.rem(me + n - k, n)
            if k:
                landed(arr, s2, r2, k)
            absorb(arr[src], src * count, count)
            if k not in late:
                renew(arr[src], src * count, count)
    else:
        each(lambda k: landed(arr, s2, r2, k))
        some = 4 * heads // rows
        for i in range(tiles // 4):
            whole = arr[i * some:(i + 1) * some].reshape(4 * heads, LANES)
            absorb(whole, i * 4, 4)
            renew(whole, i * 4, 4)

    to_rows(1, yb[1] + (unit_in * dl[1]) * yr[...])
    swaps[1].start()
    if small and rows % heads == 0:
        for k in late:
            src = lax.rem(me + n - k, n)
            renew(arr[src], src * count, count)
    finish(1)
    for sw in swaps:
        sw.wait_send()
    each(lambda k: first(k).wait_send())
    each(lambda k: second(k).wait_send())
    each(lambda k: third(k).wait_send())


def store_kernel(*refs):
    sem = refs[-1]
    half = (len(refs) - 1) // 2
    copies = []
    for a, b in zip(refs[:half], refs[half:-1]):
        cuts = 4 if a.shape[1] % 32 == 0 else 1
        size = a.shape[1] // cuts
        for s in range(a.shape[0] if cuts > 1 else 1):
            for c in range(cuts):
                at = (s, pl.ds(c * size, size)) if cuts > 1 else slice(None)
                copies.append(pltpu.make_async_copy(a.at[at], b.at[at], sem.at[len(copies)]))
    for c in copies:
        c.start()
    for c in copies:
        c.wait()


def on_device(
    counts,
    move_plan,
    ssm_state,
    conv_x_state,
    conv_bc_state,
    x_in,
    bc_in,
    z_in,
    dt_in,
    conv_w_x,
    conv_b_x,
    conv_w_bc,
    conv_b_bc,
    dt_bias,
    a_log,
    d_skip,
    norm_w,
):
    n = lax.axis_size("req")
    slots, heads, cols = ssm_state.shape
    _, steps, channels = x_in.shape
    groups = conv_bc_state.shape[2]
    args = (
        counts,
        move_plan,
        ssm_state,
        conv_x_state.transpose(1, 0, 2),
        conv_bc_state,
        x_in,
        bc_in,
        z_in,
        dt_in,
        conv_w_x,
        conv_b_x.reshape(1, -1),
        conv_w_bc,
        conv_b_bc,
        dt_bias.reshape(1, -1),
        a_log.reshape(1, -1),
        d_skip.reshape(1, -1),
        norm_w.reshape(1, -1),
    )
    vm = pltpu.VMEM
    flat = (cols // LANES) * heads
    width = steps * HALF
    extra_rows = 3 * (channels // LANES) + 6 * groups + 4
    extra = -(-extra_rows // (16 * n)) * 16
    scratch = [pltpu.SMEM(a.shape, a.dtype) for a in args[:2]]
    scratch += [vm(a.shape, a.dtype) for a in args[2:]]
    scratch += [vm((n, flat // n + extra, LANES), jnp.int16)] * 3
    scratch += [
        vm((n, flat // n, LANES), jnp.int16),
        vm((n, extra, LANES), jnp.int16),
        vm((n * extra, LANES), F32),
        vm((2, 8, channels), F32),
        vm((2, groups, 8, LANES), F32),
        vm((2, steps, channels), F32),
        vm((steps * channels // LANES, LANES), F32),
        vm((steps, heads, LANES), F32),
        vm((2, steps, channels), F32),
        vm((2, heads, width), F32),
        vm((heads, width), F32),
        vm((2, heads, width), F32),
        vm((2, heads, LANES), F32),
        vm((2, groups, 2 * LANES, width), BF16),
        vm((2, groups, LANES, width), BF16),
        vm((groups, width, 2 * LANES), BF16),
        vm((heads, width), F32),
        vm((heads, LANES), F32),
        vm((2, heads, cols), F32),
        vm((2, steps, LANES), F32),
        vm((2, steps, LANES), F32),
    ]
    dma = pltpu.SemaphoreType.DMA
    scratch += [dma((len(args),))] + [dma((n,))] * 6 + [dma((2,)), dma((2,))]
    outs = [
        jax.ShapeDtypeStruct(x_in.shape, BF16),
        jax.ShapeDtypeStruct(ssm_state.shape, F32),
        jax.ShapeDtypeStruct(args[3].shape, BF16),
        jax.ShapeDtypeStruct(conv_bc_state.shape, BF16),
    ]
    hbm = pl.BlockSpec(memory_space=pltpu.HBM)
    made = pl.pallas_call(
        functools.partial(fused_kernel, n),
        out_shape=[vm(o.shape, o.dtype) for o in outs],
        in_specs=[hbm] * len(args),
        out_specs=[pl.BlockSpec(memory_space=vm)] * len(outs),
        scratch_shapes=scratch,
        compiler_params=pltpu.CompilerParams(
            collective_id=0, has_side_effects=True, vmem_limit_bytes=40 * 1024 * 1024
        ),
    )(*[pltpu.with_memory_space_constraint(a, pltpu.HBM) for a in args])
    made = [pltpu.with_memory_space_constraint(a, vm) for a in made]
    y_out, new_ssm, new_x, new_bc = pl.pallas_call(
        store_kernel,
        out_shape=outs,
        in_specs=[pl.BlockSpec(memory_space=vm)] * len(outs),
        out_specs=[hbm] * len(outs),
        scratch_shapes=[dma((16,))],
    )(*made)
    return y_out, new_ssm, new_x.transpose(1, 0, 2), new_bc


def solution(mesh):
    in_specs = (
        P("parts"),
        P("parts"),
        P(("parts", "req"), "tp", None),
        P(("parts", "req"), None, "tp"),
        P(("parts", "req"), None, "tp", None),
        P(("parts", "req"), None, "tp"),
        P(("parts", "req"), None, "tp", None),
        P(("parts", "req"), None, "tp"),
        P(("parts", "req"), None, "tp"),
        P(None, "tp"),
        P("tp"),
        P(None, "tp", None),
        P("tp", None),
        P("tp"),
        P("tp"),
        P("tp"),
        P("tp"),
    )
    out_specs = (
        P(("parts", "req"), None, "tp"),
        P(("parts", "req"), "tp", None),
        P(("parts", "req"), None, "tp"),
        P(("parts", "req"), None, "tp", None),
    )
    return jax.shard_map(
        on_device, mesh=mesh, in_specs=in_specs, out_specs=out_specs, check_vma=False
    )
```

```python
import functools

import jax
import jax.numpy as jnp
from jax import lax
from jax.experimental import pallas as pl
from jax.experimental.pallas import tpu as pltpu
from jax.sharding import PartitionSpec as P

MESH = pl.DeviceIdType.MESH
F32 = jnp.float32
BF16 = jnp.bfloat16
LANES = 128
HALF = 64
LATE = 4
PAIR = 4
TOP = 32767.0
GRAIN = 6.0 / (TOP * 32000.0)


def silu(v):
    return v / (1.0 + jnp.exp(-v))


def split(v):
    hi = v.astype(BF16)
    return hi, (v - hi.astype(F32)).astype(BF16)


def mm(a, b):
    return jnp.dot(a, b, preferred_element_type=F32)


def fused_kernel(
    n,
    counts_h,
    plan_h,
    state_h,
    cx_h,
    cb_h,
    x_h,
    bc_h,
    z_h,
    dt_h,
    wx_h,
    bx_h,
    wbc_h,
    bbc_h,
    dtb_h,
    alog_h,
    dskip_h,
    nw_h,
    yv,
    new,
    ncx,
    ncb,
    counts,
    plan,
    state,
    cx,
    cb,
    xv,
    bcv,
    zv,
    dtv,
    wx,
    bx,
    wbc,
    bbc,
    dtb,
    alog,
    dskip,
    nw,
    code,
    spread,
    picked,
    arr,
    hf,
    winx,
    winb,
    xc,
    rowt,
    xs,
    gate,
    yb,
    vv,
    dl,
    dcol,
    wc2,
    wcl,
    wb2,
    yr,
    ye,
    made,
    ssv,
    ssr,
    in_sem,
    s1,
    r1,
    s2,
    r2,
    s3,
    r3,
    st,
    rt,
):
    slots, heads, cols = state.shape
    steps, channels = xv.shape[1], xv.shape[2]
    groups = bbc.shape[0]
    per = heads // groups
    tiles = cols // LANES
    rows = tiles * heads // n
    ctiles = channels // LANES
    extra = hf.shape[0] // n
    small = n <= 16
    whole_tiles = small and rows % heads == 0
    cut = extra if whole_tiles else extra + rows
    row_bc = 3 * ctiles
    row_unit = row_bc + 3 * groups
    me = lax.axis_index("req")
    tp = lax.axis_index("tp")
    order = sorted(range(1, n), key=lambda k: (-min(k, n - k), k)) if small else None
    hellos = order[::-1] if small else None
    turns = order
    if n == 8:
        order = [4, 5, 3, 6, 2, 7, 1]
        turns = [4, 1, 7, 3, 5, 2, 6]

    def each(body, which=None):
        if small:
            for k in which or order:
                body(k)
        else:
            lax.fori_loop(1, n, lambda k, c: (body(k), c)[1], 0)

    barrier = pltpu.get_barrier_semaphore()

    def greet(k):
        pl.semaphore_signal(
            barrier, inc=1, device_id={"req": lax.rem(me + k, n)}, device_id_type=MESH
        )

    each(greet, hellos)
    pl.semaphore_signal(barrier, inc=1, device_id={"tp": 1 - tp}, device_id_type=MESH)

    pairs = [
        (counts_h, counts),
        (plan_h, plan),
        (state_h, state),
        (cx_h, cx),
        (cb_h, cb),
        (x_h, xv),
        (bc_h, bcv),
        (z_h, zv),
        (dt_h, dtv),
        (wx_h, wx),
        (bx_h, bx),
        (wbc_h, wbc),
        (bbc_h, bbc),
        (dtb_h, dtb),
        (alog_h, alog),
        (dskip_h, dskip),
        (nw_h, nw),
    ]
    loads = [pltpu.make_async_copy(a, b, in_sem.at[i]) for i, (a, b) in enumerate(pairs)]
    for ld in loads:
        ld.start()

    def send(src, dst, ss, rs, k):
        return pltpu.make_async_remote_copy(
            src_ref=src,
            dst_ref=dst,
            send_sem=ss.at[k],
            recv_sem=rs.at[k],
            device_id={"req": lax.rem(me + k, n)},
            device_id_type=MESH,
        )

    def landed(dst, at, ss, rs, k):
        origin = lax.rem(me + n - k, n)
        pltpu.make_async_remote_copy(
            src_ref=dst.at[origin, at],
            dst_ref=dst.at[origin, at],
            send_sem=ss.at[k],
            recv_sem=rs.at[k],
            device_id={"req": origin},
            device_id_type=MESH,
        ).wait_recv()

    whole = pl.ds(0, extra + rows)
    fore = pl.ds(0, cut)
    rear = pl.ds(cut, extra + rows - cut)

    def first(k):
        return send(code.at[lax.rem(me + k, n)], spread.at[me], s1, r1, k)

    def second(k):
        return send(picked.at[lax.rem(me + k, n), fore], arr.at[me, fore], s2, r2, k)

    def third(k):
        return send(picked.at[lax.rem(me + k, n), rear], arr.at[me, rear], s3, r3, k)

    loads[0].wait()
    loads[1].wait()
    one, zero = jnp.int32(1), jnp.int32(0)

    def live(r):
        return (r % slots) < counts[r // slots]

    def leaving(r):
        return live(r) & (plan[r] // slots != r // slots)

    send_j = zero
    for j in range(slots):
        send_j = jnp.where(leaving(me * slots + j), j, send_j)

    sub = lax.broadcasted_iota(jnp.int32, (heads, heads), 0)
    lane = lax.broadcasted_iota(jnp.int32, (heads, heads), 1)
    eye = sub == lane

    def column(row):
        return jnp.sum(jnp.where(eye, row, 0.0), axis=1, keepdims=True)

    def ts(i):
        return slice(i * LANES, (i + 1) * LANES)

    loads[2].wait()
    top = jnp.abs(state[send_j, :, ts(0)])
    for i in range(1, tiles):
        top = jnp.maximum(top, jnp.abs(state[send_j, :, ts(i)]))

    def grains(v):
        return jnp.minimum(jnp.floor(v * (1.0 / (TOP * GRAIN))) + 1.0, TOP)

    unit = grains(jnp.max(top, axis=1, keepdims=True))
    inv = 1.0 / (unit * GRAIN)
    for i in range(tiles):
        q = jnp.round(state[send_j, :, ts(i)] * inv)
        q = q.astype(jnp.int32).astype(jnp.int16)
        chunk = min(rows, heads)
        for at in range(0, heads, chunk):
            row = i * heads + at
            to = extra + row % rows
            code[row // rows, to:to + chunk, :] = q[at:at + chunk, :]

    loads[3].wait()
    loads[4].wait()
    hf[...] = jnp.zeros_like(hf)

    def tap(j, slot):
        both = cx[j].astype(F32)
        row = both[0:1, :]
        for s in range(1, slots):
            row = jnp.where(slot == s, both[s:s + 1, :], row)
        return row

    hf[row_unit:row_unit + 1, 0:heads] = jnp.sum(jnp.where(eye, unit, 0.0), axis=0, keepdims=True)
    for j in range(3):
        row = tap(j, send_j)
        x_unit = grains(jnp.max(jnp.abs(row), axis=1, keepdims=True))
        row = jnp.round(row * (1.0 / (x_unit * GRAIN)))
        for i in range(ctiles):
            hf[j * ctiles + i:j * ctiles + i + 1, :] = row[:, ts(i)]
        pair = cb[send_j, j].astype(F32)
        bc_unit = grains(jnp.max(jnp.abs(pair), axis=1, keepdims=True))
        hf[row_bc + j * groups:row_bc + (j + 1) * groups, :] = jnp.round(
            pair * (1.0 / (bc_unit * GRAIN))
        )
        hf[row_unit + 1 + j:row_unit + 2 + j, :] = jnp.broadcast_to(x_unit, (1, LANES))
        at = row_unit + 4 + j * groups
        hf[at:at + groups, :] = jnp.broadcast_to(bc_unit, (groups, LANES))
    for i in range(n):
        part = hf[i * extra:(i + 1) * extra, :]
        code[i, 0:extra, :] = part.astype(jnp.int32).astype(jnp.int16)

    pl.semaphore_wait(barrier, n)
    each(lambda k: first(k).start())
    spread[me] = code[me]

    def for_reqs(body, init):
        if small:
            for r in range(n * slots):
                init = body(r, init)
            return init
        return lax.fori_loop(0, n * slots, body, init)

    def scan_mine(r, carry):
        ok = live(r)
        out = []
        for k in range(slots):
            hit, src = carry[2 * k], carry[2 * k + 1]
            m = ok & (plan[r] == me * slots + k)
            out += [jnp.where(m, one, hit), jnp.where(m, r, src)]
        return tuple(out)

    mine_of = for_reqs(scan_mine, (zero,) * (2 * slots))
    hit = [mine_of[2 * k] == 1 for k in range(slots)]
    source = [mine_of[2 * k + 1] for k in range(slots)]
    rec = [hit[k] & (source[k] // slots != me) for k in range(slots)]
    keep = [hit[k] & (source[k] // slots == me) for k in range(slots)]
    k_rec, k_keep, slot_keep, src_me = zero, zero, zero, zero
    for k in range(slots):
        k_rec = jnp.where(rec[k], k, k_rec)
        k_keep = jnp.where(keep[k], k, k_keep)
        slot_keep = jnp.where(keep[k], source[k] % slots, slot_keep)
        src_me = jnp.where(rec[k], source[k] // slots, src_me)
    if small:
        goes = [jnp.where(leaving(jnp.int32(r)), plan[r] // slots, -1) for r in range(n * slots)]

    def source_owner(d):
        if small:
            src = zero
            for r in range(n * slots):
                src = jnp.where(goes[r] == d, r // slots, src)
            return src
        return lax.fori_loop(
            0,
            n * slots,
            lambda r, c: jnp.where(leaving(r) & (plan[r] // slots == d), r // slots, c),
            zero,
        )

    for ld in loads[5:]:
        ld.wait()
    rate = jnp.exp(alog[...])
    skip = column(dskip[...])
    width = steps * HALF
    low = lax.broadcasted_iota(jnp.int32, (heads, LANES), 1) < HALF
    low4 = lax.broadcasted_iota(jnp.int32, (steps, LANES), 1) < HALF
    low_c = lax.broadcasted_iota(jnp.int32, (ctiles, LANES), 1) < HALF
    lane_w = lax.broadcasted_iota(jnp.int32, (HALF, width), 1)
    even_w = lane_w % 2 == 0
    row_b = lax.broadcasted_iota(jnp.int32, (HALF, LANES), 0)
    lane_b = lax.broadcasted_iota(jnp.int32, (HALF, LANES), 1)
    match_b = (row_b % 2) == (lane_b // HALF)
    lane_p = (lax.broadcasted_iota(jnp.int32, (per, width), 1) % HALF) // 2
    batch = 8

    def convolve(role, place):
        winx[role, 3:3 + steps, :] = xv[place].astype(F32)
        for t in range(steps):
            pair = bcv[place, t].astype(F32)
            for g in range(groups):
                winb[role, g, 3 + t:4 + t, :] = pair[g:g + 1, :]
        acc = bx[...] + winx[role, 0:steps, :] * wx[0:1, :]
        for j in range(1, 4):
            acc += winx[role, j:j + steps, :] * wx[j:j + 1, :]
        acc = silu(acc)
        for i in range(ctiles):
            rowt[pl.ds(i, steps, stride=ctiles), :] = acc[:, ts(i)]
        for t in range(steps):
            r = rowt[t * ctiles:(t + 1) * ctiles, :]
            xs[t, pl.ds(0, ctiles, stride=2), :] = r
            xs[t, pl.ds(1, ctiles, stride=2), :] = pltpu.roll(r, HALF, 1)

    def prepare(role, place):
        gate[role] = silu(zv[place].astype(F32))
        raw = dtv[place] + dtb[...]
        delta = jnp.maximum(raw, 0.0) + jnp.log(1.0 + jnp.exp(-jnp.abs(raw)))
        decay = jnp.exp(-delta * rate)
        delta_col = [column(delta[t:t + 1, :]) for t in range(steps)]
        decay_col = [column(decay[t:t + 1, :]) for t in range(steps)]
        cum = [decay_col[0]]
        for t in range(1, steps):
            cum.append(cum[-1] * decay_col[t])
        for t in range(0, steps, 2):
            dl[role, :, ts(t // 2)] = jnp.where(low, cum[t], cum[t + 1])
        dcol[role] = jnp.broadcast_to(cum[-1], (heads, LANES))
        across = []
        for g in range(groups):
            acc = bbc[g:g + 1, :] + winb[role, g, 0:steps, :] * wbc[0, g:g + 1, :]
            for j in range(1, 4):
                acc += winb[role, g, j:j + steps, :] * wbc[j, g:g + 1, :]
            bw = silu(acc)
            turned = pltpu.roll(bw, HALF, 1)
            b_two = jnp.where(low4, bw, turned)
            c_two = jnp.where(low4, turned, bw)
            across.append(
                [
                    0.5 * jnp.sum(c_two * b_two[s:s + 1, :], axis=1, keepdims=True)
                    for s in range(steps)
                ]
            )
            c_cols = [column(c_two[t:t + 1, 0:HALF]) for t in range(steps)]
            halves = [
                jnp.where(low, c_cols[t], c_cols[t + 1]) for t in range(0, steps, 2)
            ]
            base = jnp.concatenate(halves, axis=1)
            for j in range(2):
                w = jnp.where(even_w == (j == 0), base, 0.0)
                hi, lo = split(w)
                wc2[role, g, j * HALF:(j + 1) * HALF, :] = hi
                wc2[role, g, LANES + j * HALF:LANES + (j + 1) * HALF, :] = hi
                wcl[role, g, j * HALF:(j + 1) * HALF, :] = lo
            for s in range(steps):
                w = jnp.where(match_b, b_two[s:s + 1, :], 0.0)
                hi, lo = split(w)
                wb2[g, s * HALF:(s + 1) * HALF, 0:LANES] = hi
                wb2[g, s * HALF:(s + 1) * HALF, LANES:2 * LANES] = lo

        def cross(t, s):
            return jnp.concatenate(
                [jnp.broadcast_to(across[g][s][t:t + 1, :], (per, 1)) for g in range(groups)],
                axis=0,
            )

        x_of = [xs[t] for t in range(steps)]
        for t in range(steps):
            acc = skip * x_of[t]
            weight = jnp.ones_like(skip)
            for s in range(t, -1, -1):
                acc += (weight * delta_col[s] * cross(t, s)) * x_of[s]
                weight = decay_col[s] * weight
            if t % 2 == 0:
                first_half = acc
            else:
                yb[role, :, ts(t // 2)] = jnp.where(low, first_half, pltpu.roll(acc, HALF, 1))
        weight = jnp.ones_like(skip)
        v_of = [None] * steps
        for s in range(steps - 1, -1, -1):
            v_of[s] = (weight * delta_col[s]) * x_of[s]
            weight = decay_col[s] * weight
        for s in range(0, steps, 2):
            vv[:, ts(s // 2)] = jnp.where(low, v_of[s], pltpu.roll(v_of[s + 1], HALF, 1))

    def added(role):
        for g in range(groups):
            hs = slice(g * per, (g + 1) * per)
            v = vv[hs, :]
            v_hi = v.astype(BF16).astype(F32)
            v_lo = v - v_hi
            for b in range(0, tiles, batch):
                hi = jnp.concatenate(
                    [jnp.where(lane_p == i, v_hi, 0.0) for i in range(b, b + batch)], axis=0
                ).astype(BF16)
                lo = jnp.concatenate(
                    [jnp.where(lane_p == i, v_lo, 0.0) for i in range(b, b + batch)], axis=0
                ).astype(BF16)
                out = mm(hi, wb2[g])
                out = out[:, 0:LANES] + out[:, LANES:] + mm(lo, wb2[g, :, 0:LANES])
                for j in range(batch):
                    got = out[j * per:(j + 1) * per, :]
                    if role == 0:
                        got += dcol[0, hs, :] * state[slot_keep, hs, ts(b + j)]
                    made[role, hs, ts(b + j)] = got

    def to_rows(role, y):
        for p in range(steps // 2):
            ye[...] = y[:, ts(p)]
            even = ye[pl.ds(0, ctiles, stride=2), :]
            odd = ye[pl.ds(1, ctiles, stride=2), :]
            at = 2 * p * ctiles
            rowt[at:at + ctiles, :] = jnp.where(low_c, even, pltpu.roll(odd, HALF, 1))
            rowt[at + ctiles:at + 2 * ctiles, :] = jnp.where(
                low_c, pltpu.roll(even, HALF, 1), odd
            )
        total = jnp.zeros((steps, LANES), F32)
        for i in range(ctiles):
            v = rowt[pl.ds(i, steps, stride=ctiles), :] * gate[role, :, ts(i)]
            xc[role, :, ts(i)] = v
            total += v * v
        own = jnp.sum(total, axis=1, keepdims=True)
        ssv[role] = jnp.broadcast_to(own, ssv.shape[1:])

    swaps = [
        pltpu.make_async_remote_copy(
            src_ref=ssv.at[role],
            dst_ref=ssr.at[role],
            send_sem=st.at[role],
            recv_sem=rt.at[role],
            device_id={"tp": 1 - tp},
            device_id_type=MESH,
        )
        for role in range(2)
    ]

    def finish(role):
        swaps[role].wait_recv()
        both = (ssv[role] + ssr[role])[:, 0:1]
        norm = lax.rsqrt(both * (1.0 / (channels * 2)) + 1e-5)
        out = xc[role] * norm * nw[...]
        for k in range(slots):
            if role == 0:
                yv[k] = jnp.where(keep[k], out, 0.0).astype(BF16)
            else:
                yv[k] = jnp.where(rec[k], out, yv[k].astype(F32)).astype(BF16)

    slot_row = lax.broadcasted_iota(jnp.int32, (slots, channels), 0)
    for j in range(3):
        row = jnp.zeros((slots, channels), F32)
        for k in range(slots):
            new_row = xv[k].astype(F32)[steps - 3 + j:steps - 2 + j, :]
            row = jnp.where(slot_row == k, jnp.where(hit[k], new_row, 0.0), row)
        ncx[j] = row.astype(BF16)
        for k in range(slots):
            pair = bcv[k, steps - 3 + j].astype(F32)
            ncb[k, j] = jnp.where(hit[k], pair, 0.0).astype(BF16)
    for j in range(3):
        winx[0, j:j + 1, :] = tap(j, slot_keep)
        pair = cb[slot_keep, j].astype(F32)
        for g in range(groups):
            winb[0, g, j:j + 1, :] = pair[g:g + 1, :]
    convolve(0, k_keep)
    prepare(0, k_keep)
    added(0)
    for g in range(groups):
        hs = slice(g * per, (g + 1) * per)
        acc = jnp.zeros((per, width), F32)
        for b in range(0, tiles, batch):
            parts_s = [state[slot_keep, hs, ts(i)] for i in range(b, b + batch)]
            hi, lo = split(jnp.concatenate(parts_s, axis=0))
            out = mm(jnp.concatenate([hi, lo], axis=1), wc2[0, g]) + mm(hi, wcl[0, g])
            for j in range(batch):
                acc += jnp.where(lane_p == b + j, out[j * per:(j + 1) * per, :], 0.0)
        yb[0, hs, :] = yb[0, hs, :] + dl[0, hs, :] * acc
    to_rows(0, yb[0])
    swaps[0].start()
    owner_for = {k: source_owner(lax.rem(me + k, n)) for k in order} if small else None

    def origin_of(k):
        return owner_for[k] if small else source_owner(lax.rem(me + k, n))

    each(lambda k: landed(spread, whole, s1, r1, k))

    def pick_fore(k):
        picked[lax.rem(me + k, n), 0:cut, :] = spread[origin_of(k), 0:cut, :]
        second(k).start()

    def pick_rear(k):
        picked[lax.rem(me + k, n), cut:, :] = spread[origin_of(k), cut:, :]
        third(k).start()

    each(pick_fore, turns)
    if whole_tiles:
        each(pick_rear, turns)
    arr[me] = spread[src_me]
    finish(0)

    each(lambda k: landed(arr, fore, s2, r2, k), turns)
    for i in range(n):
        hf[i * extra:(i + 1) * extra, :] = arr[i, 0:extra, :].astype(jnp.int32).astype(F32)
    unit_in = column(hf[row_unit:row_unit + 1, 0:heads]) * GRAIN
    for j in range(3):
        x_unit = hf[row_unit + 1 + j:row_unit + 2 + j, :] * GRAIN
        for i in range(ctiles):
            at = j * ctiles + i
            winx[1, j:j + 1, ts(i)] = hf[at:at + 1, :] * x_unit
        for g in range(groups):
            at = j * groups + g
            winb[1, g, j:j + 1, :] = hf[row_bc + at:row_bc + at + 1, :] * (
                hf[row_unit + 4 + at:row_unit + 5 + at, :] * GRAIN
            )
    convolve(1, k_rec)
    prepare(1, k_rec)

    gain = unit_in * dcol[1]
    yr[...] = jnp.zeros_like(yr)

    def renew(piece, start, count):
        q = piece.astype(jnp.int32).astype(F32)
        for j in range(count):
            at = pl.ds(pl.multiple_of((start + j) * LANES, LANES), LANES)
            arrived = made[1, :, at] + gain * q[j * heads:(j + 1) * heads, :]
            stayed = made[0, :, at]
            for k in range(slots):
                new[k, :, at] = jnp.where(
                    rec[k], arrived, jnp.where(keep[k], stayed, 0.0)
                )

    def absorb(pieces, starts, count):
        qs = [p.astype(jnp.int32).astype(F32) for p in pieces]
        for g in range(groups):
            at = [(i, j) for i in range(len(qs)) for j in range(count)]
            part = jnp.concatenate(
                [qs[i][j * heads + g * per:j * heads + (g + 1) * per, :] for i, j in at], axis=0
            )
            hi, lo = split(part)
            out = mm(jnp.concatenate([hi, lo], axis=1), wc2[1, g]) + mm(hi, wcl[1, g])
            acc = yr[g * per:(g + 1) * per, :]
            for m, (i, j) in enumerate(at):
                acc += jnp.where(lane_p == starts[i] + j, out[m * per:(m + 1) * per, :], 0.0)
            yr[g * per:(g + 1) * per, :] = acc

    late = []
    if whole_tiles:
        per_owner = rows // heads
        added(1)
        all_k = [0] + turns
        for b in range(0, n, PAIR):
            ks = all_k[b:b + PAIR]
            for k in ks:
                if k:
                    landed(arr, rear, s3, r3, k)
            origins = [lax.rem(me + n - k, n) for k in ks]
            starts = [o * per_owner for o in origins]
            absorb([arr[o, cut:, :] for o in origins], starts, per_owner)
            for o, st_at in zip(origins, starts):
                if b < n - LATE:
                    renew(arr[o, cut:, :], st_at, per_owner)
                else:
                    late.append((o, st_at))
    else:
        added(1)
        some = 4 * heads // rows
        for i in range(tiles // 4):
            four = arr[i * some:(i + 1) * some, extra:, :].reshape(4 * heads, LANES)
            absorb([four], [i * 4], 4)
            renew(four, i * 4, 4)

    to_rows(1, yb[1] + (unit_in * dl[1]) * yr[...])
    swaps[1].start()
    for o, st_at in late:
        renew(arr[o, cut:, :], st_at, per_owner)
    finish(1)
    for sw in swaps:
        sw.wait_send()
    each(lambda k: first(k).wait_send())
    each(lambda k: second(k).wait_send())
    if whole_tiles:
        each(lambda k: third(k).wait_send())


def store_kernel(*refs):
    sem = refs[-1]
    half = (len(refs) - 1) // 2
    copies = []
    for a, b in zip(refs[:half], refs[half:-1]):
        cuts = 4 if a.shape[1] % 32 == 0 else 1
        size = a.shape[1] // cuts
        for s in range(a.shape[0] if cuts > 1 else 1):
            for c in range(cuts):
                at = (s, pl.ds(c * size, size)) if cuts > 1 else slice(None)
                copies.append(pltpu.make_async_copy(a.at[at], b.at[at], sem.at[len(copies)]))
    for c in copies:
        c.start()
    for c in copies:
        c.wait()


def on_device(
    counts,
    move_plan,
    ssm_state,
    conv_x_state,
    conv_bc_state,
    x_in,
    bc_in,
    z_in,
    dt_in,
    conv_w_x,
    conv_b_x,
    conv_w_bc,
    conv_b_bc,
    dt_bias,
    a_log,
    d_skip,
    norm_w,
):
    n = lax.axis_size("req")
    slots, heads, cols = ssm_state.shape
    _, steps, channels = x_in.shape
    groups = conv_bc_state.shape[2]
    args = (
        counts,
        move_plan,
        ssm_state,
        conv_x_state.transpose(1, 0, 2),
        conv_bc_state,
        x_in,
        bc_in,
        z_in,
        dt_in,
        conv_w_x,
        conv_b_x.reshape(1, -1),
        conv_w_bc,
        conv_b_bc,
        dt_bias.reshape(1, -1),
        a_log.reshape(1, -1),
        d_skip.reshape(1, -1),
        norm_w.reshape(1, -1),
    )
    vm = pltpu.VMEM
    flat = (cols // LANES) * heads
    width = steps * HALF
    extra_rows = 3 * (channels // LANES) + 6 * groups + 4
    extra = -(-extra_rows // (16 * n)) * 16
    scratch = [pltpu.SMEM(a.shape, a.dtype) for a in args[:2]]
    scratch += [vm(a.shape, a.dtype) for a in args[2:]]
    scratch += [vm((n, flat // n + extra, LANES), jnp.int16)] * 4
    scratch += [
        vm((n * extra, LANES), F32),
        vm((2, 8, channels), F32),
        vm((2, groups, 8, LANES), F32),
        vm((2, steps, channels), F32),
        vm((steps * channels // LANES, LANES), F32),
        vm((steps, heads, LANES), F32),
        vm((2, steps, channels), F32),
        vm((2, heads, width), F32),
        vm((heads, width), F32),
        vm((2, heads, width), F32),
        vm((2, heads, LANES), F32),
        vm((2, groups, 2 * LANES, width), BF16),
        vm((2, groups, LANES, width), BF16),
        vm((groups, width, 2 * LANES), BF16),
        vm((heads, width), F32),
        vm((heads, LANES), F32),
        vm((2, heads, cols), F32),
        vm((2, steps, LANES), F32),
        vm((2, steps, LANES), F32),
    ]
    dma = pltpu.SemaphoreType.DMA
    scratch += [dma((len(args),))] + [dma((n,))] * 6 + [dma((2,)), dma((2,))]
    outs = [
        jax.ShapeDtypeStruct(x_in.shape, BF16),
        jax.ShapeDtypeStruct(ssm_state.shape, F32),
        jax.ShapeDtypeStruct(args[3].shape, BF16),
        jax.ShapeDtypeStruct(conv_bc_state.shape, BF16),
    ]
    hbm = pl.BlockSpec(memory_space=pltpu.HBM)
    made = pl.pallas_call(
        functools.partial(fused_kernel, n),
        out_shape=[vm(o.shape, o.dtype) for o in outs],
        in_specs=[hbm] * len(args),
        out_specs=[pl.BlockSpec(memory_space=vm)] * len(outs),
        scratch_shapes=scratch,
        compiler_params=pltpu.CompilerParams(
            collective_id=0, has_side_effects=True, vmem_limit_bytes=40 * 1024 * 1024
        ),
    )(*[pltpu.with_memory_space_constraint(a, pltpu.HBM) for a in args])
    made = [pltpu.with_memory_space_constraint(a, vm) for a in made]
    y_out, new_ssm, new_x, new_bc = pl.pallas_call(
        store_kernel,
        out_shape=outs,
        in_specs=[pl.BlockSpec(memory_space=vm)] * len(outs),
        out_specs=[hbm] * len(outs),
        scratch_shapes=[dma((16,))],
    )(*made)
    return y_out, new_ssm, new_x.transpose(1, 0, 2), new_bc


def solution(mesh):
    in_specs = (
        P("parts"),
        P("parts"),
        P(("parts", "req"), "tp", None),
        P(("parts", "req"), None, "tp"),
        P(("parts", "req"), None, "tp", None),
        P(("parts", "req"), None, "tp"),
        P(("parts", "req"), None, "tp", None),
        P(("parts", "req"), None, "tp"),
        P(("parts", "req"), None, "tp"),
        P(None, "tp"),
        P("tp"),
        P(None, "tp", None),
        P("tp", None),
        P("tp"),
        P("tp"),
        P("tp"),
        P("tp"),
    )
    out_specs = (
        P(("parts", "req"), None, "tp"),
        P(("parts", "req"), "tp", None),
        P(("parts", "req"), None, "tp"),
        P(("parts", "req"), None, "tp", None),
    )
    return jax.shard_map(
        on_device, mesh=mesh, in_specs=in_specs, out_specs=out_specs, check_vma=False
    )
```

```python
import functools

import jax
import jax.numpy as jnp
from jax import lax
from jax.experimental import pallas as pl
from jax.experimental.pallas import tpu as pltpu
from jax.sharding import PartitionSpec as P

MESH = pl.DeviceIdType.MESH
F32 = jnp.float32
BF16 = jnp.bfloat16
LANES = 128
HALF = 64
LATE = 4
PAIR = 4
TOP = 32767.0
GRAIN = 6.0 / (TOP * 32000.0)


def silu(v):
    return v / (1.0 + jnp.exp(-v))


def split(v):
    hi = v.astype(BF16)
    return hi, (v - hi.astype(F32)).astype(BF16)


def mm(a, b):
    return jnp.dot(a, b, preferred_element_type=F32)


def fused_kernel(
    n,
    counts_h,
    plan_h,
    state_h,
    cx_h,
    cb_h,
    x_h,
    bc_h,
    z_h,
    dt_h,
    wx_h,
    bx_h,
    wbc_h,
    bbc_h,
    dtb_h,
    alog_h,
    dskip_h,
    nw_h,
    gw,
    nrm,
    new,
    ncx,
    ncb,
    counts,
    plan,
    state,
    cx,
    cb,
    xv,
    bcv,
    zv,
    dtv,
    wx,
    bx,
    wbc,
    bbc,
    dtb,
    alog,
    dskip,
    nw,
    code,
    spread,
    picked,
    arr,
    hf,
    winx,
    winb,
    xc,
    rowt,
    xs,
    gate,
    yb,
    vv,
    dl,
    dcol,
    wc2,
    wcl,
    wb2,
    yr,
    ye,
    made,
    ssv,
    ssr,
    in_sem,
    s1,
    r1,
    s2,
    r2,
    s3,
    r3,
    st,
    rt,
):
    slots, heads, cols = state.shape
    steps, channels = xv.shape[1], xv.shape[2]
    groups = bbc.shape[0]
    per = heads // groups
    tiles = cols // LANES
    rows = tiles * heads // n
    ctiles = channels // LANES
    extra = hf.shape[0] // n
    small = n <= 16
    whole_tiles = small and rows % heads == 0
    cut = extra if whole_tiles else extra + rows
    row_bc = 3 * ctiles
    row_unit = row_bc + 3 * groups
    me = lax.axis_index("req")
    tp = lax.axis_index("tp")
    order = sorted(range(1, n), key=lambda k: (-min(k, n - k), k)) if small else None
    hellos = order[::-1] if small else None
    turns = order
    if n == 8:
        order = [4, 5, 3, 6, 2, 7, 1]
        turns = [4, 1, 7, 3, 5, 2, 6]

    def each(body, which=None):
        if small:
            for k in which or order:
                body(k)
        else:
            lax.fori_loop(1, n, lambda k, c: (body(k), c)[1], 0)

    barrier = pltpu.get_barrier_semaphore()

    def greet(k):
        pl.semaphore_signal(
            barrier, inc=1, device_id={"req": lax.rem(me + k, n)}, device_id_type=MESH
        )

    each(greet, hellos)
    pl.semaphore_signal(barrier, inc=1, device_id={"tp": 1 - tp}, device_id_type=MESH)

    pairs = [
        (counts_h, counts),
        (plan_h, plan),
        (state_h, state),
        (cx_h, cx),
        (cb_h, cb),
        (x_h, xv),
        (bc_h, bcv),
        (z_h, zv),
        (dt_h, dtv),
        (wx_h, wx),
        (bx_h, bx),
        (wbc_h, wbc),
        (bbc_h, bbc),
        (dtb_h, dtb),
        (alog_h, alog),
        (dskip_h, dskip),
        (nw_h, nw),
    ]
    loads = [pltpu.make_async_copy(a, b, in_sem.at[i]) for i, (a, b) in enumerate(pairs)]
    for ld in loads:
        ld.start()

    def send(src, dst, ss, rs, k):
        return pltpu.make_async_remote_copy(
            src_ref=src,
            dst_ref=dst,
            send_sem=ss.at[k],
            recv_sem=rs.at[k],
            device_id={"req": lax.rem(me + k, n)},
            device_id_type=MESH,
        )

    def landed(dst, at, ss, rs, k):
        origin = lax.rem(me + n - k, n)
        pltpu.make_async_remote_copy(
            src_ref=dst.at[origin, at],
            dst_ref=dst.at[origin, at],
            send_sem=ss.at[k],
            recv_sem=rs.at[k],
            device_id={"req": origin},
            device_id_type=MESH,
        ).wait_recv()

    whole = pl.ds(0, extra + rows)
    fore = pl.ds(0, cut)
    rear = pl.ds(cut, extra + rows - cut)

    def first(k):
        return send(code.at[lax.rem(me + k, n)], spread.at[me], s1, r1, k)

    def second(k):
        return send(picked.at[lax.rem(me + k, n), fore], arr.at[me, fore], s2, r2, k)

    def third(k):
        return send(picked.at[lax.rem(me + k, n), rear], arr.at[me, rear], s3, r3, k)

    loads[0].wait()
    loads[1].wait()
    one, zero = jnp.int32(1), jnp.int32(0)

    def live(r):
        return (r % slots) < counts[r // slots]

    def leaving(r):
        return live(r) & (plan[r] // slots != r // slots)

    send_j = zero
    for j in range(slots):
        send_j = jnp.where(leaving(me * slots + j), j, send_j)

    sub = lax.broadcasted_iota(jnp.int32, (heads, heads), 0)
    lane = lax.broadcasted_iota(jnp.int32, (heads, heads), 1)
    eye = sub == lane

    def column(row):
        return jnp.sum(jnp.where(eye, row, 0.0), axis=1, keepdims=True)

    def ts(i):
        return slice(i * LANES, (i + 1) * LANES)

    loads[2].wait()
    top = jnp.abs(state[send_j, :, ts(0)])
    for i in range(1, tiles):
        top = jnp.maximum(top, jnp.abs(state[send_j, :, ts(i)]))

    def grains(v):
        return jnp.minimum(jnp.floor(v * (1.0 / (TOP * GRAIN))) + 1.0, TOP)

    unit = grains(jnp.max(top, axis=1, keepdims=True))
    inv = 1.0 / (unit * GRAIN)
    for i in range(tiles):
        q = jnp.round(state[send_j, :, ts(i)] * inv)
        q = q.astype(jnp.int32).astype(jnp.int16)
        chunk = min(rows, heads)
        for at in range(0, heads, chunk):
            row = i * heads + at
            to = extra + row % rows
            code[row // rows, to:to + chunk, :] = q[at:at + chunk, :]

    loads[3].wait()
    loads[4].wait()
    hf[...] = jnp.zeros_like(hf)

    def tap(j, slot):
        both = cx[j].astype(F32)
        row = both[0:1, :]
        for s in range(1, slots):
            row = jnp.where(slot == s, both[s:s + 1, :], row)
        return row

    hf[row_unit:row_unit + 1, 0:heads] = jnp.sum(jnp.where(eye, unit, 0.0), axis=0, keepdims=True)
    for j in range(3):
        row = tap(j, send_j)
        x_unit = grains(jnp.max(jnp.abs(row), axis=1, keepdims=True))
        row = jnp.round(row * (1.0 / (x_unit * GRAIN)))
        for i in range(ctiles):
            hf[j * ctiles + i:j * ctiles + i + 1, :] = row[:, ts(i)]
        pair = cb[send_j, j].astype(F32)
        bc_unit = grains(jnp.max(jnp.abs(pair), axis=1, keepdims=True))
        hf[row_bc + j * groups:row_bc + (j + 1) * groups, :] = jnp.round(
            pair * (1.0 / (bc_unit * GRAIN))
        )
        hf[row_unit + 1 + j:row_unit + 2 + j, :] = jnp.broadcast_to(x_unit, (1, LANES))
        at = row_unit + 4 + j * groups
        hf[at:at + groups, :] = jnp.broadcast_to(bc_unit, (groups, LANES))
    for i in range(n):
        part = hf[i * extra:(i + 1) * extra, :]
        code[i, 0:extra, :] = part.astype(jnp.int32).astype(jnp.int16)

    pl.semaphore_wait(barrier, n)
    each(lambda k: first(k).start())
    spread[me] = code[me]

    def for_reqs(body, init):
        if small:
            for r in range(n * slots):
                init = body(r, init)
            return init
        return lax.fori_loop(0, n * slots, body, init)

    def scan_mine(r, carry):
        ok = live(r)
        out = []
        for k in range(slots):
            hit, src = carry[2 * k], carry[2 * k + 1]
            m = ok & (plan[r] == me * slots + k)
            out += [jnp.where(m, one, hit), jnp.where(m, r, src)]
        return tuple(out)

    mine_of = for_reqs(scan_mine, (zero,) * (2 * slots))
    hit = [mine_of[2 * k] == 1 for k in range(slots)]
    source = [mine_of[2 * k + 1] for k in range(slots)]
    rec = [hit[k] & (source[k] // slots != me) for k in range(slots)]
    keep = [hit[k] & (source[k] // slots == me) for k in range(slots)]
    k_rec, k_keep, slot_keep, src_me = zero, zero, zero, zero
    for k in range(slots):
        k_rec = jnp.where(rec[k], k, k_rec)
        k_keep = jnp.where(keep[k], k, k_keep)
        slot_keep = jnp.where(keep[k], source[k] % slots, slot_keep)
        src_me = jnp.where(rec[k], source[k] // slots, src_me)
    if small:
        goes = [jnp.where(leaving(jnp.int32(r)), plan[r] // slots, -1) for r in range(n * slots)]

    def source_owner(d):
        if small:
            src = zero
            for r in range(n * slots):
                src = jnp.where(goes[r] == d, r // slots, src)
            return src
        return lax.fori_loop(
            0,
            n * slots,
            lambda r, c: jnp.where(leaving(r) & (plan[r] // slots == d), r // slots, c),
            zero,
        )

    for ld in loads[5:]:
        ld.wait()
    rate = jnp.exp(alog[...])
    skip = column(dskip[...])
    width = steps * HALF
    low = lax.broadcasted_iota(jnp.int32, (heads, LANES), 1) < HALF
    low4 = lax.broadcasted_iota(jnp.int32, (steps, LANES), 1) < HALF
    low_c = lax.broadcasted_iota(jnp.int32, (ctiles, LANES), 1) < HALF
    lane_w = lax.broadcasted_iota(jnp.int32, (HALF, width), 1)
    even_w = lane_w % 2 == 0
    row_b = lax.broadcasted_iota(jnp.int32, (HALF, LANES), 0)
    lane_b = lax.broadcasted_iota(jnp.int32, (HALF, LANES), 1)
    match_b = (row_b % 2) == (lane_b // HALF)
    lane_p = (lax.broadcasted_iota(jnp.int32, (per, width), 1) % HALF) // 2
    batch = 8

    def convolve(role, place):
        winx[role, 3:3 + steps, :] = xv[place].astype(F32)
        for t in range(steps):
            pair = bcv[place, t].astype(F32)
            for g in range(groups):
                winb[role, g, 3 + t:4 + t, :] = pair[g:g + 1, :]
        acc = bx[...] + winx[role, 0:steps, :] * wx[0:1, :]
        for j in range(1, 4):
            acc += winx[role, j:j + steps, :] * wx[j:j + 1, :]
        acc = silu(acc)
        for i in range(ctiles):
            rowt[pl.ds(i, steps, stride=ctiles), :] = acc[:, ts(i)]
        for t in range(steps):
            r = rowt[t * ctiles:(t + 1) * ctiles, :]
            xs[t, pl.ds(0, ctiles, stride=2), :] = r
            xs[t, pl.ds(1, ctiles, stride=2), :] = pltpu.roll(r, HALF, 1)

    def prepare(role, place):
        gate[role] = silu(zv[place].astype(F32))
        raw = dtv[place] + dtb[...]
        delta = jnp.maximum(raw, 0.0) + jnp.log(1.0 + jnp.exp(-jnp.abs(raw)))
        decay = jnp.exp(-delta * rate)
        delta_col = [column(delta[t:t + 1, :]) for t in range(steps)]
        decay_col = [column(decay[t:t + 1, :]) for t in range(steps)]
        cum = [decay_col[0]]
        for t in range(1, steps):
            cum.append(cum[-1] * decay_col[t])
        for t in range(0, steps, 2):
            dl[role, :, ts(t // 2)] = jnp.where(low, cum[t], cum[t + 1])
        dcol[role] = jnp.broadcast_to(cum[-1], (heads, LANES))
        across = []
        for g in range(groups):
            acc = bbc[g:g + 1, :] + winb[role, g, 0:steps, :] * wbc[0, g:g + 1, :]
            for j in range(1, 4):
                acc += winb[role, g, j:j + steps, :] * wbc[j, g:g + 1, :]
            bw = silu(acc)
            turned = pltpu.roll(bw, HALF, 1)
            b_two = jnp.where(low4, bw, turned)
            c_two = jnp.where(low4, turned, bw)
            across.append(
                [
                    0.5 * jnp.sum(c_two * b_two[s:s + 1, :], axis=1, keepdims=True)
                    for s in range(steps)
                ]
            )
            c_cols = [column(c_two[t:t + 1, 0:HALF]) for t in range(steps)]
            halves = [
                jnp.where(low, c_cols[t], c_cols[t + 1]) for t in range(0, steps, 2)
            ]
            base = jnp.concatenate(halves, axis=1)
            for j in range(2):
                w = jnp.where(even_w == (j == 0), base, 0.0)
                hi, lo = split(w)
                wc2[role, g, j * HALF:(j + 1) * HALF, :] = hi
                wc2[role, g, LANES + j * HALF:LANES + (j + 1) * HALF, :] = hi
                wcl[role, g, j * HALF:(j + 1) * HALF, :] = lo
            for s in range(steps):
                w = jnp.where(match_b, b_two[s:s + 1, :], 0.0)
                hi, lo = split(w)
                wb2[g, s * HALF:(s + 1) * HALF, 0:LANES] = hi
                wb2[g, s * HALF:(s + 1) * HALF, LANES:2 * LANES] = lo

        def cross(t, s):
            return jnp.concatenate(
                [jnp.broadcast_to(across[g][s][t:t + 1, :], (per, 1)) for g in range(groups)],
                axis=0,
            )

        x_of = [xs[t] for t in range(steps)]
        for t in range(steps):
            acc = skip * x_of[t]
            weight = jnp.ones_like(skip)
            for s in range(t, -1, -1):
                acc += (weight * delta_col[s] * cross(t, s)) * x_of[s]
                weight = decay_col[s] * weight
            if t % 2 == 0:
                first_half = acc
            else:
                yb[role, :, ts(t // 2)] = jnp.where(low, first_half, pltpu.roll(acc, HALF, 1))
        weight = jnp.ones_like(skip)
        v_of = [None] * steps
        for s in range(steps - 1, -1, -1):
            v_of[s] = (weight * delta_col[s]) * x_of[s]
            weight = decay_col[s] * weight
        for s in range(0, steps, 2):
            vv[:, ts(s // 2)] = jnp.where(low, v_of[s], pltpu.roll(v_of[s + 1], HALF, 1))

    def added(role):
        for g in range(groups):
            hs = slice(g * per, (g + 1) * per)
            v = vv[hs, :]
            v_hi = v.astype(BF16).astype(F32)
            v_lo = v - v_hi
            for b in range(0, tiles, batch):
                hi = jnp.concatenate(
                    [jnp.where(lane_p == i, v_hi, 0.0) for i in range(b, b + batch)], axis=0
                ).astype(BF16)
                lo = jnp.concatenate(
                    [jnp.where(lane_p == i, v_lo, 0.0) for i in range(b, b + batch)], axis=0
                ).astype(BF16)
                out = mm(hi, wb2[g])
                out = out[:, 0:LANES] + out[:, LANES:] + mm(lo, wb2[g, :, 0:LANES])
                for j in range(batch):
                    got = out[j * per:(j + 1) * per, :]
                    if role == 0:
                        got += dcol[0, hs, :] * state[slot_keep, hs, ts(b + j)]
                    made[role, hs, ts(b + j)] = got

    def to_rows(role, y):
        for p in range(steps // 2):
            ye[...] = y[:, ts(p)]
            even = ye[pl.ds(0, ctiles, stride=2), :]
            odd = ye[pl.ds(1, ctiles, stride=2), :]
            at = 2 * p * ctiles
            rowt[at:at + ctiles, :] = jnp.where(low_c, even, pltpu.roll(odd, HALF, 1))
            rowt[at + ctiles:at + 2 * ctiles, :] = jnp.where(
                low_c, pltpu.roll(even, HALF, 1), odd
            )
        total = jnp.zeros((steps, LANES), F32)
        for i in range(ctiles):
            v = rowt[pl.ds(i, steps, stride=ctiles), :] * gate[role, :, ts(i)]
            xc[role, :, ts(i)] = v
            total += v * v
        own = jnp.sum(total, axis=1, keepdims=True)
        ssv[role] = jnp.broadcast_to(own, ssv.shape[1:])

    swaps = [
        pltpu.make_async_remote_copy(
            src_ref=ssv.at[role],
            dst_ref=ssr.at[role],
            send_sem=st.at[role],
            recv_sem=rt.at[role],
            device_id={"tp": 1 - tp},
            device_id_type=MESH,
        )
        for role in range(2)
    ]

    slot_row = lax.broadcasted_iota(jnp.int32, (slots, channels), 0)
    for j in range(3):
        row = jnp.zeros((slots, channels), F32)
        for k in range(slots):
            new_row = xv[k].astype(F32)[steps - 3 + j:steps - 2 + j, :]
            row = jnp.where(slot_row == k, jnp.where(hit[k], new_row, 0.0), row)
        ncx[j] = row.astype(BF16)
        for k in range(slots):
            pair = bcv[k, steps - 3 + j].astype(F32)
            ncb[k, j] = jnp.where(hit[k], pair, 0.0).astype(BF16)
    for j in range(3):
        winx[0, j:j + 1, :] = tap(j, slot_keep)
        pair = cb[slot_keep, j].astype(F32)
        for g in range(groups):
            winb[0, g, j:j + 1, :] = pair[g:g + 1, :]
    convolve(0, k_keep)
    prepare(0, k_keep)
    added(0)
    for g in range(groups):
        hs = slice(g * per, (g + 1) * per)
        acc = jnp.zeros((per, width), F32)
        for b in range(0, tiles, batch):
            parts_s = [state[slot_keep, hs, ts(i)] for i in range(b, b + batch)]
            hi, lo = split(jnp.concatenate(parts_s, axis=0))
            out = mm(jnp.concatenate([hi, lo], axis=1), wc2[0, g]) + mm(hi, wcl[0, g])
            for j in range(batch):
                acc += jnp.where(lane_p == b + j, out[j * per:(j + 1) * per, :], 0.0)
        yb[0, hs, :] = yb[0, hs, :] + dl[0, hs, :] * acc
    to_rows(0, yb[0])
    swaps[0].start()
    owner_for = {k: source_owner(lax.rem(me + k, n)) for k in order} if small else None

    def origin_of(k):
        return owner_for[k] if small else source_owner(lax.rem(me + k, n))

    each(lambda k: landed(spread, whole, s1, r1, k))

    def pick_fore(k):
        picked[lax.rem(me + k, n), 0:cut, :] = spread[origin_of(k), 0:cut, :]
        second(k).start()

    def pick_rear(k):
        picked[lax.rem(me + k, n), cut:, :] = spread[origin_of(k), cut:, :]
        third(k).start()

    each(pick_fore, turns)
    if whole_tiles:
        each(pick_rear, turns)
    arr[me] = spread[src_me]
    swaps[0].wait_recv()
    each(lambda k: first(k).wait_send())

    each(lambda k: landed(arr, fore, s2, r2, k), turns)
    for i in range(n):
        hf[i * extra:(i + 1) * extra, :] = arr[i, 0:extra, :].astype(jnp.int32).astype(F32)
    unit_in = column(hf[row_unit:row_unit + 1, 0:heads]) * GRAIN
    for j in range(3):
        x_unit = hf[row_unit + 1 + j:row_unit + 2 + j, :] * GRAIN
        for i in range(ctiles):
            at = j * ctiles + i
            winx[1, j:j + 1, ts(i)] = hf[at:at + 1, :] * x_unit
        for g in range(groups):
            at = j * groups + g
            winb[1, g, j:j + 1, :] = hf[row_bc + at:row_bc + at + 1, :] * (
                hf[row_unit + 4 + at:row_unit + 5 + at, :] * GRAIN
            )
    convolve(1, k_rec)
    prepare(1, k_rec)

    gain = unit_in * dcol[1]
    yr[...] = jnp.zeros_like(yr)

    def renew(piece, start, count):
        q = piece.astype(jnp.int32).astype(F32)
        for j in range(count):
            at = pl.ds(pl.multiple_of((start + j) * LANES, LANES), LANES)
            arrived = made[1, :, at] + gain * q[j * heads:(j + 1) * heads, :]
            stayed = made[0, :, at]
            for k in range(slots):
                new[k, :, at] = jnp.where(
                    rec[k], arrived, jnp.where(keep[k], stayed, 0.0)
                )

    def absorb(pieces, starts, count):
        qs = [p.astype(jnp.int32).astype(F32) for p in pieces]
        for g in range(groups):
            at = [(i, j) for i in range(len(qs)) for j in range(count)]
            part = jnp.concatenate(
                [qs[i][j * heads + g * per:j * heads + (g + 1) * per, :] for i, j in at], axis=0
            )
            hi, lo = split(part)
            out = mm(jnp.concatenate([hi, lo], axis=1), wc2[1, g]) + mm(hi, wcl[1, g])
            acc = yr[g * per:(g + 1) * per, :]
            for m, (i, j) in enumerate(at):
                acc += jnp.where(lane_p == starts[i] + j, out[m * per:(m + 1) * per, :], 0.0)
            yr[g * per:(g + 1) * per, :] = acc

    late = []
    if whole_tiles:
        per_owner = rows // heads
        added(1)
        all_k = [0] + turns
        for b in range(0, n, PAIR):
            ks = all_k[b:b + PAIR]
            for k in ks:
                if k:
                    landed(arr, rear, s3, r3, k)
            origins = [lax.rem(me + n - k, n) for k in ks]
            starts = [o * per_owner for o in origins]
            absorb([arr[o, cut:, :] for o in origins], starts, per_owner)
            for o, st_at in zip(origins, starts):
                if b < n - LATE:
                    renew(arr[o, cut:, :], st_at, per_owner)
                else:
                    late.append((o, st_at))
    else:
        added(1)
        some = 4 * heads // rows
        for i in range(tiles // 4):
            four = arr[i * some:(i + 1) * some, extra:, :].reshape(4 * heads, LANES)
            absorb([four], [i * 4], 4)
            renew(four, i * 4, 4)

    to_rows(1, yb[1] + (unit_in * dl[1]) * yr[...])
    swaps[1].start()
    for o, st_at in late:
        renew(arr[o, cut:, :], st_at, per_owner)
    for k in range(slots):
        gw[k] = jnp.where(rec[k], xc[1], jnp.where(keep[k], xc[0], 0.0)) * nw[...]
    each(lambda k: second(k).wait_send())
    if whole_tiles:
        each(lambda k: third(k).wait_send())
    swaps[1].wait_recv()
    for k in range(slots):
        both = jnp.where(rec[k], ssv[1] + ssr[1], ssv[0] + ssr[0])
        nrm[k] = lax.rsqrt(both * (1.0 / (channels * 2)) + 1e-5)
    for sw in swaps:
        sw.wait_send()


def store_kernel(gw, nrm, new, ncx, ncb, y_o, new_o, ncx_o, ncb_o, yv, sem):
    pairs = [(new, new_o), (ncx, ncx_o), (ncb, ncb_o), (yv, y_o)]
    copies = [pltpu.make_async_copy(a, b, sem.at[i]) for i, (a, b) in enumerate(pairs)]
    for c in copies[:3]:
        c.start()
    for k in range(yv.shape[0]):
        yv[k] = (gw[k] * nrm[k][:, 0:1]).astype(BF16)
    copies[3].start()
    for c in copies:
        c.wait()


def on_device(
    counts,
    move_plan,
    ssm_state,
    conv_x_state,
    conv_bc_state,
    x_in,
    bc_in,
    z_in,
    dt_in,
    conv_w_x,
    conv_b_x,
    conv_w_bc,
    conv_b_bc,
    dt_bias,
    a_log,
    d_skip,
    norm_w,
):
    n = lax.axis_size("req")
    slots, heads, cols = ssm_state.shape
    _, steps, channels = x_in.shape
    groups = conv_bc_state.shape[2]
    args = (
        counts,
        move_plan,
        ssm_state,
        conv_x_state.transpose(1, 0, 2),
        conv_bc_state,
        x_in,
        bc_in,
        z_in,
        dt_in,
        conv_w_x,
        conv_b_x.reshape(1, -1),
        conv_w_bc,
        conv_b_bc,
        dt_bias.reshape(1, -1),
        a_log.reshape(1, -1),
        d_skip.reshape(1, -1),
        norm_w.reshape(1, -1),
    )
    vm = pltpu.VMEM
    flat = (cols // LANES) * heads
    width = steps * HALF
    extra_rows = 3 * (channels // LANES) + 6 * groups + 4
    extra = -(-extra_rows // (16 * n)) * 16
    scratch = [pltpu.SMEM(a.shape, a.dtype) for a in args[:2]]
    scratch += [vm(a.shape, a.dtype) for a in args[2:]]
    scratch += [vm((n, flat // n + extra, LANES), jnp.int16)] * 4
    scratch += [
        vm((n * extra, LANES), F32),
        vm((2, 8, channels), F32),
        vm((2, groups, 8, LANES), F32),
        vm((2, steps, channels), F32),
        vm((steps * channels // LANES, LANES), F32),
        vm((steps, heads, LANES), F32),
        vm((2, steps, channels), F32),
        vm((2, heads, width), F32),
        vm((heads, width), F32),
        vm((2, heads, width), F32),
        vm((2, heads, LANES), F32),
        vm((2, groups, 2 * LANES, width), BF16),
        vm((2, groups, LANES, width), BF16),
        vm((groups, width, 2 * LANES), BF16),
        vm((heads, width), F32),
        vm((heads, LANES), F32),
        vm((2, heads, cols), F32),
        vm((2, steps, LANES), F32),
        vm((2, steps, LANES), F32),
    ]
    dma = pltpu.SemaphoreType.DMA
    scratch += [dma((len(args),))] + [dma((n,))] * 6 + [dma((2,)), dma((2,))]
    outs = [
        jax.ShapeDtypeStruct(x_in.shape, BF16),
        jax.ShapeDtypeStruct(ssm_state.shape, F32),
        jax.ShapeDtypeStruct(args[3].shape, BF16),
        jax.ShapeDtypeStruct(conv_bc_state.shape, BF16),
    ]
    hbm = pl.BlockSpec(memory_space=pltpu.HBM)
    made = pl.pallas_call(
        functools.partial(fused_kernel, n),
        out_shape=[vm(x_in.shape, F32), vm((slots, steps, LANES), F32)]
        + [vm(o.shape, o.dtype) for o in outs[1:]],
        in_specs=[hbm] * len(args),
        out_specs=[pl.BlockSpec(memory_space=vm)] * 5,
        scratch_shapes=scratch,
        compiler_params=pltpu.CompilerParams(
            collective_id=0, has_side_effects=True, vmem_limit_bytes=40 * 1024 * 1024
        ),
    )(*[pltpu.with_memory_space_constraint(a, pltpu.HBM) for a in args])
    made = [pltpu.with_memory_space_constraint(a, vm) for a in made]
    y_out, new_ssm, new_x, new_bc = pl.pallas_call(
        store_kernel,
        out_shape=outs,
        in_specs=[pl.BlockSpec(memory_space=vm)] * 5,
        out_specs=[hbm] * 4,
        scratch_shapes=[vm(x_in.shape, BF16), dma((4,))],
    )(*made)
    return y_out, new_ssm, new_x.transpose(1, 0, 2), new_bc


def solution(mesh):
    in_specs = (
        P("parts"),
        P("parts"),
        P(("parts", "req"), "tp", None),
        P(("parts", "req"), None, "tp"),
        P(("parts", "req"), None, "tp", None),
        P(("parts", "req"), None, "tp"),
        P(("parts", "req"), None, "tp", None),
        P(("parts", "req"), None, "tp"),
        P(("parts", "req"), None, "tp"),
        P(None, "tp"),
        P("tp"),
        P(None, "tp", None),
        P("tp", None),
        P("tp"),
        P("tp"),
        P("tp"),
        P("tp"),
    )
    out_specs = (
        P(("parts", "req"), None, "tp"),
        P(("parts", "req"), "tp", None),
        P(("parts", "req"), None, "tp"),
        P(("parts", "req"), None, "tp", None),
    )
    return jax.shard_map(
        on_device, mesh=mesh, in_specs=in_specs, out_specs=out_specs, check_vma=False
    )
```

```python
import functools

import jax
import jax.numpy as jnp
from jax import lax
from jax.experimental import pallas as pl
from jax.experimental.pallas import tpu as pltpu
from jax.sharding import PartitionSpec as P

MESH = pl.DeviceIdType.MESH
F32 = jnp.float32
BF16 = jnp.bfloat16
LANES = 128
HALF = 64
LATE = 4
PAIR = 4
TOP = 32767.0
GRAIN = 6.0 / (TOP * 32000.0)


def silu(v):
    return v / (1.0 + jnp.exp(-v))


def split(v):
    hi = v.astype(BF16)
    return hi, (v - hi.astype(F32)).astype(BF16)


def mm(a, b):
    return jnp.dot(a, b, preferred_element_type=F32)


def fused_kernel(
    n,
    counts_h,
    plan_h,
    state_h,
    cx_h,
    cb_h,
    x_h,
    bc_h,
    z_h,
    dt_h,
    wx_h,
    bx_h,
    wbc_h,
    bbc_h,
    dtb_h,
    alog_h,
    dskip_h,
    nw_h,
    gw,
    nrm,
    new,
    ncx,
    ncb,
    counts,
    plan,
    state,
    cx,
    cb,
    xv,
    bcv,
    zv,
    dtv,
    wx,
    bx,
    wbc,
    bbc,
    dtb,
    alog,
    dskip,
    nw,
    code,
    spread,
    picked,
    arr,
    hf,
    winx,
    winb,
    xc,
    rowt,
    xs,
    gate,
    yb,
    vv,
    dl,
    dcol,
    wc2,
    wb2,
    yr,
    ye,
    made,
    ssv,
    ssr,
    in_sem,
    s1,
    r1,
    s2,
    r2,
    s3,
    r3,
    st,
    rt,
):
    slots, heads, cols = state.shape
    steps, channels = xv.shape[1], xv.shape[2]
    groups = bbc.shape[0]
    per = heads // groups
    tiles = cols // LANES
    rows = tiles * heads // n
    ctiles = channels // LANES
    extra = hf.shape[0] // n
    small = n <= 16
    whole_tiles = small and rows % heads == 0
    cut = extra if whole_tiles else extra + rows
    row_bc = 3 * ctiles
    row_unit = row_bc + 3 * groups
    me = lax.axis_index("req")
    tp = lax.axis_index("tp")
    order = sorted(range(1, n), key=lambda k: (-min(k, n - k), k)) if small else None
    hellos = order[::-1] if small else None
    turns = order
    if n == 8:
        order = [4, 5, 3, 6, 2, 7, 1]
        turns = [4, 1, 7, 3, 5, 2, 6]

    def each(body, which=None):
        if small:
            for k in which or order:
                body(k)
        else:
            lax.fori_loop(1, n, lambda k, c: (body(k), c)[1], 0)

    barrier = pltpu.get_barrier_semaphore()

    def greet(k):
        pl.semaphore_signal(
            barrier, inc=1, device_id={"req": lax.rem(me + k, n)}, device_id_type=MESH
        )

    each(greet, hellos)
    pl.semaphore_signal(barrier, inc=1, device_id={"tp": 1 - tp}, device_id_type=MESH)

    pairs = [
        (counts_h, counts),
        (plan_h, plan),
        (state_h, state),
        (cx_h, cx),
        (cb_h, cb),
        (x_h, xv),
        (bc_h, bcv),
        (z_h, zv),
        (dt_h, dtv),
        (wx_h, wx),
        (bx_h, bx),
        (wbc_h, wbc),
        (bbc_h, bbc),
        (dtb_h, dtb),
        (alog_h, alog),
        (dskip_h, dskip),
        (nw_h, nw),
    ]
    loads = [pltpu.make_async_copy(a, b, in_sem.at[i]) for i, (a, b) in enumerate(pairs)]
    for ld in loads:
        ld.start()

    def send(src, dst, ss, rs, k):
        return pltpu.make_async_remote_copy(
            src_ref=src,
            dst_ref=dst,
            send_sem=ss.at[k],
            recv_sem=rs.at[k],
            device_id={"req": lax.rem(me + k, n)},
            device_id_type=MESH,
        )

    def landed(dst, at, ss, rs, k):
        origin = lax.rem(me + n - k, n)
        pltpu.make_async_remote_copy(
            src_ref=dst.at[origin, at],
            dst_ref=dst.at[origin, at],
            send_sem=ss.at[k],
            recv_sem=rs.at[k],
            device_id={"req": origin},
            device_id_type=MESH,
        ).wait_recv()

    whole = pl.ds(0, extra + rows)
    fore = pl.ds(0, cut)
    rear = pl.ds(cut, extra + rows - cut)

    def first(k):
        return send(code.at[lax.rem(me + k, n)], spread.at[me], s1, r1, k)

    def second(k):
        return send(picked.at[lax.rem(me + k, n), fore], arr.at[me, fore], s2, r2, k)

    def third(k):
        return send(picked.at[lax.rem(me + k, n), rear], arr.at[me, rear], s3, r3, k)

    loads[0].wait()
    loads[1].wait()
    one, zero = jnp.int32(1), jnp.int32(0)

    def live(r):
        return (r % slots) < counts[r // slots]

    def leaving(r):
        return live(r) & (plan[r] // slots != r // slots)

    send_j = zero
    for j in range(slots):
        send_j = jnp.where(leaving(me * slots + j), j, send_j)

    sub = lax.broadcasted_iota(jnp.int32, (heads, heads), 0)
    lane = lax.broadcasted_iota(jnp.int32, (heads, heads), 1)
    eye = sub == lane

    def column(row):
        return jnp.sum(jnp.where(eye, row, 0.0), axis=1, keepdims=True)

    def ts(i):
        return slice(i * LANES, (i + 1) * LANES)

    loads[2].wait()
    top = jnp.abs(state[send_j, :, ts(0)])
    for i in range(1, tiles):
        top = jnp.maximum(top, jnp.abs(state[send_j, :, ts(i)]))

    def grains(v):
        return jnp.minimum(jnp.floor(v * (1.0 / (TOP * GRAIN))) + 1.0, TOP)

    unit = grains(jnp.max(top, axis=1, keepdims=True))
    inv = 1.0 / (unit * GRAIN)
    for i in range(tiles):
        q = jnp.round(state[send_j, :, ts(i)] * inv)
        q = q.astype(jnp.int32).astype(jnp.int16)
        chunk = min(rows, heads)
        for at in range(0, heads, chunk):
            row = i * heads + at
            to = extra + row % rows
            code[row // rows, to:to + chunk, :] = q[at:at + chunk, :]

    loads[3].wait()
    loads[4].wait()
    hf[...] = jnp.zeros_like(hf)

    def tap(j, slot):
        both = cx[j].astype(F32)
        row = both[0:1, :]
        for s in range(1, slots):
            row = jnp.where(slot == s, both[s:s + 1, :], row)
        return row

    hf[row_unit:row_unit + 1, 0:heads] = jnp.sum(jnp.where(eye, unit, 0.0), axis=0, keepdims=True)
    for j in range(3):
        row = tap(j, send_j)
        x_unit = grains(jnp.max(jnp.abs(row), axis=1, keepdims=True))
        row = jnp.round(row * (1.0 / (x_unit * GRAIN)))
        for i in range(ctiles):
            hf[j * ctiles + i:j * ctiles + i + 1, :] = row[:, ts(i)]
        pair = cb[send_j, j].astype(F32)
        bc_unit = grains(jnp.max(jnp.abs(pair), axis=1, keepdims=True))
        hf[row_bc + j * groups:row_bc + (j + 1) * groups, :] = jnp.round(
            pair * (1.0 / (bc_unit * GRAIN))
        )
        hf[row_unit + 1 + j:row_unit + 2 + j, :] = jnp.broadcast_to(x_unit, (1, LANES))
        at = row_unit + 4 + j * groups
        hf[at:at + groups, :] = jnp.broadcast_to(bc_unit, (groups, LANES))
    for i in range(n):
        part = hf[i * extra:(i + 1) * extra, :]
        code[i, 0:extra, :] = part.astype(jnp.int32).astype(jnp.int16)

    pl.semaphore_wait(barrier, n)
    each(lambda k: first(k).start())
    spread[me] = code[me]

    def for_reqs(body, init):
        if small:
            for r in range(n * slots):
                init = body(r, init)
            return init
        return lax.fori_loop(0, n * slots, body, init)

    def scan_mine(r, carry):
        ok = live(r)
        out = []
        for k in range(slots):
            hit, src = carry[2 * k], carry[2 * k + 1]
            m = ok & (plan[r] == me * slots + k)
            out += [jnp.where(m, one, hit), jnp.where(m, r, src)]
        return tuple(out)

    mine_of = for_reqs(scan_mine, (zero,) * (2 * slots))
    hit = [mine_of[2 * k] == 1 for k in range(slots)]
    source = [mine_of[2 * k + 1] for k in range(slots)]
    rec = [hit[k] & (source[k] // slots != me) for k in range(slots)]
    keep = [hit[k] & (source[k] // slots == me) for k in range(slots)]
    k_rec, k_keep, slot_keep, src_me = zero, zero, zero, zero
    for k in range(slots):
        k_rec = jnp.where(rec[k], k, k_rec)
        k_keep = jnp.where(keep[k], k, k_keep)
        slot_keep = jnp.where(keep[k], source[k] % slots, slot_keep)
        src_me = jnp.where(rec[k], source[k] // slots, src_me)
    if small:
        goes = [jnp.where(leaving(jnp.int32(r)), plan[r] // slots, -1) for r in range(n * slots)]

    def source_owner(d):
        if small:
            src = zero
            for r in range(n * slots):
                src = jnp.where(goes[r] == d, r // slots, src)
            return src
        return lax.fori_loop(
            0,
            n * slots,
            lambda r, c: jnp.where(leaving(r) & (plan[r] // slots == d), r // slots, c),
            zero,
        )

    for ld in loads[5:]:
        ld.wait()
    rate = jnp.exp(alog[...])
    skip = column(dskip[...])
    width = steps * HALF
    low = lax.broadcasted_iota(jnp.int32, (heads, LANES), 1) < HALF
    low4 = lax.broadcasted_iota(jnp.int32, (steps, LANES), 1) < HALF
    low_c = lax.broadcasted_iota(jnp.int32, (ctiles, LANES), 1) < HALF
    lane_w = lax.broadcasted_iota(jnp.int32, (HALF, width), 1)
    even_w = lane_w % 2 == 0
    row_b = lax.broadcasted_iota(jnp.int32, (HALF, LANES), 0)
    lane_b = lax.broadcasted_iota(jnp.int32, (HALF, LANES), 1)
    match_b = (row_b % 2) == (lane_b // HALF)
    lane_p = (lax.broadcasted_iota(jnp.int32, (per, width), 1) % HALF) // 2
    batch = 8

    def convolve(role, place):
        winx[role, 3:3 + steps, :] = xv[place].astype(F32)
        for t in range(steps):
            pair = bcv[place, t].astype(F32)
            for g in range(groups):
                winb[role, g, 3 + t:4 + t, :] = pair[g:g + 1, :]
        acc = bx[...] + winx[role, 0:steps, :] * wx[0:1, :]
        for j in range(1, 4):
            acc += winx[role, j:j + steps, :] * wx[j:j + 1, :]
        acc = silu(acc)
        for i in range(ctiles):
            rowt[pl.ds(i, steps, stride=ctiles), :] = acc[:, ts(i)]
        for t in range(steps):
            r = rowt[t * ctiles:(t + 1) * ctiles, :]
            xs[t, pl.ds(0, ctiles, stride=2), :] = r
            xs[t, pl.ds(1, ctiles, stride=2), :] = pltpu.roll(r, HALF, 1)

    def prepare(role, place):
        gate[role] = silu(zv[place].astype(F32))
        raw = dtv[place] + dtb[...]
        delta = jnp.maximum(raw, 0.0) + jnp.log(1.0 + jnp.exp(-jnp.abs(raw)))
        decay = jnp.exp(-delta * rate)
        delta_col = [column(delta[t:t + 1, :]) for t in range(steps)]
        decay_col = [column(decay[t:t + 1, :]) for t in range(steps)]
        cum = [decay_col[0]]
        for t in range(1, steps):
            cum.append(cum[-1] * decay_col[t])
        for t in range(0, steps, 2):
            dl[role, :, ts(t // 2)] = jnp.where(low, cum[t], cum[t + 1])
        dcol[role] = jnp.broadcast_to(cum[-1], (heads, LANES))
        across = []
        for g in range(groups):
            acc = bbc[g:g + 1, :] + winb[role, g, 0:steps, :] * wbc[0, g:g + 1, :]
            for j in range(1, 4):
                acc += winb[role, g, j:j + steps, :] * wbc[j, g:g + 1, :]
            bw = silu(acc)
            turned = pltpu.roll(bw, HALF, 1)
            b_two = jnp.where(low4, bw, turned)
            c_two = jnp.where(low4, turned, bw)
            across.append(
                [
                    0.5 * jnp.sum(c_two * b_two[s:s + 1, :], axis=1, keepdims=True)
                    for s in range(steps)
                ]
            )
            c_cols = [column(c_two[t:t + 1, 0:HALF]) for t in range(steps)]
            halves = [
                jnp.where(low, c_cols[t], c_cols[t + 1]) for t in range(0, steps, 2)
            ]
            base = jnp.concatenate(halves, axis=1)
            for j in range(2):
                w = jnp.where(even_w == (j == 0), base, 0.0)
                hi, lo = split(w)
                wc2[role, g, j * HALF:(j + 1) * HALF, :] = hi
                wc2[role, g, LANES + j * HALF:LANES + (j + 1) * HALF, :] = hi
                wc2[role, g, 2 * LANES + j * HALF:2 * LANES + (j + 1) * HALF, :] = lo
            for s in range(steps):
                w = jnp.where(match_b, b_two[s:s + 1, :], 0.0)
                hi, lo = split(w)
                wb2[g, s * HALF:(s + 1) * HALF, 0:LANES] = hi
                wb2[g, s * HALF:(s + 1) * HALF, LANES:2 * LANES] = lo

        def cross(t, s):
            return jnp.concatenate(
                [jnp.broadcast_to(across[g][s][t:t + 1, :], (per, 1)) for g in range(groups)],
                axis=0,
            )

        x_of = [xs[t] for t in range(steps)]
        for t in range(steps):
            acc = skip * x_of[t]
            weight = jnp.ones_like(skip)
            for s in range(t, -1, -1):
                acc += (weight * delta_col[s] * cross(t, s)) * x_of[s]
                weight = decay_col[s] * weight
            if t % 2 == 0:
                first_half = acc
            else:
                yb[role, :, ts(t // 2)] = jnp.where(low, first_half, pltpu.roll(acc, HALF, 1))
        weight = jnp.ones_like(skip)
        v_of = [None] * steps
        for s in range(steps - 1, -1, -1):
            v_of[s] = (weight * delta_col[s]) * x_of[s]
            weight = decay_col[s] * weight
        for s in range(0, steps, 2):
            vv[:, ts(s // 2)] = jnp.where(low, v_of[s], pltpu.roll(v_of[s + 1], HALF, 1))

    def added(role):
        for g in range(groups):
            hs = slice(g * per, (g + 1) * per)
            v = vv[hs, :]
            v_hi = v.astype(BF16).astype(F32)
            v_lo = v - v_hi
            for b in range(0, tiles, batch):
                hi = jnp.concatenate(
                    [jnp.where(lane_p == i, v_hi, 0.0) for i in range(b, b + batch)], axis=0
                ).astype(BF16)
                lo = jnp.concatenate(
                    [jnp.where(lane_p == i, v_lo, 0.0) for i in range(b, b + batch)], axis=0
                ).astype(BF16)
                out = mm(hi, wb2[g])
                out = out[:, 0:LANES] + out[:, LANES:] + mm(lo, wb2[g, :, 0:LANES])
                for j in range(batch):
                    got = out[j * per:(j + 1) * per, :]
                    if role == 0:
                        got += dcol[0, hs, :] * state[slot_keep, hs, ts(b + j)]
                    made[role, hs, ts(b + j)] = got

    def to_rows(role, y):
        for p in range(steps // 2):
            ye[...] = y[:, ts(p)]
            even = ye[pl.ds(0, ctiles, stride=2), :]
            odd = ye[pl.ds(1, ctiles, stride=2), :]
            at = 2 * p * ctiles
            rowt[at:at + ctiles, :] = jnp.where(low_c, even, pltpu.roll(odd, HALF, 1))
            rowt[at + ctiles:at + 2 * ctiles, :] = jnp.where(
                low_c, pltpu.roll(even, HALF, 1), odd
            )
        total = jnp.zeros((steps, LANES), F32)
        for i in range(ctiles):
            v = rowt[pl.ds(i, steps, stride=ctiles), :] * gate[role, :, ts(i)]
            xc[role, :, ts(i)] = v
            total += v * v
        own = jnp.sum(total, axis=1, keepdims=True)
        ssv[role] = jnp.broadcast_to(own, ssv.shape[1:])

    swaps = [
        pltpu.make_async_remote_copy(
            src_ref=ssv.at[role],
            dst_ref=ssr.at[role],
            send_sem=st.at[role],
            recv_sem=rt.at[role],
            device_id={"tp": 1 - tp},
            device_id_type=MESH,
        )
        for role in range(2)
    ]

    slot_row = lax.broadcasted_iota(jnp.int32, (slots, channels), 0)
    for j in range(3):
        row = jnp.zeros((slots, channels), F32)
        for k in range(slots):
            new_row = xv[k].astype(F32)[steps - 3 + j:steps - 2 + j, :]
            row = jnp.where(slot_row == k, jnp.where(hit[k], new_row, 0.0), row)
        ncx[j] = row.astype(BF16)
        for k in range(slots):
            pair = bcv[k, steps - 3 + j].astype(F32)
            ncb[k, j] = jnp.where(hit[k], pair, 0.0).astype(BF16)
    for j in range(3):
        winx[0, j:j + 1, :] = tap(j, slot_keep)
        pair = cb[slot_keep, j].astype(F32)
        for g in range(groups):
            winb[0, g, j:j + 1, :] = pair[g:g + 1, :]
    convolve(0, k_keep)
    prepare(0, k_keep)
    added(0)
    for g in range(groups):
        hs = slice(g * per, (g + 1) * per)
        acc = jnp.zeros((per, width), F32)
        for b in range(0, tiles, batch):
            parts_s = [state[slot_keep, hs, ts(i)] for i in range(b, b + batch)]
            hi, lo = split(jnp.concatenate(parts_s, axis=0))
            out = mm(jnp.concatenate([hi, lo, hi], axis=1), wc2[0, g])
            for j in range(batch):
                acc += jnp.where(lane_p == b + j, out[j * per:(j + 1) * per, :], 0.0)
        yb[0, hs, :] = yb[0, hs, :] + dl[0, hs, :] * acc
    to_rows(0, yb[0])
    swaps[0].start()
    owner_for = {k: source_owner(lax.rem(me + k, n)) for k in order} if small else None

    def origin_of(k):
        return owner_for[k] if small else source_owner(lax.rem(me + k, n))

    each(lambda k: landed(spread, whole, s1, r1, k))

    def pick_fore(k):
        picked[lax.rem(me + k, n), 0:cut, :] = spread[origin_of(k), 0:cut, :]
        second(k).start()

    def pick_rear(k):
        picked[lax.rem(me + k, n), cut:, :] = spread[origin_of(k), cut:, :]
        third(k).start()

    each(pick_fore, turns)
    if whole_tiles:
        each(pick_rear, turns)
    arr[me] = spread[src_me]
    swaps[0].wait_recv()
    each(lambda k: first(k).wait_send())

    each(lambda k: landed(arr, fore, s2, r2, k), turns)
    for i in range(n):
        hf[i * extra:(i + 1) * extra, :] = arr[i, 0:extra, :].astype(jnp.int32).astype(F32)
    unit_in = column(hf[row_unit:row_unit + 1, 0:heads]) * GRAIN
    for j in range(3):
        x_unit = hf[row_unit + 1 + j:row_unit + 2 + j, :] * GRAIN
        for i in range(ctiles):
            at = j * ctiles + i
            winx[1, j:j + 1, ts(i)] = hf[at:at + 1, :] * x_unit
        for g in range(groups):
            at = j * groups + g
            winb[1, g, j:j + 1, :] = hf[row_bc + at:row_bc + at + 1, :] * (
                hf[row_unit + 4 + at:row_unit + 5 + at, :] * GRAIN
            )
    convolve(1, k_rec)
    prepare(1, k_rec)

    gain = unit_in * dcol[1]
    yr[...] = jnp.zeros_like(yr)

    def renew(piece, start, count):
        q = piece.astype(jnp.int32).astype(F32)
        for j in range(count):
            at = pl.ds(pl.multiple_of((start + j) * LANES, LANES), LANES)
            arrived = made[1, :, at] + gain * q[j * heads:(j + 1) * heads, :]
            stayed = made[0, :, at]
            for k in range(slots):
                new[k, :, at] = jnp.where(
                    rec[k], arrived, jnp.where(keep[k], stayed, 0.0)
                )

    def absorb(pieces, starts, count):
        qs = [p.astype(jnp.int32).astype(F32) for p in pieces]
        for g in range(groups):
            at = [(i, j) for i in range(len(qs)) for j in range(count)]
            part = jnp.concatenate(
                [qs[i][j * heads + g * per:j * heads + (g + 1) * per, :] for i, j in at], axis=0
            )
            hi, lo = split(part)
            out = mm(jnp.concatenate([hi, lo, hi], axis=1), wc2[1, g])
            acc = yr[g * per:(g + 1) * per, :]
            for m, (i, j) in enumerate(at):
                acc += jnp.where(lane_p == starts[i] + j, out[m * per:(m + 1) * per, :], 0.0)
            yr[g * per:(g + 1) * per, :] = acc

    late = []
    if whole_tiles:
        per_owner = rows // heads
        added(1)
        all_k = [0] + turns
        for b in range(0, n, PAIR):
            ks = all_k[b:b + PAIR]
            for k in ks:
                if k:
                    landed(arr, rear, s3, r3, k)
            origins = [lax.rem(me + n - k, n) for k in ks]
            starts = [o * per_owner for o in origins]
            absorb([arr[o, cut:, :] for o in origins], starts, per_owner)
            for o, st_at in zip(origins, starts):
                if b < n - LATE:
                    renew(arr[o, cut:, :], st_at, per_owner)
                else:
                    late.append((o, st_at))
    else:
        added(1)
        some = 4 * heads // rows
        for i in range(tiles // 4):
            four = arr[i * some:(i + 1) * some, extra:, :].reshape(4 * heads, LANES)
            absorb([four], [i * 4], 4)
            renew(four, i * 4, 4)

    to_rows(1, yb[1] + (unit_in * dl[1]) * yr[...])
    swaps[1].start()
    for o, st_at in late:
        renew(arr[o, cut:, :], st_at, per_owner)
    for k in range(slots):
        gw[k] = jnp.where(rec[k], xc[1], jnp.where(keep[k], xc[0], 0.0)) * nw[...]
    each(lambda k: second(k).wait_send())
    if whole_tiles:
        each(lambda k: third(k).wait_send())
    swaps[1].wait_recv()
    for k in range(slots):
        both = jnp.where(rec[k], ssv[1] + ssr[1], ssv[0] + ssr[0])
        nrm[k] = lax.rsqrt(both * (1.0 / (channels * 2)) + 1e-5)
    for sw in swaps:
        sw.wait_send()


def store_kernel(gw, nrm, new, ncx, ncb, y_o, new_o, ncx_o, ncb_o, yv, sem):
    pairs = [(new, new_o), (ncx, ncx_o), (ncb, ncb_o), (yv, y_o)]
    copies = [pltpu.make_async_copy(a, b, sem.at[i]) for i, (a, b) in enumerate(pairs)]
    for c in copies[:3]:
        c.start()
    for k in range(yv.shape[0]):
        yv[k] = (gw[k] * nrm[k][:, 0:1]).astype(BF16)
    copies[3].start()
    for c in copies:
        c.wait()


def on_device(
    counts,
    move_plan,
    ssm_state,
    conv_x_state,
    conv_bc_state,
    x_in,
    bc_in,
    z_in,
    dt_in,
    conv_w_x,
    conv_b_x,
    conv_w_bc,
    conv_b_bc,
    dt_bias,
    a_log,
    d_skip,
    norm_w,
):
    n = lax.axis_size("req")
    slots, heads, cols = ssm_state.shape
    _, steps, channels = x_in.shape
    groups = conv_bc_state.shape[2]
    args = (
        counts,
        move_plan,
        ssm_state,
        conv_x_state.transpose(1, 0, 2),
        conv_bc_state,
        x_in,
        bc_in,
        z_in,
        dt_in,
        conv_w_x,
        conv_b_x.reshape(1, -1),
        conv_w_bc,
        conv_b_bc,
        dt_bias.reshape(1, -1),
        a_log.reshape(1, -1),
        d_skip.reshape(1, -1),
        norm_w.reshape(1, -1),
    )
    vm = pltpu.VMEM
    flat = (cols // LANES) * heads
    width = steps * HALF
    extra_rows = 3 * (channels // LANES) + 6 * groups + 4
    extra = -(-extra_rows // (16 * n)) * 16
    scratch = [pltpu.SMEM(a.shape, a.dtype) for a in args[:2]]
    scratch += [vm(a.shape, a.dtype) for a in args[2:]]
    scratch += [vm((n, flat // n + extra, LANES), jnp.int16)] * 4
    scratch += [
        vm((n * extra, LANES), F32),
        vm((2, 8, channels), F32),
        vm((2, groups, 8, LANES), F32),
        vm((2, steps, channels), F32),
        vm((steps * channels // LANES, LANES), F32),
        vm((steps, heads, LANES), F32),
        vm((2, steps, channels), F32),
        vm((2, heads, width), F32),
        vm((heads, width), F32),
        vm((2, heads, width), F32),
        vm((2, heads, LANES), F32),
        vm((2, groups, 3 * LANES, width), BF16),
        vm((groups, width, 2 * LANES), BF16),
        vm((heads, width), F32),
        vm((heads, LANES), F32),
        vm((2, heads, cols), F32),
        vm((2, steps, LANES), F32),
        vm((2, steps, LANES), F32),
    ]
    dma = pltpu.SemaphoreType.DMA
    scratch += [dma((len(args),))] + [dma((n,))] * 6 + [dma((2,)), dma((2,))]
    outs = [
        jax.ShapeDtypeStruct(x_in.shape, BF16),
        jax.ShapeDtypeStruct(ssm_state.shape, F32),
        jax.ShapeDtypeStruct(args[3].shape, BF16),
        jax.ShapeDtypeStruct(conv_bc_state.shape, BF16),
    ]
    hbm = pl.BlockSpec(memory_space=pltpu.HBM)
    made = pl.pallas_call(
        functools.partial(fused_kernel, n),
        out_shape=[vm(x_in.shape, F32), vm((slots, steps, LANES), F32)]
        + [vm(o.shape, o.dtype) for o in outs[1:]],
        in_specs=[hbm] * len(args),
        out_specs=[pl.BlockSpec(memory_space=vm)] * 5,
        scratch_shapes=scratch,
        compiler_params=pltpu.CompilerParams(
            collective_id=0, has_side_effects=True, vmem_limit_bytes=40 * 1024 * 1024
        ),
    )(*[pltpu.with_memory_space_constraint(a, pltpu.HBM) for a in args])
    made = [pltpu.with_memory_space_constraint(a, vm) for a in made]
    y_out, new_ssm, new_x, new_bc = pl.pallas_call(
        store_kernel,
        out_shape=outs,
        in_specs=[pl.BlockSpec(memory_space=vm)] * 5,
        out_specs=[hbm] * 4,
        scratch_shapes=[vm(x_in.shape, BF16), dma((4,))],
    )(*made)
    return y_out, new_ssm, new_x.transpose(1, 0, 2), new_bc


def solution(mesh):
    in_specs = (
        P("parts"),
        P("parts"),
        P(("parts", "req"), "tp", None),
        P(("parts", "req"), None, "tp"),
        P(("parts", "req"), None, "tp", None),
        P(("parts", "req"), None, "tp"),
        P(("parts", "req"), None, "tp", None),
        P(("parts", "req"), None, "tp"),
        P(("parts", "req"), None, "tp"),
        P(None, "tp"),
        P("tp"),
        P(None, "tp", None),
        P("tp", None),
        P("tp"),
        P("tp"),
        P("tp"),
        P("tp"),
    )
    out_specs = (
        P(("parts", "req"), None, "tp"),
        P(("parts", "req"), "tp", None),
        P(("parts", "req"), None, "tp"),
        P(("parts", "req"), None, "tp", None),
    )
    return jax.shard_map(
        on_device, mesh=mesh, in_specs=in_specs, out_specs=out_specs, check_vma=False
    )
```
